256 devices in a mesh: tile: 16 (over z, core), state: 16 (over x, y).
Axes of the slice: x: 4, y: 4, z: 8, core: 2. Of those that a mesh axis runs over, the one named last changes fastest.
Arguments:
- states: float32 [2, 128, 512, 128], P(None, 'tile', 'state'), parts along dimension 2, may hold values from -6 to 6
- onsite: float32 [2, 128, 128], P(None, 'tile'), may hold values from -0.5 to 0.5
- hop_row: float32 [2, 128, 128], P(None, 'tile'), may hold values from -3.2 to -2.2
- hop_up: float32 [2, 128, 128], P(None, 'tile'), may hold values from -3.2 to -2.2
- partner: int32 [128, 16], P('tile'), may hold values from -1 to 127, as said below
- coupling: bfloat16 [128, 16, 128, 128], P('tile'), may hold values from -0.125 to 0.125
- coefs: float32 [7], replicated, may hold values from 0.3 to 1
Outputs:
- filtered: float32 [2, 128, 512, 128], P(None, 'tile', 'state'), parts along dimension 2
The draws below stay inside these ranges and needn't reach their ends.
There are 16 independent parts, one for each index of `state`. The reference program is written for one: setup_inputs(seed, part) draws one part's arguments, and reference() takes and returns one part's arrays. A program takes and returns all parts, laid end to end along the dimension named above; an argument that names none is the same for every part. Nothing has to cross between parts.
Inputs may be any that keep to these rules, and one draw needn't show every extreme that they name: `partner`: A layer-one row r names only layer-two rows within 8 rows of r, cyclically; every row has at least 8 filled slots, filled slots come first.
All inputs are finite; a program needn't handle non-finite values.
Results may differ from the reference program's by a relative error of at most 0.00087.
Values may be sent and summed in bfloat16 or wider, within the bound.
No kernel may reach another device: no remote copies, remote signals or barrier semaphores. Data moves between devices by JAX's collectives and lax.ppermute only.
A program may use at most 64 MiB of HBM per device.

```python
import jax
import jax.numpy as jnp
from jax import lax

ROWS = 8
COLS = 128
NB = 16
REACH = 8
STATES = 32
DEGREE = 6
NROWS = 128


def draw_partner(key, part):
    first_key, second_key = jax.random.split(jax.random.fold_in(key, 17), 2)
    rows_all = jnp.arange(NROWS, dtype=jnp.int32)
    local = rows_all % ROWS
    offset = jax.random.randint(first_key, (NROWS, NB), -REACH, REACH + 1).astype(jnp.int32)
    slot_zero = jnp.where(local == 0, -REACH, jnp.where(local == ROWS - 1, REACH, offset[:, 0]))
    offset = offset.at[:, 0].set(slot_zero.astype(jnp.int32))
    target = (rows_all[:, None] + offset) % NROWS
    filled = jax.random.randint(second_key, (NROWS, 1), NB // 2, NB + 1).astype(jnp.int32)
    filled = jnp.where(local[:, None] == 0, NB, filled)
    filled = jnp.where(local[:, None] == 1, NB // 2, filled)
    slots = jnp.arange(NB, dtype=jnp.int32)[None, :]
    return jnp.where(slots < filled, target, -1).astype(jnp.int32)


def block_levels(stream_key, dims, shards, least, top_value):
    def one(position, parts):
        heights = jax.random.uniform(jax.random.fold_in(jax.random.fold_in(stream_key, 6), position), (parts,), jnp.float32, least / len(shards), top_value / len(shards))
        return jnp.repeat(jnp.exp(heights), dims[position] // parts).reshape((-1,) + (1,) * (len(dims) - position - 1))

    loudness = one(*shards[0])
    for cut in shards[1:]:
        loudness = loudness * one(*cut)
    return loudness


def gaussian(rng, shape, width, reach, shards=(), kind=jnp.bfloat16):
    level = block_levels(rng, shape, shards, -0.22, 0.18) if shards else 1.0
    drawn = jax.random.normal(rng, shape, jnp.float32) * width * level
    return jnp.minimum(jnp.maximum(drawn, -reach), reach).astype(kind)


def setup_inputs(seed: int = 0, part: int = 0) -> dict:
    seeds = jax.random.split(jax.random.key(seed), 8)
    part_keys = jax.random.split(jax.random.fold_in(seeds[7], part), 8)
    return {
        "states": gaussian(part_keys[0], (2, NROWS, STATES, COLS), 1.0, 6.0, ((1, 16),), jnp.float32),
        "onsite": jnp.clip(jax.random.uniform(seeds[1], (2, NROWS, COLS), jnp.float32, -0.5, 0.5) * block_levels(seeds[1], (2, NROWS, COLS), ((1, 16),), -0.4, 0.0), -0.5, 0.5),
        "hop_row": jnp.clip(-3.2 + 1.0 * jax.random.uniform(seeds[2], (2, NROWS, COLS), jnp.float32) ** block_levels(seeds[2], (2, NROWS, COLS), ((1, 16),), -0.2, 0.2), -3.2, -2.2),
        "hop_up": jnp.clip(-3.2 + 1.0 * jax.random.uniform(seeds[3], (2, NROWS, COLS), jnp.float32) ** block_levels(seeds[3], (2, NROWS, COLS), ((1, 16),), -0.2, 0.2), -3.2, -2.2),
        "partner": draw_partner(jax.random.fold_in(seeds[7], 71), part),
        "coupling": gaussian(seeds[5], (NROWS, NB, COLS, COLS), (NB * COLS) ** -0.5, 0.125, ((0, 16),)),
        "coefs": jnp.clip(jax.random.uniform(seeds[6], (DEGREE + 1,), jnp.float32, 0.3, 1.0), 0.3, 1.0),
    }


def hamiltonian(field, onsite, hop_row, bond_up, target, valid, coupling):
    intra = onsite[:, :, None, :] * field
    intra = intra + hop_row[:, :, None, :] * jnp.roll(field, -1, 3)
    intra = intra + jnp.roll(hop_row, 1, 2)[:, :, None, :] * jnp.roll(field, 1, 3)
    intra = intra + bond_up[:, :, None, :] * jnp.roll(field, -1, 1)
    intra = intra + jnp.roll(bond_up, 1, 1)[:, :, None, :] * jnp.roll(field, 1, 1)
    rounded = field.astype(jnp.bfloat16)
    first = rounded[0].astype(jnp.float32)
    second = rounded[1].astype(jnp.float32)
    weights = coupling.astype(jnp.float32)
    picked = second[target] * valid[:, :, None, None]
    upper = jnp.einsum("bksj,bkij->bsi", picked, weights, precision=lax.Precision.HIGHEST)
    terms = jnp.einsum("bsi,bkij->bksj", first, weights, precision=lax.Precision.HIGHEST)
    terms = terms * valid[:, :, None, None]
    count = target.shape[0] * target.shape[1]
    lower = jnp.zeros(second.shape, jnp.float32).at[target.reshape(count)].add(
        terms.reshape((count,) + terms.shape[2:]))
    return (intra + jnp.stack([upper, lower])) * (1.0 / 12.0)


def reference(states, onsite, hop_row, hop_up, partner, coupling, coefs):
    rows_all = jnp.arange(NROWS, dtype=jnp.int32)
    column = jnp.arange(COLS, dtype=jnp.int32)
    parity = (rows_all[:, None] + column[None, :]) % 2 == 0
    bond_up = jnp.where(parity[None], hop_up, jnp.float32(0.0))
    valid = (partner >= 0).astype(jnp.float32)
    target = jnp.where(partner >= 0, partner, 0).astype(jnp.int32)
    previous = states
    current = hamiltonian(states, onsite, hop_row, bond_up, target, valid, coupling)
    filtered = coefs[0] * previous + coefs[1] * current
    for order in range(2, DEGREE + 1):
        following = 2.0 * hamiltonian(current, onsite, hop_row, bond_up, target, valid, coupling) - previous
        filtered = filtered + coefs[order] * following
        previous, current = current, following
    return filtered
```

```python
import functools

import jax
import jax.numpy as jnp
from jax import lax
from jax.experimental import pallas as pl
from jax.experimental.pallas import tpu as pltpu
from jax.sharding import PartitionSpec as P

REACH = 8
LOCAL, MATE, FAR = 0, 1, 2
IN_VMEM = pl.BlockSpec(memory_space=pltpu.VMEM)
IN_SMEM = pl.BlockSpec(memory_space=pltpu.SMEM)
ANYWHERE = pl.BlockSpec(memory_space=pl.ANY)


def near(x):
    return pltpu.with_memory_space_constraint(x, pltpu.VMEM)


def held(shape, dtype):
    return pltpu.VMEM(shape, dtype)


def times(x, w):
    return lax.dot_general(x, w, (((1,), (0,)), ((), ())), preferred_element_type=jnp.float32)


def times_back(x, w):
    return lax.dot_general(x, w, (((1,), (1,)), ((), ())), preferred_element_type=jnp.float32)


def core():
    return lax.rem(lax.axis_index("tile"), 2)


def lanes(row, cols):
    return pl.ds(pl.multiple_of(row * cols, cols), cols)


def write_payloads(x_ref, w_ref, rim_ref, far_ref, mate_ref):
    wide = x_ref.shape[2]
    cols = rim_ref.shape[2]
    rows = wide // cols
    second = x_ref[1].astype(jnp.bfloat16)
    first = x_ref[0].astype(jnp.bfloat16)
    far_row = (rows - 1) * core()
    for side, (ref, row, w) in enumerate(
        ((far_ref, far_row, FAR), (mate_ref, rows - 1 - far_row, MATE))
    ):
        ref[:, 0:wide] = second
        ref[:, wide : 2 * wide] = times(first, w_ref[w]).astype(jnp.bfloat16)
        for layer in range(2):
            edge = x_ref[layer, :, lanes(row, cols)] * rim_ref[layer, side : side + 1, :]
            high = edge.astype(jnp.bfloat16)
            low = (edge - high.astype(jnp.float32)).astype(jnp.bfloat16)
            at = 2 * wide + 2 * layer * cols
            ref[:, at : at + cols] = high
            ref[:, at + cols : at + 2 * cols] = low


def add_received(scale, got_ref, side, w, row, w_ref, rim_ref, sum_ref):
    wide = sum_ref.shape[2]
    cols = rim_ref.shape[2]
    sum_ref[0] += scale * times_back(got_ref[:, 0:wide], w_ref[w])
    sum_ref[1] += scale * got_ref[:, wide : 2 * wide].astype(jnp.float32)
    for layer in range(2):
        at = 2 * wide + 2 * layer * cols
        edge = got_ref[:, at : at + cols].astype(jnp.float32) + got_ref[
            :, at + cols : at + 2 * cols
        ].astype(jnp.float32)
        sum_ref[layer, :, lanes(row, cols)] += scale * (edge * rim_ref[layer, side : side + 1, :])


def prepare(
    partner_ref, states_ref, onsite_ref, hop_row_ref, hop_up_ref, coupling_ref,
    x_ref, w_ref, coef_ref, rim_ref, far_ref, mate_ref, blocks, total, sems,
):
    rows, slots = partner_ref.shape
    cols = onsite_ref.shape[2]
    tile = lax.axis_index("tile")
    all_rows = rows * lax.axis_size("tile")
    here = core()

    def fetch(r):
        return pltpu.make_async_copy(coupling_ref.at[r], blocks.at[r], sems.at[r])

    for r in range(rows):
        fetch(r).start()
    for layer in range(2):
        for r in range(rows):
            x_ref[layer, :, r * cols : (r + 1) * cols] = states_ref[layer, r]
        hop_row = hop_row_ref[layer]
        row = lax.broadcasted_iota(jnp.int32, (rows, cols), 0) + tile * rows
        column = lax.broadcasted_iota(jnp.int32, (rows, cols), 1)
        bond = jnp.where((row + column) % 2 == 0, hop_up_ref[layer], 0.0)
        coef_ref[layer, 0] = onsite_ref[layer]
        coef_ref[layer, 1] = hop_row
        coef_ref[layer, 2] = pltpu.roll(hop_row, 1, axis=1)
        coef_ref[layer, 3] = bond
        coef_ref[layer, 4] = pltpu.roll(bond, 1, axis=0)
        last = bond[rows - 1 :]
        ones = jnp.ones_like(last)
        rim_ref[layer, 0:1] = jnp.where(here == 0, ones, last)
        rim_ref[layer, 1:2] = jnp.where(here == 0, last, ones)

    def one_row(r, carry):
        fetch(r).wait()
        total[...] = jnp.zeros_like(total)
        for k in range(slots):
            slot = partner_ref[r, k]

            @pl.when(slot >= 0)
            def _():
                away = lax.rem(slot - tile * rows + REACH + all_rows, all_rows)
                part = lax.div(away, rows)
                is_far = part == 2 * here
                place = jnp.where(part == 1, LOCAL, jnp.where(is_far, FAR, MATE))
                at = place * rows + lax.rem(away, rows)
                total[at] += blocks[r, k].astype(jnp.float32)

        for w in range(3):
            for g in range(rows):
                w_ref[w, pl.ds(pl.multiple_of(r * cols, cols), cols), g * cols : (g + 1) * cols] = total[
                    w * rows + g
                ].astype(jnp.bfloat16)
        return carry

    lax.fori_loop(0, rows, one_row, 0)
    write_payloads(x_ref, w_ref, rim_ref, far_ref, mate_ref)


def inner(order, coefs_ref, *refs):
    if order == 0:
        x_ref, w_ref, coef_ref, rim_ref, got_ref, sum_ref, filt_out = refs
        scale = 1.0 / 12.0
    else:
        x_ref, prev_ref, filt_ref, w_ref, coef_ref, rim_ref, got_ref, sum_ref, filt_out = refs
        scale = 2.0 / 12.0
    wide = x_ref.shape[2]
    cols = rim_ref.shape[2]
    rows = wide // cols
    first = x_ref[0].astype(jnp.bfloat16)
    second = x_ref[1].astype(jnp.bfloat16)
    sum_ref[0] = scale * times_back(second, w_ref[LOCAL])
    sum_ref[1] = scale * times(first, w_ref[LOCAL])
    for layer in range(2):
        for r in range(rows):
            here = slice(r * cols, (r + 1) * cols)
            x = x_ref[layer, :, here]

            def factor(i):
                return coef_ref[layer, i, r : r + 1, :]

            hop = factor(0) * x
            hop += factor(1) * pltpu.roll(x, cols - 1, axis=1)
            hop += factor(2) * pltpu.roll(x, 1, axis=1)
            if r < rows - 1:
                hop += factor(3) * x_ref[layer, :, (r + 1) * cols : (r + 2) * cols]
            if r > 0:
                hop += factor(4) * x_ref[layer, :, (r - 1) * cols : r * cols]
            term = sum_ref[layer, :, here] + scale * hop
            if order == 0:
                filt_out[layer, :, here] = coefs_ref[0] * x
            else:
                term -= prev_ref[layer, :, here]
                filt_out[layer, :, here] = filt_ref[layer, :, here] + coefs_ref[order] * x
            sum_ref[layer, :, here] = term
    mate_row = (rows - 1) * (1 - core())
    add_received(scale, got_ref, 1, MATE, mate_row, w_ref, rim_ref, sum_ref)


def outer(order, degree, coefs_ref, *refs):
    scale = 1.0 / 12.0 if order == 0 else 2.0 / 12.0
    last = order == degree - 1
    if last:
        sum_ref, filt_ref, w_ref, rim_ref, got_ref, out_ref, x_ref = refs
    else:
        sum_ref, w_ref, rim_ref, got_ref, x_ref, far_ref, mate_ref = refs
    wide = x_ref.shape[2]
    cols = rim_ref.shape[2]
    rows = wide // cols
    x_ref[...] = sum_ref[...]
    add_received(scale, got_ref, 0, FAR, (rows - 1) * core(), w_ref, rim_ref, x_ref)
    if last:
        for layer in range(2):
            for r in range(rows):
                here = slice(r * cols, (r + 1) * cols)
                out_ref[layer, r] = filt_ref[layer, :, here] + coefs_ref[degree] * x_ref[layer, :, here]
    else:
        write_payloads(x_ref, w_ref, rim_ref, far_ref, mate_ref)


def call(kernel, outs, args, scratch=(), specs=None, out_specs=None, limit=12):
    return pl.pallas_call(
        kernel,
        out_shape=outs,
        in_specs=specs or [IN_SMEM] + [IN_VMEM] * (len(args) - 1),
        out_specs=out_specs or [IN_VMEM] * len(outs),
        scratch_shapes=list(scratch),
        compiler_params=pltpu.CompilerParams(vmem_limit_bytes=limit << 20),
    )(*args)


def body(states, onsite, hop_row, hop_up, partner, coupling, coefs):
    rows, count, cols = states.shape[1:]
    slots = partner.shape[1]
    wide = rows * cols
    degree = coefs.shape[0] - 1
    size = lax.axis_size("tile")
    far_pairs = [(i, (i + 1) % size if i % 2 else (i - 1) % size) for i in range(size)]
    mate_pairs = [(i, i ^ 1) for i in range(size)]

    field = held((2, count, wide), jnp.float32)
    payload = held((count, 2 * wide + 4 * cols), jnp.bfloat16)
    x, w, coef, rim, far, mate = call(
        prepare,
        [field, held((3, wide, wide), jnp.bfloat16), held((2, 5, rows, cols), jnp.float32),
         held((2, 2, cols), jnp.float32), payload, payload],
        [partner, states, onsite, hop_row, hop_up, coupling],
        scratch=[
            pltpu.VMEM((rows, slots, cols, cols), jnp.bfloat16),
            pltpu.VMEM((3 * rows, cols, cols), jnp.float32),
            pltpu.SemaphoreType.DMA((rows,)),
        ],
        specs=[IN_SMEM] + [IN_VMEM] * 4 + [ANYWHERE],
        limit=24,
    )
    w, coef, rim = near(w), near(coef), near(rim)
    prev = filt = None
    for order in range(degree):
        got_far = lax.ppermute(far, "tile", far_pairs)
        got_mate = lax.ppermute(mate, "tile", mate_pairs)
        x = near(x)
        past = [] if order == 0 else [near(prev), near(filt)]
        partial, filt = call(
            functools.partial(inner, order),
            [field, field],
            [coefs, x, *past, w, coef, rim, near(got_mate)],
        )
        prev = x
        partial = near(partial)
        if order < degree - 1:
            x, far, mate = call(
                functools.partial(outer, order, degree),
                [field, payload, payload],
                [coefs, partial, w, rim, near(got_far)],
            )
        else:
            (out,) = call(
                functools.partial(outer, order, degree),
                [jax.ShapeDtypeStruct(states.shape, jnp.float32)],
                [coefs, partial, near(filt), w, rim, near(got_far)],
                scratch=[pltpu.VMEM((2, count, wide), jnp.float32)],
            )
    return out


def solution(mesh):
    placed = (
        P(None, "tile", "state", None),
        P(None, "tile", None),
        P(None, "tile", None),
        P(None, "tile", None),
        P("tile", None),
        P("tile", None, None, None),
        P(),
    )
    return jax.shard_map(
        body, mesh=mesh, in_specs=placed, out_specs=P(None, "tile", "state", None), check_vma=False
    )
```

```python
import functools

import jax
import jax.numpy as jnp
from jax import lax
from jax.experimental import pallas as pl
from jax.experimental.pallas import tpu as pltpu
from jax.sharding import PartitionSpec as P

REACH = 8
LOCAL, MATE, FAR = 0, 1, 2
IN_VMEM = pl.BlockSpec(memory_space=pltpu.VMEM)
ANYWHERE = pl.BlockSpec(memory_space=pl.ANY)
PAIR = 2


def near(x):
    return pltpu.with_memory_space_constraint(x, pltpu.VMEM)


def outside(x):
    return pltpu.with_memory_space_constraint(x, pltpu.HBM)


def held(shape, dtype):
    return pltpu.VMEM(shape, dtype)


def dot(x, w, contract):
    return lax.dot_general(x, w, (((1,), (contract,)), ((), ())), preferred_element_type=jnp.float32)


def span(side, group, groups, step):
    if side == FAR:
        return slice(0, (groups - group) * step)
    if side == MATE:
        return slice((groups - 1 - group) * step, groups * step)
    return slice(0, groups * step)


def products(x, w_ref, side, contract, cols):
    step = PAIR * cols
    groups = w_ref.shape[1] // step
    for group in range(groups):
        outs = slice(group * step, (group + 1) * step)
        ins = span(side, group, groups, step)
        block = w_ref[side, ins, outs] if contract == 0 else w_ref[side, outs, ins]
        yield outs, dot(x[:, ins], block, contract)


def write_payload(x_ref, w_ref, rim_ref, side, out_ref):
    wide = x_ref.shape[2]
    cols = rim_ref.shape[2]
    edge = slice(0, cols) if side == FAR else slice(wide - cols, wide)
    which = side - 1
    out_ref[:, 0:wide] = x_ref[1].astype(jnp.bfloat16)
    rim = x_ref[0, :, edge] * rim_ref[which, 0:1, :]
    rim += pltpu.roll(x_ref[1, :, edge] * rim_ref[which, 1:2, :], cols - 1, axis=1)
    high = rim.astype(jnp.bfloat16)
    out_ref[:, 2 * wide : 2 * wide + cols] = high
    out_ref[:, 2 * wide + cols :] = (rim - high.astype(jnp.float32)).astype(jnp.bfloat16)
    first = x_ref[0].astype(jnp.bfloat16)
    for outs, term in products(first, w_ref, side, 0, cols):
        out_ref[:, wide + outs.start : wide + outs.stop] = term.astype(jnp.bfloat16)


def add_received(scale, got_ref, w_ref, rim_ref, side, from_ref, to_ref):
    wide = to_ref.shape[2]
    cols = rim_ref.shape[2]
    edge = slice(0, cols) if side == FAR else slice(wide - cols, wide)
    which = side - 1
    to_ref[1] = from_ref[1] + scale * got_ref[:, wide : 2 * wide].astype(jnp.float32)
    for outs, term in products(got_ref[:, 0:wide], w_ref, side, 1, cols):
        to_ref[0, :, outs] = from_ref[0, :, outs] + scale * term
    rim = got_ref[:, 2 * wide : 2 * wide + cols].astype(jnp.float32)
    rim += got_ref[:, 2 * wide + cols :].astype(jnp.float32)
    to_ref[0, :, edge] += scale * (rim * rim_ref[which, 0:1, :])
    to_ref[1, :, edge] += scale * (pltpu.roll(rim, 1, axis=1) * rim_ref[which, 1:2, :])


def prepare(
    partner_hbm, states_hbm, onsite_hbm, hop_row_hbm, hop_up_hbm, coefs_hbm, coupling_hbm,
    x_ref, w_ref, coef_ref, rim_ref, weight_ref, far_ref, mate_ref,
    partner_ref, states_ref, small_ref, coefs_ref, blocks, total, sems, row_sems,
):
    rows, slots = partner_hbm.shape
    cols = onsite_hbm.shape[2]
    tile = lax.axis_index("tile")
    all_rows = rows * lax.axis_size("tile")
    here = lax.rem(tile, 2)
    offsets = 2 * REACH + 1
    spare = offsets + 1

    def kept(place):
        return place + here * (rows - 1 - 2 * place)

    copies = [
        pltpu.make_async_copy(src, dst, sems.at[i])
        for i, (src, dst) in enumerate(
            (
                (partner_hbm, partner_ref),
                (hop_up_hbm, small_ref.at[0]),
                (onsite_hbm, small_ref.at[1]),
                (hop_row_hbm, small_ref.at[2]),
                (coefs_hbm, coefs_ref),
                (states_hbm, states_ref),
            )
        )
    ]

    def fetch(r):
        return pltpu.make_async_copy(coupling_hbm.at[r], blocks.at[r], row_sems.at[r])

    copies[0].start()
    for place in range(rows):
        fetch(kept(place)).start()
    for copy in copies[1:]:
        copy.start()

    total[...] = jnp.zeros_like(total)
    for side, place, sigma in (
        [(FAR, p, rows - p) for p in range(1, rows, PAIR)]
        + [(MATE, p, rows - PAIR - p) for p in range(0, rows, PAIR)]
    ):
        w_ref[side, place * cols : (place + 1) * cols, sigma * cols : (sigma + 1) * cols] = jnp.zeros(
            (cols, cols), jnp.bfloat16
        )

    for copy in copies:
        copy.wait()
    for n in range(coefs_ref.shape[0]):
        weight_ref[n : n + 1, :] = jnp.full((1, cols), coefs_ref[n], jnp.float32)
    column = lax.broadcasted_iota(jnp.int32, (rows, cols), 1)
    parity = lax.broadcasted_iota(jnp.int32, (rows, cols), 0) + column + tile * rows
    odd = lax.rem(column[0:1], 2) == 1
    for layer in range(2):
        bond = jnp.where(lax.rem(parity, 2) == 0, small_ref[0, layer], 0.0)
        hop_row = small_ref[2, layer]
        left = pltpu.roll(hop_row, 1, axis=1)
        for place in range(rows):
            back = rows - 1 - place
            at = slice(place, place + 1)

            def ours(value):
                return jnp.where(here == 0, value[at], value[back : back + 1])

            coef_ref[layer, 0, at] = ours(small_ref[1, layer])
            coef_ref[layer, 1, at] = ours(hop_row)
            coef_ref[layer, 2, at] = ours(left)
            if place < rows - 1:
                coef_ref[layer, 3, at] = jnp.where(here == 0, bond[at], bond[back - 1 : back])
            if place > 0:
                coef_ref[layer, 4, at] = jnp.where(here == 0, bond[place - 1 : place], bond[back : back + 1])
        last = bond[rows - 1 :]
        raw = jnp.where(odd, 1.0, 0.0)
        rim_ref[FAR - 1, layer : layer + 1] = jnp.where(here == 0, raw, last)
        rim_ref[MATE - 1, layer : layer + 1] = jnp.where(here == 0, last, raw)
        for place in range(rows):
            x_ref[layer, :, place * cols : (place + 1) * cols] = states_ref[layer, kept(place)]

    for place in range(rows):
        row = kept(place)
        fetch(row).wait()
        for k in range(slots):
            slot = partner_ref[row, k]
            away = slot - tile * rows - row
            away = jnp.where(away > all_rows // 2, away - all_rows, away)
            away = jnp.where(away < -(all_rows // 2), away + all_rows, away)
            at = jnp.where(slot >= 0, REACH + (1 - 2 * here) * away, offsets) + place * spare
            total[at] += blocks[row, k].astype(jnp.float32)
        for offset in range(offsets):
            reached = place + offset - REACH
            if reached < 0:
                side, sigma = FAR, -1 - reached
            elif reached < rows:
                side, sigma = LOCAL, reached
            else:
                side, sigma = MATE, 2 * rows - 1 - reached
            w_ref[side, place * cols : (place + 1) * cols, sigma * cols : (sigma + 1) * cols] = total[
                place * spare + offset
            ].astype(jnp.bfloat16)
    write_payload(x_ref, w_ref, rim_ref, FAR, far_ref)
    write_payload(x_ref, w_ref, rim_ref, MATE, mate_ref)


def inner(order, *refs):
    if order == 0:
        x_ref, w_ref, coef_ref, weight_ref, sum_ref, filt_out = refs
        scale = 1.0 / 12.0
    else:
        x_ref, prev_ref, filt_ref, w_ref, coef_ref, weight_ref, sum_ref, filt_out = refs
        scale = 2.0 / 12.0
    wide = x_ref.shape[2]
    cols = weight_ref.shape[1]
    rows = wide // cols
    first = x_ref[0].astype(jnp.bfloat16)
    second = x_ref[1].astype(jnp.bfloat16)
    for outs, term in products(second, w_ref, LOCAL, 1, cols):
        sum_ref[0, :, outs] = scale * term
    for outs, term in products(first, w_ref, LOCAL, 0, cols):
        sum_ref[1, :, outs] = scale * term
    for layer in range(2):
        for r in range(rows):
            here = slice(r * cols, (r + 1) * cols)
            x = x_ref[layer, :, here]

            def factor(i):
                return coef_ref[layer, i, r : r + 1, :]

            hop = factor(0) * x
            hop += factor(1) * pltpu.roll(x, cols - 1, axis=1)
            hop += factor(2) * pltpu.roll(x, 1, axis=1)
            if r < rows - 1:
                hop += factor(3) * x_ref[layer, :, (r + 1) * cols : (r + 2) * cols]
            if r > 0:
                hop += factor(4) * x_ref[layer, :, (r - 1) * cols : r * cols]
            term = sum_ref[layer, :, here] + scale * hop
            filt = weight_ref[order : order + 1, :] * x
            if order > 0:
                term -= prev_ref[layer, :, here]
                filt += filt_ref[layer, :, here]
            filt_out[layer, :, here] = filt
            sum_ref[layer, :, here] = term


def from_mate(scale, part_ref, w_ref, rim_ref, got_ref, sum_ref):
    add_received(scale, got_ref, w_ref, rim_ref, MATE, part_ref, sum_ref)


def outer(scale, sum_ref, w_ref, rim_ref, got_ref, x_ref, far_ref, mate_ref):
    add_received(scale, got_ref, w_ref, rim_ref, FAR, sum_ref, x_ref)
    write_payload(x_ref, w_ref, rim_ref, FAR, far_ref)
    write_payload(x_ref, w_ref, rim_ref, MATE, mate_ref)


def finish(scale, degree, sum_ref, filt_ref, w_ref, rim_ref, weight_ref, got_ref, out_ref, x_ref):
    cols = rim_ref.shape[2]
    rows = out_ref.shape[1]
    add_received(scale, got_ref, w_ref, rim_ref, FAR, sum_ref, x_ref)
    flip = lax.rem(lax.axis_index("tile"), 2)
    for layer in range(2):
        for place in range(rows):
            here = slice(place * cols, (place + 1) * cols)
            out_ref[layer, place + flip * (rows - 1 - 2 * place)] = (
                filt_ref[layer, :, here] + weight_ref[degree : degree + 1, :] * x_ref[layer, :, here]
            )


def call(kernel, outs, args, scratch=(), specs=None, limit=12):
    return pl.pallas_call(
        kernel,
        out_shape=outs,
        in_specs=specs or [IN_VMEM] * len(args),
        out_specs=[IN_VMEM] * len(outs),
        scratch_shapes=list(scratch),
        cost_estimate=pl.CostEstimate(flops=1 << 20, bytes_accessed=1 << 12, transcendentals=0),
        compiler_params=pltpu.CompilerParams(vmem_limit_bytes=limit << 20),
    )(*args)


def body(states, onsite, hop_row, hop_up, partner, coupling, coefs):
    rows, count, cols = states.shape[1:]
    slots = partner.shape[1]
    wide = rows * cols
    degree = coefs.shape[0] - 1
    size = lax.axis_size("tile")
    far_pairs = [(i, (i + 1) % size if i % 2 else (i - 1) % size) for i in range(size)]
    mate_pairs = [(i, i ^ 1) for i in range(size)]

    field = held((2, count, wide), jnp.float32)
    payload = held((count, 2 * wide + 2 * cols), jnp.bfloat16)
    x, w, coef, rim, weight, far, mate = call(
        prepare,
        [field, held((3, wide, wide), jnp.bfloat16), held((2, 5, rows, cols), jnp.float32),
         held((2, 2, cols), jnp.float32), held((degree + 1, cols), jnp.float32), payload, payload],
        [outside(v) for v in (partner, states, onsite, hop_row, hop_up, coefs, coupling)],
        scratch=[
            pltpu.SMEM((rows, slots), jnp.int32),
            pltpu.VMEM((2, rows, count, cols), jnp.float32),
            pltpu.VMEM((3, 2, rows, cols), jnp.float32),
            pltpu.SMEM((degree + 1,), jnp.float32),
            pltpu.VMEM((rows, slots, cols, cols), jnp.bfloat16),
            pltpu.VMEM((rows * (2 * REACH + 2), cols, cols), jnp.float32),
            pltpu.SemaphoreType.DMA((6,)),
            pltpu.SemaphoreType.DMA((rows,)),
        ],
        specs=[ANYWHERE] * 7,
        limit=24,
    )
    w, coef, rim, weight, x = near(w), near(coef), near(rim), near(weight), near(x)
    prev = filt = None
    for order in range(degree):
        scale = 1.0 / 12.0 if order == 0 else 2.0 / 12.0
        got_far = lax.ppermute(far, "tile", far_pairs)
        got_mate = lax.ppermute(mate, "tile", mate_pairs)
        past = [] if order == 0 else [near(prev), near(filt)]
        part, filt = call(
            functools.partial(inner, order), [field, field], [x, *past, w, coef, weight]
        )
        (part,) = call(
            functools.partial(from_mate, scale), [field], [near(part), w, rim, near(got_mate)]
        )
        prev = x
        if order < degree - 1:
            x, far, mate = call(
                functools.partial(outer, scale),
                [field, payload, payload],
                [near(part), w, rim, near(got_far)],
            )
            x = near(x)
        else:
            (out,) = call(
                functools.partial(finish, scale, degree),
                [jax.ShapeDtypeStruct(states.shape, jnp.float32)],
                [near(part), near(filt), w, rim, weight, near(got_far)],
                scratch=[pltpu.VMEM((2, count, wide), jnp.float32)],
            )
    return out


def solution(mesh):
    placed = (
        P(None, "tile", "state", None),
        P(None, "tile", None),
        P(None, "tile", None),
        P(None, "tile", None),
        P("tile", None),
        P("tile", None, None, None),
        P(),
    )
    return jax.shard_map(
        body, mesh=mesh, in_specs=placed, out_specs=P(None, "tile", "state", None), check_vma=False
    )
```

```python
import functools

import jax
import jax.numpy as jnp
from jax import lax
from jax.experimental import pallas as pl
from jax.experimental.pallas import tpu as pltpu
from jax.sharding import PartitionSpec as P

REACH = 8
LOCAL, MATE, FAR = 0, 1, 2
IN_VMEM = pl.BlockSpec(memory_space=pltpu.VMEM)
ANYWHERE = pl.BlockSpec(memory_space=pl.ANY)
PAIR = 2


def near(x):
    return pltpu.with_memory_space_constraint(x, pltpu.VMEM)


def outside(x):
    return pltpu.with_memory_space_constraint(x, pltpu.HBM)


def held(shape, dtype):
    return pltpu.VMEM(shape, dtype)


def dot(x, w, contract):
    return lax.dot_general(x, w, (((1,), (contract,)), ((), ())), preferred_element_type=jnp.float32)


def span(side, group, groups, step):
    if side == FAR:
        return slice(0, (groups - group) * step)
    if side == MATE:
        return slice((groups - 1 - group) * step, groups * step)
    return slice(0, groups * step)


def products(x, w_ref, side, contract, cols):
    step = PAIR * cols
    groups = w_ref.shape[1] // step
    for group in range(groups):
        outs = slice(group * step, (group + 1) * step)
        ins = span(side, group, groups, step)
        block = w_ref[side, ins, outs] if contract == 0 else w_ref[side, outs, ins]
        yield outs, dot(x[:, ins], block, contract)


def edge_of(x_ref, rim_ref, side, layer):
    wide = x_ref.shape[2]
    cols = rim_ref.shape[2]
    at = slice(0, cols) if side == FAR else slice(wide - cols, wide)
    value = x_ref[layer, :, at] * rim_ref[side - 1, layer : layer + 1, :]
    high = value.astype(jnp.bfloat16).astype(jnp.float32)
    return (high + pltpu.roll(value - high, cols - 1, axis=1)).astype(jnp.bfloat16)


def write_terms(first, w_ref, side, cols, out_ref):
    for outs, term in products(first, w_ref, side, 0, cols):
        out_ref[:, outs] = term.astype(jnp.bfloat16)


def write_payloads(x_ref, rim_ref, far_terms, mate_terms, rows_ref, terms_ref, mate_ref):
    wide = x_ref.shape[2]
    second = x_ref[1].astype(jnp.bfloat16)
    rows_ref[:, 0:wide] = second
    rows_ref[:, wide:] = edge_of(x_ref, rim_ref, FAR, 0)
    terms_ref[:, 0:wide] = far_terms[...]
    terms_ref[:, wide:] = edge_of(x_ref, rim_ref, FAR, 1)
    half = mate_ref.shape[1] // 2
    mate_ref[:, 0:wide] = second
    mate_ref[:, wide:half] = edge_of(x_ref, rim_ref, MATE, 0)
    mate_ref[:, half : half + wide] = mate_terms[...]
    mate_ref[:, half + wide :] = edge_of(x_ref, rim_ref, MATE, 1)


def edge_sum(edge, rim_ref, side, layer):
    edge = edge.astype(jnp.float32)
    return (edge + pltpu.roll(edge, 1, axis=1)) * rim_ref[side - 1, layer : layer + 1, :]


def add_rows(scale, got, w_ref, rim_ref, side, base, to_ref):
    for outs, term in products(got, w_ref, side, 1, rim_ref.shape[2]):
        to_ref[:, outs] = base[:, outs] + scale * term


def add_edge(scale, edge, rim_ref, side, layer, to_ref):
    wide = to_ref.shape[1]
    cols = rim_ref.shape[2]
    at = slice(0, cols) if side == FAR else slice(wide - cols, wide)
    to_ref[:, at] += scale * edge_sum(edge, rim_ref, side, layer)


def prepare(
    partner_hbm, states_hbm, onsite_hbm, hop_row_hbm, hop_up_hbm, coefs_hbm, coupling_hbm,
    x_ref, w_ref, coef_ref, rim_ref, weight_ref, rows_ref, terms_ref, mate_ref,
    partner_ref, states_ref, small_ref, coefs_ref, blocks, total, far_terms, mate_terms, sems, row_sems,
):
    rows, slots = partner_hbm.shape
    cols = onsite_hbm.shape[2]
    tile = lax.axis_index("tile")
    all_rows = rows * lax.axis_size("tile")
    here = lax.rem(tile, 2)
    offsets = 2 * REACH + 1
    spare = offsets + 1

    def kept(place):
        return place + here * (rows - 1 - 2 * place)

    copies = [
        pltpu.make_async_copy(src, dst, sems.at[i])
        for i, (src, dst) in enumerate(
            (
                (partner_hbm, partner_ref),
                (hop_up_hbm, small_ref.at[0]),
                (onsite_hbm, small_ref.at[1]),
                (hop_row_hbm, small_ref.at[2]),
                (coefs_hbm, coefs_ref),
                (states_hbm, states_ref),
            )
        )
    ]

    def fetch(r):
        return pltpu.make_async_copy(coupling_hbm.at[r], blocks.at[r], row_sems.at[r])

    copies[0].start()
    for place in range(rows):
        fetch(kept(place)).start()
    for copy in copies[1:]:
        copy.start()

    total[...] = jnp.zeros_like(total)
    for side, place, sigma in (
        [(FAR, p, rows - p) for p in range(1, rows, PAIR)]
        + [(MATE, p, rows - PAIR - p) for p in range(0, rows, PAIR)]
    ):
        w_ref[side, place * cols : (place + 1) * cols, sigma * cols : (sigma + 1) * cols] = jnp.zeros(
            (cols, cols), jnp.bfloat16
        )

    for copy in copies:
        copy.wait()
    for n in range(coefs_ref.shape[0]):
        weight_ref[n : n + 1, :] = jnp.full((1, cols), coefs_ref[n], jnp.float32)
    column = lax.broadcasted_iota(jnp.int32, (rows, cols), 1)
    parity = lax.broadcasted_iota(jnp.int32, (rows, cols), 0) + column + tile * rows
    odd = lax.rem(column[0:1], 2) == 1
    for layer in range(2):
        bond = jnp.where(lax.rem(parity, 2) == 0, small_ref[0, layer], 0.0)
        hop_row = small_ref[2, layer]
        left = pltpu.roll(hop_row, 1, axis=1)
        for place in range(rows):
            back = rows - 1 - place
            at = slice(place, place + 1)

            def ours(value):
                return jnp.where(here == 0, value[at], value[back : back + 1])

            coef_ref[layer, 0, at] = ours(small_ref[1, layer])
            coef_ref[layer, 1, at] = ours(hop_row)
            coef_ref[layer, 2, at] = ours(left)
            if place < rows - 1:
                coef_ref[layer, 3, at] = jnp.where(here == 0, bond[at], bond[back - 1 : back])
            if place > 0:
                coef_ref[layer, 4, at] = jnp.where(here == 0, bond[place - 1 : place], bond[back : back + 1])
        last = bond[rows - 1 :]
        raw = jnp.where(odd, 1.0, 0.0)
        rim_ref[FAR - 1, layer : layer + 1] = jnp.where(here == 0, raw, last)
        rim_ref[MATE - 1, layer : layer + 1] = jnp.where(here == 0, last, raw)
        for place in range(rows):
            x_ref[layer, :, place * cols : (place + 1) * cols] = states_ref[layer, kept(place)]

    for place in range(rows):
        row = kept(place)
        fetch(row).wait()
        for k in range(slots):
            slot = partner_ref[row, k]
            away = slot - tile * rows - row
            away = jnp.where(away > all_rows // 2, away - all_rows, away)
            away = jnp.where(away < -(all_rows // 2), away + all_rows, away)
            at = jnp.where(slot >= 0, REACH + (1 - 2 * here) * away, offsets) + place * spare
            total[at] += blocks[row, k].astype(jnp.float32)
        for offset in range(offsets):
            reached = place + offset - REACH
            if reached < 0:
                side, sigma = FAR, -1 - reached
            elif reached < rows:
                side, sigma = LOCAL, reached
            else:
                side, sigma = MATE, 2 * rows - 1 - reached
            w_ref[side, place * cols : (place + 1) * cols, sigma * cols : (sigma + 1) * cols] = total[
                place * spare + offset
            ].astype(jnp.bfloat16)
    first = x_ref[0].astype(jnp.bfloat16)
    write_terms(first, w_ref, FAR, cols, far_terms)
    write_terms(first, w_ref, MATE, cols, mate_terms)
    write_payloads(x_ref, rim_ref, far_terms, mate_terms, rows_ref, terms_ref, mate_ref)


def inner(order, *refs):
    if order == 0:
        x_ref, w_ref, coef_ref, weight_ref, sum_ref, filt_out = refs
        scale = 1.0 / 12.0
    else:
        x_ref, prev_ref, filt_ref, w_ref, coef_ref, weight_ref, sum_ref, filt_out = refs
        scale = 2.0 / 12.0
    wide = x_ref.shape[2]
    cols = weight_ref.shape[1]
    rows = wide // cols
    first = x_ref[0].astype(jnp.bfloat16)
    second = x_ref[1].astype(jnp.bfloat16)
    for outs, term in products(second, w_ref, LOCAL, 1, cols):
        sum_ref[0, :, outs] = scale * term
    for outs, term in products(first, w_ref, LOCAL, 0, cols):
        sum_ref[1, :, outs] = scale * term
    for layer in range(2):
        for r in range(rows):
            here = slice(r * cols, (r + 1) * cols)
            x = x_ref[layer, :, here]

            def factor(i):
                return coef_ref[layer, i, r : r + 1, :]

            hop = factor(0) * x
            hop += factor(1) * pltpu.roll(x, cols - 1, axis=1)
            hop += factor(2) * pltpu.roll(x, 1, axis=1)
            if r < rows - 1:
                hop += factor(3) * x_ref[layer, :, (r + 1) * cols : (r + 2) * cols]
            if r > 0:
                hop += factor(4) * x_ref[layer, :, (r - 1) * cols : r * cols]
            term = sum_ref[layer, :, here] + scale * hop
            filt = weight_ref[order : order + 1, :] * x
            if order > 0:
                term -= prev_ref[layer, :, here]
                filt += filt_ref[layer, :, here]
            filt_out[layer, :, here] = filt
            sum_ref[layer, :, here] = term


def from_mate(scale, part_ref, w_ref, rim_ref, got_ref, sum_ref):
    wide = sum_ref.shape[2]
    half = got_ref.shape[1] // 2
    add_rows(scale, got_ref[:, 0:wide], w_ref, rim_ref, MATE, part_ref[0], sum_ref.at[0])
    add_edge(scale, got_ref[:, wide:half], rim_ref, MATE, 0, sum_ref.at[0])
    sum_ref[1] = part_ref[1] + scale * got_ref[:, half : half + wide].astype(jnp.float32)
    add_edge(scale, got_ref[:, half + wide :], rim_ref, MATE, 1, sum_ref.at[1])


def outer_first(scale, last, sum_ref, w_ref, rim_ref, rows_ref, first_ref, *terms):
    wide = sum_ref.shape[2]
    cols = rim_ref.shape[2]
    add_rows(scale, rows_ref[:, 0:wide], w_ref, rim_ref, FAR, sum_ref[0], first_ref)
    add_edge(scale, rows_ref[:, wide:], rim_ref, FAR, 0, first_ref)
    if not last:
        first = first_ref[...].astype(jnp.bfloat16)
        write_terms(first, w_ref, FAR, cols, terms[0])
        write_terms(first, w_ref, MATE, cols, terms[1])


def add_terms(scale, sum_ref, rim_ref, terms_ref, second_ref):
    wide = sum_ref.shape[2]
    second_ref[...] = sum_ref[1] + scale * terms_ref[:, 0:wide].astype(jnp.float32)
    add_edge(scale, terms_ref[:, wide:], rim_ref, FAR, 1, second_ref)


def outer_second(
    scale, sum_ref, first_ref, far_ref, near_ref, rim_ref, got_ref, x_ref, rows_ref, terms_ref, mate_ref
):
    x_ref[0] = first_ref[...]
    add_terms(scale, sum_ref, rim_ref, got_ref, x_ref.at[1])
    write_payloads(x_ref, rim_ref, far_ref, near_ref, rows_ref, terms_ref, mate_ref)


def finish(scale, degree, sum_ref, first_ref, filt_ref, rim_ref, weight_ref, got_ref, out_ref, second_ref):
    cols = rim_ref.shape[2]
    rows = out_ref.shape[1]
    add_terms(scale, sum_ref, rim_ref, got_ref, second_ref)
    flip = lax.rem(lax.axis_index("tile"), 2)
    for layer, x_ref in enumerate((first_ref, second_ref)):
        for place in range(rows):
            here = slice(place * cols, (place + 1) * cols)
            out_ref[layer, place + flip * (rows - 1 - 2 * place)] = (
                filt_ref[layer, :, here] + weight_ref[degree : degree + 1, :] * x_ref[:, here]
            )


def call(kernel, outs, args, scratch=(), specs=None, limit=12):
    return pl.pallas_call(
        kernel,
        out_shape=outs,
        in_specs=specs or [IN_VMEM] * len(args),
        out_specs=[IN_VMEM] * len(outs),
        scratch_shapes=list(scratch),
        cost_estimate=pl.CostEstimate(flops=1 << 20, bytes_accessed=1 << 12, transcendentals=0),
        compiler_params=pltpu.CompilerParams(vmem_limit_bytes=limit << 20),
    )(*args)


def body(states, onsite, hop_row, hop_up, partner, coupling, coefs):
    rows, count, cols = states.shape[1:]
    slots = partner.shape[1]
    wide = rows * cols
    degree = coefs.shape[0] - 1
    size = lax.axis_size("tile")
    far_pairs = [(i, (i + 1) % size if i % 2 else (i - 1) % size) for i in range(size)]
    mate_pairs = [(i, i ^ 1) for i in range(size)]

    field = held((2, count, wide), jnp.float32)
    layer = held((count, wide), jnp.float32)
    terms = held((count, wide), jnp.bfloat16)
    half = held((count, wide + cols), jnp.bfloat16)
    whole = held((count, 2 * (wide + cols)), jnp.bfloat16)
    x, w, coef, rim, weight, far_rows, far_terms, mate = call(
        prepare,
        [field, held((3, wide, wide), jnp.bfloat16), held((2, 5, rows, cols), jnp.float32),
         held((2, 2, cols), jnp.float32), held((degree + 1, cols), jnp.float32), half, half, whole],
        [outside(v) for v in (partner, states, onsite, hop_row, hop_up, coefs, coupling)],
        scratch=[
            pltpu.SMEM((rows, slots), jnp.int32),
            pltpu.VMEM((2, rows, count, cols), jnp.float32),
            pltpu.VMEM((3, 2, rows, cols), jnp.float32),
            pltpu.SMEM((degree + 1,), jnp.float32),
            pltpu.VMEM((rows, slots, cols, cols), jnp.bfloat16),
            pltpu.VMEM((rows * (2 * REACH + 2), cols, cols), jnp.float32),
            pltpu.VMEM((count, wide), jnp.bfloat16),
            pltpu.VMEM((count, wide), jnp.bfloat16),
            pltpu.SemaphoreType.DMA((6,)),
            pltpu.SemaphoreType.DMA((rows,)),
        ],
        specs=[ANYWHERE] * 7,
        limit=24,
    )
    w, coef, rim, weight, x = near(w), near(coef), near(rim), near(weight), near(x)
    prev = filt = None
    for order in range(degree):
        scale = 1.0 / 12.0 if order == 0 else 2.0 / 12.0
        got_rows = lax.ppermute(far_rows, "tile", far_pairs)
        got_terms = lax.ppermute(far_terms, "tile", far_pairs)
        got_mate = lax.ppermute(mate, "tile", mate_pairs)
        past = [] if order == 0 else [near(prev), near(filt)]
        part, filt = call(
            functools.partial(inner, order), [field, field], [x, *past, w, coef, weight]
        )
        (part,) = call(
            functools.partial(from_mate, scale), [field], [near(part), w, rim, near(got_mate)]
        )
        part = near(part)
        prev = x
        last = order == degree - 1
        first, *made = call(
            functools.partial(outer_first, scale, last),
            [layer] if last else [layer, terms, terms],
            [part, w, rim, near(got_rows)],
        )
        if not last:
            x, far_rows, far_terms, mate = call(
                functools.partial(outer_second, scale),
                [field, half, half, whole],
                [part, near(first), near(made[0]), near(made[1]), rim, near(got_terms)],
            )
            x = near(x)
        else:
            (out,) = call(
                functools.partial(finish, scale, degree),
                [jax.ShapeDtypeStruct(states.shape, jnp.float32)],
                [part, near(first), near(filt), rim, weight, near(got_terms)],
                scratch=[pltpu.VMEM((count, wide), jnp.float32)],
            )
    return out


def solution(mesh):
    placed = (
        P(None, "tile", "state", None),
        P(None, "tile", None),
        P(None, "tile", None),
        P(None, "tile", None),
        P("tile", None),
        P("tile", None, None, None),
        P(),
    )
    return jax.shard_map(
        body, mesh=mesh, in_specs=placed, out_specs=P(None, "tile", "state", None), check_vma=False
    )
```

```python
import functools

import jax
import jax.numpy as jnp
from jax import lax
from jax.experimental import pallas as pl
from jax.experimental.pallas import tpu as pltpu
from jax.sharding import PartitionSpec as P

REACH = 8
LOCAL, MATE, FAR = 0, 1, 2
IN_VMEM = pl.BlockSpec(memory_space=pltpu.VMEM)
ANYWHERE = pl.BlockSpec(memory_space=pl.ANY)
PAIR = 2


def near(x):
    return pltpu.with_memory_space_constraint(x, pltpu.VMEM)


def outside(x):
    return pltpu.with_memory_space_constraint(x, pltpu.HBM)


def held(shape, dtype):
    return pltpu.VMEM(shape, dtype)


def dot(x, w, contract):
    return lax.dot_general(x, w, (((1,), (contract,)), ((), ())), preferred_element_type=jnp.float32)


def span(side, group, groups, step):
    if side == FAR:
        return slice(0, (groups - group) * step)
    if side == MATE:
        return slice((groups - 1 - group) * step, groups * step)
    return slice(0, groups * step)


def products(x, w_ref, side, contract, cols):
    step = PAIR * cols
    groups = w_ref.shape[1] // step
    for group in range(groups):
        outs = slice(group * step, (group + 1) * step)
        ins = span(side, group, groups, step)
        block = w_ref[side, ins, outs] if contract == 0 else w_ref[side, outs, ins]
        yield outs, dot(x[:, ins], block, contract)


def write_payload(x_ref, w_ref, rim_ref, side, out_ref):
    wide = x_ref.shape[2]
    cols = rim_ref.shape[2]
    edge = slice(0, cols) if side == FAR else slice(wide - cols, wide)
    which = side - 1
    out_ref[:, 0:wide] = x_ref[1].astype(jnp.bfloat16)
    rim = x_ref[0, :, edge] * rim_ref[which, 0:1, :]
    rim += pltpu.roll(x_ref[1, :, edge] * rim_ref[which, 1:2, :], cols - 1, axis=1)
    high = rim.astype(jnp.bfloat16)
    out_ref[:, 2 * wide : 2 * wide + cols] = high
    out_ref[:, 2 * wide + cols : 2 * wide + 2 * cols] = (rim - high.astype(jnp.float32)).astype(
        jnp.bfloat16
    )
    spare = out_ref.shape[1] - 2 * wide - 2 * cols
    if spare:
        out_ref[:, 2 * wide + 2 * cols :] = jnp.zeros((out_ref.shape[0], spare), jnp.bfloat16)
    first = x_ref[0].astype(jnp.bfloat16)
    for outs, term in products(first, w_ref, side, 0, cols):
        out_ref[:, wide + outs.start : wide + outs.stop] = term.astype(jnp.bfloat16)


def add_received(scale, got_ref, w_ref, rim_ref, side, from_ref, to_ref):
    wide = to_ref.shape[2]
    cols = rim_ref.shape[2]
    edge = slice(0, cols) if side == FAR else slice(wide - cols, wide)
    which = side - 1
    to_ref[1] = from_ref[1] + scale * got_ref[:, wide : 2 * wide].astype(jnp.float32)
    for outs, term in products(got_ref[:, 0:wide], w_ref, side, 1, cols):
        to_ref[0, :, outs] = from_ref[0, :, outs] + scale * term
    rim = got_ref[:, 2 * wide : 2 * wide + cols].astype(jnp.float32)
    rim += got_ref[:, 2 * wide + cols : 2 * wide + 2 * cols].astype(jnp.float32)
    to_ref[0, :, edge] += scale * (rim * rim_ref[which, 0:1, :])
    to_ref[1, :, edge] += scale * (pltpu.roll(rim, 1, axis=1) * rim_ref[which, 1:2, :])


def prepare(
    partner_hbm, states_hbm, onsite_hbm, hop_row_hbm, hop_up_hbm, coefs_hbm, coupling_hbm,
    x_ref, w_ref, coef_ref, rim_ref, weight_ref, far_ref,
    partner_ref, states_ref, small_ref, coefs_ref, blocks, sems, row_sems, *totals,
):
    rows, slots = partner_hbm.shape
    cols = onsite_hbm.shape[2]
    tile = lax.axis_index("tile")
    all_rows = rows * lax.axis_size("tile")
    here = lax.rem(tile, 2)
    offsets = 2 * REACH + 1

    def kept(place):
        return place + here * (rows - 1 - 2 * place)

    copies = [
        pltpu.make_async_copy(src, dst, sems.at[i])
        for i, (src, dst) in enumerate(
            (
                (partner_hbm, partner_ref),
                (hop_up_hbm, small_ref.at[0]),
                (onsite_hbm, small_ref.at[1]),
                (hop_row_hbm, small_ref.at[2]),
                (coefs_hbm, coefs_ref),
                (states_hbm, states_ref),
            )
        )
    ]

    def fetch(r):
        return pltpu.make_async_copy(coupling_hbm.at[r], blocks.at[r], row_sems.at[r])

    copies[0].start()
    for place in range(rows):
        fetch(kept(place)).start()
    for copy in copies[1:]:
        copy.start()

    for total in totals:
        total[...] = jnp.zeros_like(total)
    for side, place, sigma in (
        [(FAR, p, rows - p) for p in range(1, rows, PAIR)]
        + [(MATE, p, rows - PAIR - p) for p in range(0, rows, PAIR)]
    ):
        w_ref[side, place * cols : (place + 1) * cols, sigma * cols : (sigma + 1) * cols] = jnp.zeros(
            (cols, cols), jnp.bfloat16
        )

    for copy in copies:
        copy.wait()
    for n in range(coefs_ref.shape[0]):
        weight_ref[n : n + 1, :] = jnp.full((1, cols), coefs_ref[n], jnp.float32)
    column = lax.broadcasted_iota(jnp.int32, (rows, cols), 1)
    parity = lax.broadcasted_iota(jnp.int32, (rows, cols), 0) + column + tile * rows
    odd = lax.rem(column[0:1], 2) == 1
    for layer in range(2):
        bond = jnp.where(lax.rem(parity, 2) == 0, small_ref[0, layer], 0.0)
        hop_row = small_ref[2, layer]
        left = pltpu.roll(hop_row, 1, axis=1)
        for place in range(rows):
            back = rows - 1 - place
            at = slice(place, place + 1)

            def ours(value):
                return jnp.where(here == 0, value[at], value[back : back + 1])

            coef_ref[layer, 0, at] = ours(small_ref[1, layer])
            coef_ref[layer, 1, at] = ours(hop_row)
            coef_ref[layer, 2, at] = ours(left)
            if place < rows - 1:
                coef_ref[layer, 3, at] = jnp.where(here == 0, bond[at], bond[back - 1 : back])
            if place > 0:
                coef_ref[layer, 4, at] = jnp.where(here == 0, bond[place - 1 : place], bond[back : back + 1])
        last = bond[rows - 1 :]
        raw = jnp.where(odd, 1.0, 0.0)
        rim_ref[FAR - 1, layer : layer + 1] = jnp.where(here == 0, raw, last)
        rim_ref[MATE - 1, layer : layer + 1] = jnp.where(here == 0, last, raw)
        for place in range(rows):
            x_ref[layer, :, place * cols : (place + 1) * cols] = states_ref[layer, kept(place)]

    for pair in range(0, rows, PAIR):
        places = range(pair, pair + PAIR)
        for place in places:
            fetch(kept(place)).wait()
        for k in range(slots):
            for place in places:
                row = kept(place)
                slot = partner_ref[row, k]
                away = slot - tile * rows - row
                away = jnp.where(away > all_rows // 2, away - all_rows, away)
                away = jnp.where(away < -(all_rows // 2), away + all_rows, away)
                at = jnp.where(slot >= 0, REACH + (1 - 2 * here) * away, offsets)
                totals[place][at] += blocks[row, k].astype(jnp.float32)
        for place in places:
            for offset in range(offsets):
                reached = place + offset - REACH
                if reached < 0:
                    side, sigma = FAR, -1 - reached
                elif reached < rows:
                    side, sigma = LOCAL, reached
                else:
                    side, sigma = MATE, 2 * rows - 1 - reached
                w_ref[
                    side, place * cols : (place + 1) * cols, sigma * cols : (sigma + 1) * cols
                ] = totals[place][offset].astype(jnp.bfloat16)
    write_payload(x_ref, w_ref, rim_ref, FAR, far_ref)


def to_mate(x_ref, w_ref, rim_ref, mate_ref):
    write_payload(x_ref, w_ref, rim_ref, MATE, mate_ref)


def inner(order, *refs):
    if order == 0:
        x_ref, w_ref, coef_ref, weight_ref, sum_ref, filt_out = refs
        scale = 1.0 / 12.0
    else:
        x_ref, prev_ref, filt_ref, w_ref, coef_ref, weight_ref, sum_ref, filt_out = refs
        scale = 2.0 / 12.0
    wide = x_ref.shape[2]
    cols = weight_ref.shape[1]
    rows = wide // cols
    first = x_ref[0].astype(jnp.bfloat16)
    second = x_ref[1].astype(jnp.bfloat16)
    for outs, term in products(second, w_ref, LOCAL, 1, cols):
        sum_ref[0, :, outs] = scale * term
    for outs, term in products(first, w_ref, LOCAL, 0, cols):
        sum_ref[1, :, outs] = scale * term
    for layer in range(2):
        for r in range(rows):
            here = slice(r * cols, (r + 1) * cols)
            x = x_ref[layer, :, here]

            def factor(i):
                return coef_ref[layer, i, r : r + 1, :]

            hop = factor(0) * x
            hop += factor(1) * pltpu.roll(x, cols - 1, axis=1)
            hop += factor(2) * pltpu.roll(x, 1, axis=1)
            if r < rows - 1:
                hop += factor(3) * x_ref[layer, :, (r + 1) * cols : (r + 2) * cols]
            if r > 0:
                hop += factor(4) * x_ref[layer, :, (r - 1) * cols : r * cols]
            term = sum_ref[layer, :, here] + scale * hop
            filt = weight_ref[order : order + 1, :] * x
            if order > 0:
                term -= prev_ref[layer, :, here]
                filt += filt_ref[layer, :, here]
            filt_out[layer, :, here] = filt
            sum_ref[layer, :, here] = term


def from_mate(scale, part_ref, w_ref, rim_ref, got_ref, sum_ref):
    add_received(scale, got_ref, w_ref, rim_ref, MATE, part_ref, sum_ref)


def outer(scale, sum_ref, w_ref, rim_ref, got_ref, x_ref, far_ref):
    add_received(scale, got_ref, w_ref, rim_ref, FAR, sum_ref, x_ref)
    write_payload(x_ref, w_ref, rim_ref, FAR, far_ref)


def finish(scale, degree, sum_ref, filt_ref, w_ref, rim_ref, weight_ref, got_ref, out_ref, x_ref):
    cols = rim_ref.shape[2]
    rows = out_ref.shape[1]
    add_received(scale, got_ref, w_ref, rim_ref, FAR, sum_ref, x_ref)
    flip = lax.rem(lax.axis_index("tile"), 2)
    for layer in range(2):
        for place in range(rows):
            here = slice(place * cols, (place + 1) * cols)
            out_ref[layer, place + flip * (rows - 1 - 2 * place)] = (
                filt_ref[layer, :, here] + weight_ref[degree : degree + 1, :] * x_ref[layer, :, here]
            )


def call(kernel, outs, args, scratch=(), specs=None, limit=12, flops=1 << 20):
    return pl.pallas_call(
        kernel,
        out_shape=outs,
        in_specs=specs or [IN_VMEM] * len(args),
        out_specs=[IN_VMEM] * len(outs),
        scratch_shapes=list(scratch),
        cost_estimate=pl.CostEstimate(flops=flops, bytes_accessed=0, transcendentals=0),
        compiler_params=pltpu.CompilerParams(vmem_limit_bytes=limit << 20),
    )(*args)


def body(states, onsite, hop_row, hop_up, partner, coupling, coefs):
    rows, count, cols = states.shape[1:]
    slots = partner.shape[1]
    wide = rows * cols
    degree = coefs.shape[0] - 1
    size = lax.axis_size("tile")
    far_pairs = [(i, (i + 1) % size if i % 2 else (i - 1) % size) for i in range(size)]
    mate_pairs = [(i, i ^ 1) for i in range(size)]

    field = held((2, count, wide), jnp.float32)
    payload = held((count, 2 * wide + 2 * cols), jnp.bfloat16)
    longer = held((count, 2 * wide + 3 * cols), jnp.bfloat16)
    x, w, coef, rim, weight, far = call(
        prepare,
        [field, held((3, wide, wide), jnp.bfloat16), held((2, 5, rows, cols), jnp.float32),
         held((2, 2, cols), jnp.float32), held((degree + 1, cols), jnp.float32), longer],
        [outside(v) for v in (partner, states, onsite, hop_row, hop_up, coefs, coupling)],
        scratch=[
            pltpu.SMEM((rows, slots), jnp.int32),
            pltpu.VMEM((2, rows, count, cols), jnp.float32),
            pltpu.VMEM((3, 2, rows, cols), jnp.float32),
            pltpu.SMEM((degree + 1,), jnp.float32),
            pltpu.VMEM((rows, slots, cols, cols), jnp.bfloat16),
            pltpu.SemaphoreType.DMA((6,)),
            pltpu.SemaphoreType.DMA((rows,)),
            *[pltpu.VMEM((2 * REACH + 2, cols, cols), jnp.float32)] * rows,
        ],
        specs=[ANYWHERE] * 7,
        limit=24,
    )
    w, coef, rim, weight, x = near(w), near(coef), near(rim), near(weight), near(x)
    prev = filt = None
    for order in range(degree):
        scale = 1.0 / 12.0 if order == 0 else 2.0 / 12.0
        got_far = lax.ppermute(far, "tile", far_pairs)
        past = [] if order == 0 else [near(prev), near(filt)]
        (mate,) = call(to_mate, [payload], [x, w, rim])
        got_mate = lax.ppermute(mate, "tile", mate_pairs)
        part, filt = call(
            functools.partial(inner, order), [field, field], [x, *past, w, coef, weight]
        )
        (part,) = call(
            functools.partial(from_mate, scale), [field], [near(part), w, rim, near(got_mate)], flops=0
        )
        prev = x
        if order < degree - 1:
            x, far = call(
                functools.partial(outer, scale),
                [field, longer],
                [near(part), w, rim, near(got_far)],
            )
            x = near(x)
        else:
            (out,) = call(
                functools.partial(finish, scale, degree),
                [jax.ShapeDtypeStruct(states.shape, jnp.float32)],
                [near(part), near(filt), w, rim, weight, near(got_far)],
                scratch=[pltpu.VMEM((2, count, wide), jnp.float32)],
            )
    return out


def solution(mesh):
    placed = (
        P(None, "tile", "state", None),
        P(None, "tile", None),
        P(None, "tile", None),
        P(None, "tile", None),
        P("tile", None),
        P("tile", None, None, None),
        P(),
    )
    return jax.shard_map(
        body, mesh=mesh, in_specs=placed, out_specs=P(None, "tile", "state", None), check_vma=False
    )
```

```python
import functools

import jax
import jax.numpy as jnp
from jax import lax
from jax.experimental import pallas as pl
from jax.experimental.pallas import tpu as pltpu
from jax.sharding import PartitionSpec as P

REACH = 8
LOCAL, MATE, FAR = 0, 1, 2
IN_VMEM = pl.BlockSpec(memory_space=pltpu.VMEM)
ANYWHERE = pl.BlockSpec(memory_space=pl.ANY)
PAIR = 2


def near(x):
    return pltpu.with_memory_space_constraint(x, pltpu.VMEM)


def outside(x):
    return pltpu.with_memory_space_constraint(x, pltpu.HBM)


def held(shape, dtype):
    return pltpu.VMEM(shape, dtype)


def dot(x, w, contract):
    return lax.dot_general(x, w, (((1,), (contract,)), ((), ())), preferred_element_type=jnp.float32)


def span(side, group, groups, step):
    if side == FAR:
        return slice(0, (groups - group) * step)
    if side == MATE:
        return slice((groups - 1 - group) * step, groups * step)
    return slice(0, groups * step)


def products(x, w_ref, side, contract, cols):
    step = PAIR * cols
    groups = w_ref.shape[1] // step
    for group in range(groups):
        outs = slice(group * step, (group + 1) * step)
        ins = span(side, group, groups, step)
        block = w_ref[ins, outs] if contract == 0 else w_ref[outs, ins]
        yield outs, dot(x[:, ins], block, contract)


def write_payload(x_ref, w_ref, rim_ref, side, out_ref):
    wide = x_ref.shape[2]
    cols = rim_ref.shape[2]
    edge = slice(0, cols) if side == FAR else slice(wide - cols, wide)
    which = side - 1
    out_ref[:, 0:wide] = x_ref[1].astype(jnp.bfloat16)
    rim = x_ref[0, :, edge] * rim_ref[which, 0:1, :]
    rim += pltpu.roll(x_ref[1, :, edge] * rim_ref[which, 1:2, :], cols - 1, axis=1)
    high = rim.astype(jnp.bfloat16)
    out_ref[:, 2 * wide : 2 * wide + cols] = high
    out_ref[:, 2 * wide + cols : 2 * wide + 2 * cols] = (rim - high.astype(jnp.float32)).astype(
        jnp.bfloat16
    )
    spare = out_ref.shape[1] - 2 * wide - 2 * cols
    if spare:
        out_ref[:, 2 * wide + 2 * cols :] = jnp.zeros((out_ref.shape[0], spare), jnp.bfloat16)
    first = x_ref[0].astype(jnp.bfloat16)
    for outs, term in products(first, w_ref, side, 0, cols):
        out_ref[:, wide + outs.start : wide + outs.stop] = term.astype(jnp.bfloat16)


def add_received(scale, got_ref, w_ref, contract, rim_ref, side, from_ref, to_ref):
    wide = to_ref.shape[2]
    cols = rim_ref.shape[2]
    edge = slice(0, cols) if side == FAR else slice(wide - cols, wide)
    which = side - 1
    to_ref[1] = from_ref[1] + scale * got_ref[:, wide : 2 * wide].astype(jnp.float32)
    for outs, term in products(got_ref[:, 0:wide], w_ref, side, contract, cols):
        to_ref[0, :, outs] = from_ref[0, :, outs] + scale * term
    rim = got_ref[:, 2 * wide : 2 * wide + cols].astype(jnp.float32)
    rim += got_ref[:, 2 * wide + cols : 2 * wide + 2 * cols].astype(jnp.float32)
    to_ref[0, :, edge] += scale * (rim * rim_ref[which, 0:1, :])
    to_ref[1, :, edge] += scale * (pltpu.roll(rim, 1, axis=1) * rim_ref[which, 1:2, :])


def settle(totals, side, w_ref, cols):
    rows = len(totals)

    def block(place, sigma):
        return (slice(place * cols, (place + 1) * cols), slice(sigma * cols, (sigma + 1) * cols))

    if side == FAR:
        empty = [(place, rows - place) for place in range(1, rows, PAIR)]
    elif side == MATE:
        empty = [(place, rows - PAIR - place) for place in range(0, rows, PAIR)]
    else:
        empty = []
    for place, sigma in empty:
        w_ref[block(place, sigma)] = jnp.zeros((cols, cols), jnp.bfloat16)
    for place in range(rows):
        for offset in range(2 * REACH + 1):
            reached = place + offset - REACH
            if side == FAR and reached < 0:
                sigma = -1 - reached
            elif side == LOCAL and 0 <= reached < rows:
                sigma = reached
            elif side == MATE and reached >= rows:
                sigma = 2 * rows - 1 - reached
            else:
                continue
            w_ref[block(place, sigma)] = totals[place][offset].astype(jnp.bfloat16)


def prepare(
    partner_hbm, states_hbm, onsite_hbm, hop_row_hbm, hop_up_hbm, coefs_hbm, coupling_hbm,
    x_ref, w_ref, coef_ref, rim_ref, weight_ref, far_ref, *rest,
):
    *totals, partner_ref, states_ref, small_ref, coefs_ref, blocks, sems, row_sems = rest
    rows, slots = partner_hbm.shape
    cols = onsite_hbm.shape[2]
    tile = lax.axis_index("tile")
    all_rows = rows * lax.axis_size("tile")
    here = lax.rem(tile, 2)
    offsets = 2 * REACH + 1

    def kept(place):
        return place + here * (rows - 1 - 2 * place)

    copies = [
        pltpu.make_async_copy(src, dst, sems.at[i])
        for i, (src, dst) in enumerate(
            (
                (partner_hbm, partner_ref),
                (hop_up_hbm, small_ref.at[0]),
                (onsite_hbm, small_ref.at[1]),
                (hop_row_hbm, small_ref.at[2]),
                (coefs_hbm, coefs_ref),
                (states_hbm, states_ref),
            )
        )
    ]

    def fetch(r):
        return pltpu.make_async_copy(coupling_hbm.at[r], blocks.at[r], row_sems.at[r])

    copies[0].start()
    for place in range(rows):
        fetch(kept(place)).start()
    for copy in copies[1:]:
        copy.start()

    for total in totals:
        total[...] = jnp.zeros_like(total)
    for copy in copies:
        copy.wait()
    for n in range(coefs_ref.shape[0]):
        weight_ref[n : n + 1, :] = jnp.full((1, cols), coefs_ref[n], jnp.float32)
    column = lax.broadcasted_iota(jnp.int32, (rows, cols), 1)
    parity = lax.broadcasted_iota(jnp.int32, (rows, cols), 0) + column + tile * rows
    odd = lax.rem(column[0:1], 2) == 1
    for layer in range(2):
        bond = jnp.where(lax.rem(parity, 2) == 0, small_ref[0, layer], 0.0)
        hop_row = small_ref[2, layer]
        left = pltpu.roll(hop_row, 1, axis=1)
        for place in range(rows):
            back = rows - 1 - place
            at = slice(place, place + 1)

            def ours(value):
                return jnp.where(here == 0, value[at], value[back : back + 1])

            coef_ref[layer, 0, at] = ours(small_ref[1, layer])
            coef_ref[layer, 1, at] = ours(hop_row)
            coef_ref[layer, 2, at] = ours(left)
            if place < rows - 1:
                coef_ref[layer, 3, at] = jnp.where(here == 0, bond[at], bond[back - 1 : back])
            if place > 0:
                coef_ref[layer, 4, at] = jnp.where(here == 0, bond[place - 1 : place], bond[back : back + 1])
        last = bond[rows - 1 :]
        raw = jnp.where(odd, 1.0, 0.0)
        rim_ref[FAR - 1, layer : layer + 1] = jnp.where(here == 0, raw, last)
        rim_ref[MATE - 1, layer : layer + 1] = jnp.where(here == 0, last, raw)
        for place in range(rows):
            x_ref[layer, :, place * cols : (place + 1) * cols] = states_ref[layer, kept(place)]

    for pair in range(0, rows, PAIR):
        places = range(pair, pair + PAIR)
        for place in places:
            fetch(kept(place)).wait()
        for k in range(slots):
            for place in places:
                row = kept(place)
                slot = partner_ref[row, k]
                away = slot - tile * rows - row
                away = jnp.where(away > all_rows // 2, away - all_rows, away)
                away = jnp.where(away < -(all_rows // 2), away + all_rows, away)
                at = jnp.where(slot >= 0, REACH + (1 - 2 * here) * away, offsets)
                totals[place][at] += blocks[row, k].astype(jnp.float32)
    settle(totals, FAR, w_ref, cols)
    write_payload(x_ref, w_ref, rim_ref, FAR, far_ref)


def to_mate(x_ref, w_ref, rim_ref, mate_ref):
    write_payload(x_ref, w_ref, rim_ref, MATE, mate_ref)


def to_mate_first(x_ref, rim_ref, *refs):
    *totals, mate_ref, w_ref = refs
    settle(totals, MATE, w_ref, rim_ref.shape[2])
    write_payload(x_ref, w_ref, rim_ref, MATE, mate_ref)


def inner(order, *refs):
    if order == 0:
        x_ref, coef_ref, weight_ref, *totals, sum_ref, filt_out, w_ref = refs
        settle(totals, LOCAL, w_ref, weight_ref.shape[1])
        scale = 1.0 / 12.0
    else:
        x_ref, prev_ref, filt_ref, w_ref, coef_ref, weight_ref, sum_ref, filt_out = refs
        scale = 2.0 / 12.0
    wide = x_ref.shape[2]
    cols = weight_ref.shape[1]
    rows = wide // cols
    first = x_ref[0].astype(jnp.bfloat16)
    second = x_ref[1].astype(jnp.bfloat16)
    for outs, term in products(second, w_ref, LOCAL, 1, cols):
        sum_ref[0, :, outs] = scale * term
    for outs, term in products(first, w_ref, LOCAL, 0, cols):
        sum_ref[1, :, outs] = scale * term
    for layer in range(2):
        for r in range(rows):
            here = slice(r * cols, (r + 1) * cols)
            x = x_ref[layer, :, here]

            def factor(i):
                return coef_ref[layer, i, r : r + 1, :]

            hop = factor(0) * x
            hop += factor(1) * pltpu.roll(x, cols - 1, axis=1)
            hop += factor(2) * pltpu.roll(x, 1, axis=1)
            if r < rows - 1:
                hop += factor(3) * x_ref[layer, :, (r + 1) * cols : (r + 2) * cols]
            if r > 0:
                hop += factor(4) * x_ref[layer, :, (r - 1) * cols : r * cols]
            term = sum_ref[layer, :, here] + scale * hop
            filt = weight_ref[order : order + 1, :] * x
            if order > 0:
                term -= prev_ref[layer, :, here]
                filt += filt_ref[layer, :, here]
            filt_out[layer, :, here] = filt
            sum_ref[layer, :, here] = term


def from_mate(scale, part_ref, w_ref, rim_ref, got_ref, *refs):
    if len(refs) > 1:
        far_ref, sum_ref, *turned = refs
    else:
        (sum_ref,), turned = refs, []
    add_received(scale, got_ref, w_ref, 1, rim_ref, MATE, part_ref, sum_ref)
    if turned:
        step = PAIR * rim_ref.shape[2]
        groups = sum_ref.shape[2] // step
        for group in range(groups):
            outs = slice(group * step, (group + 1) * step)
            for other in range(groups - group):
                ins = slice(other * step, (other + 1) * step)
                turned[0][ins, outs] = far_ref[outs, ins].T


def outer(scale, sum_ref, w_ref, turned_ref, rim_ref, got_ref, x_ref, far_ref):
    add_received(scale, got_ref, turned_ref, 0, rim_ref, FAR, sum_ref, x_ref)
    write_payload(x_ref, w_ref, rim_ref, FAR, far_ref)


def finish(scale, degree, sum_ref, filt_ref, turned_ref, rim_ref, weight_ref, got_ref, out_ref, x_ref):
    cols = rim_ref.shape[2]
    rows = out_ref.shape[1]
    add_received(scale, got_ref, turned_ref, 0, rim_ref, FAR, sum_ref, x_ref)
    flip = lax.rem(lax.axis_index("tile"), 2)
    for layer in range(2):
        for place in range(rows):
            here = slice(place * cols, (place + 1) * cols)
            out_ref[layer, place + flip * (rows - 1 - 2 * place)] = (
                filt_ref[layer, :, here] + weight_ref[degree : degree + 1, :] * x_ref[layer, :, here]
            )


def call(kernel, outs, args, scratch=(), specs=None, limit=12, flops=1 << 20):
    return pl.pallas_call(
        kernel,
        out_shape=outs,
        in_specs=specs or [IN_VMEM] * len(args),
        out_specs=[IN_VMEM] * len(outs),
        scratch_shapes=list(scratch),
        cost_estimate=pl.CostEstimate(flops=flops, bytes_accessed=0, transcendentals=0),
        compiler_params=pltpu.CompilerParams(vmem_limit_bytes=limit << 20),
    )(*args)


def body(states, onsite, hop_row, hop_up, partner, coupling, coefs):
    rows, count, cols = states.shape[1:]
    slots = partner.shape[1]
    wide = rows * cols
    degree = coefs.shape[0] - 1
    size = lax.axis_size("tile")
    far_pairs = [(i, (i + 1) % size if i % 2 else (i - 1) % size) for i in range(size)]
    mate_pairs = [(i, i ^ 1) for i in range(size)]

    field = held((2, count, wide), jnp.float32)
    payload = held((count, 2 * wide + 2 * cols), jnp.bfloat16)
    longer = held((count, 2 * wide + 3 * cols), jnp.bfloat16)
    matrix = held((wide, wide), jnp.bfloat16)
    x, w_far, coef, rim, weight, far, *totals = call(
        prepare,
        [field, matrix, held((2, 5, rows, cols), jnp.float32),
         held((2, 2, cols), jnp.float32), held((degree + 1, cols), jnp.float32), longer,
         *[held((2 * REACH + 2, cols, cols), jnp.float32)] * rows],
        [outside(v) for v in (partner, states, onsite, hop_row, hop_up, coefs, coupling)],
        scratch=[
            pltpu.SMEM((rows, slots), jnp.int32),
            pltpu.VMEM((2, rows, count, cols), jnp.float32),
            pltpu.VMEM((3, 2, rows, cols), jnp.float32),
            pltpu.SMEM((degree + 1,), jnp.float32),
            pltpu.VMEM((rows, slots, cols, cols), jnp.bfloat16),
            pltpu.SemaphoreType.DMA((6,)),
            pltpu.SemaphoreType.DMA((rows,)),
        ],
        specs=[ANYWHERE] * 7,
        limit=24,
    )
    w_far, coef, rim, weight, x = near(w_far), near(coef), near(rim), near(weight), near(x)
    totals = [near(total) for total in totals]
    prev = filt = None
    for order in range(degree):
        scale = 1.0 / 12.0 if order == 0 else 2.0 / 12.0
        got_far = lax.ppermute(far, "tile", far_pairs)
        if order == 0:
            mate, w_mate = call(to_mate_first, [payload, matrix], [x, rim, *totals])
            w_mate = near(w_mate)
        else:
            (mate,) = call(to_mate, [payload], [x, w_mate, rim])
        got_mate = lax.ppermute(mate, "tile", mate_pairs)
        if order == 0:
            part, filt, w_local = call(
                functools.partial(inner, order), [field, field, matrix], [x, coef, weight, *totals]
            )
            w_local = near(w_local)
        else:
            part, filt = call(
                functools.partial(inner, order),
                [field, field],
                [x, near(prev), near(filt), w_local, coef, weight],
            )
        part, *turned_now = call(
            functools.partial(from_mate, scale),
            [field, matrix] if order == 0 else [field],
            [near(part), w_mate, rim, near(got_mate)] + ([w_far] if order == 0 else []),
            flops=0,
        )
        if order == 0:
            turned = near(turned_now[0])
        prev = x
        if order < degree - 1:
            x, far = call(
                functools.partial(outer, scale),
                [field, longer],
                [near(part), w_far, turned, rim, near(got_far)],
            )
            x = near(x)
        else:
            (out,) = call(
                functools.partial(finish, scale, degree),
                [jax.ShapeDtypeStruct(states.shape, jnp.float32)],
                [near(part), near(filt), turned, rim, weight, near(got_far)],
                scratch=[pltpu.VMEM((2, count, wide), jnp.float32)],
            )
    return out


def solution(mesh):
    placed = (
        P(None, "tile", "state", None),
        P(None, "tile", None),
        P(None, "tile", None),
        P(None, "tile", None),
        P("tile", None),
        P("tile", None, None, None),
        P(),
    )
    return jax.shard_map(
        body, mesh=mesh, in_specs=placed, out_specs=P(None, "tile", "state", None), check_vma=False
    )
```

```python
import functools

import jax
import jax.numpy as jnp
from jax import lax
from jax.experimental import pallas as pl
from jax.experimental.pallas import tpu as pltpu
from jax.sharding import PartitionSpec as P

REACH = 8
LOCAL, MATE, FAR = 0, 1, 2
IN_VMEM = pl.BlockSpec(memory_space=pltpu.VMEM)
ANYWHERE = pl.BlockSpec(memory_space=pl.ANY)
PAIR = 2


def near(x):
    return pltpu.with_memory_space_constraint(x, pltpu.VMEM)


def outside(x):
    return pltpu.with_memory_space_constraint(x, pltpu.HBM)


def held(shape, dtype):
    return pltpu.VMEM(shape, dtype)


def dot(x, w, contract):
    return lax.dot_general(x, w, (((1,), (contract,)), ((), ())), preferred_element_type=jnp.float32)


def span(side, group, groups, step):
    if side == FAR:
        return slice(0, (groups - group) * step)
    if side == MATE:
        return slice((groups - 1 - group) * step, groups * step)
    return slice(0, groups * step)


def products(x, w_ref, side, contract, cols):
    step = PAIR * cols
    groups = w_ref.shape[1] // step
    for group in range(groups):
        outs = slice(group * step, (group + 1) * step)
        ins = span(side, group, groups, step)
        block = w_ref[ins, outs] if contract == 0 else w_ref[outs, ins]
        yield outs, dot(x[:, ins], block, contract)


def write_payload(x_ref, w_ref, rim_ref, side, rows_ref, terms_ref):
    wide = x_ref.shape[2]
    cols = rim_ref.shape[2]
    edge = slice(0, cols) if side == FAR else slice(wide - cols, wide)
    which = side - 1
    rows_ref[:, 0:wide] = x_ref[1].astype(jnp.bfloat16)
    rim = x_ref[0, :, edge] * rim_ref[which, 0:1, :]
    rim += pltpu.roll(x_ref[1, :, edge] * rim_ref[which, 1:2, :], cols - 1, axis=1)
    high = rim.astype(jnp.bfloat16)
    rows_ref[:, wide : wide + cols] = high
    rows_ref[:, wide + cols :] = (rim - high.astype(jnp.float32)).astype(jnp.bfloat16)
    first = x_ref[0].astype(jnp.bfloat16)
    for outs, term in products(first, w_ref, side, 0, cols):
        terms_ref[:, outs] = term.astype(jnp.bfloat16)


def write_far(x_ref, w_ref, rim_ref, far_ref):
    cut = far_ref.shape[1] - x_ref.shape[2]
    write_payload(x_ref, w_ref, rim_ref, FAR, far_ref.at[:, 0:cut], far_ref.at[:, cut:])


def add_received(scale, rows_ref, terms_ref, w_ref, contract, rim_ref, side, from_ref, to_ref):
    wide = to_ref.shape[2]
    cols = rim_ref.shape[2]
    edge = slice(0, cols) if side == FAR else slice(wide - cols, wide)
    which = side - 1
    to_ref[1] = from_ref[1] + scale * terms_ref[...].astype(jnp.float32)
    for outs, term in products(rows_ref[:, 0:wide], w_ref, side, contract, cols):
        to_ref[0, :, outs] = from_ref[0, :, outs] + scale * term
    rim = rows_ref[:, wide : wide + cols].astype(jnp.float32)
    rim += rows_ref[:, wide + cols :].astype(jnp.float32)
    to_ref[0, :, edge] += scale * (rim * rim_ref[which, 0:1, :])
    to_ref[1, :, edge] += scale * (pltpu.roll(rim, 1, axis=1) * rim_ref[which, 1:2, :])


def add_far(scale, got_ref, turned_ref, rim_ref, from_ref, to_ref):
    cut = got_ref.shape[1] - to_ref.shape[2]
    add_received(
        scale, got_ref.at[:, 0:cut], got_ref.at[:, cut:], turned_ref, 0, rim_ref, FAR, from_ref, to_ref
    )


def settle(totals, side, w_ref, cols):
    rows = len(totals)

    def block(place, sigma):
        return (slice(place * cols, (place + 1) * cols), slice(sigma * cols, (sigma + 1) * cols))

    if side == FAR:
        empty = [(place, rows - place) for place in range(1, rows, PAIR)]
    elif side == MATE:
        empty = [(place, rows - PAIR - place) for place in range(0, rows, PAIR)]
    else:
        empty = []
    for place, sigma in empty:
        w_ref[block(place, sigma)] = jnp.zeros((cols, cols), jnp.bfloat16)
    for place in range(rows):
        for offset in range(2 * REACH + 1):
            reached = place + offset - REACH
            if side == FAR and reached < 0:
                sigma = -1 - reached
            elif side == LOCAL and 0 <= reached < rows:
                sigma = reached
            elif side == MATE and reached >= rows:
                sigma = 2 * rows - 1 - reached
            else:
                continue
            w_ref[block(place, sigma)] = totals[place][offset].astype(jnp.bfloat16)


def prepare(
    partner_hbm, states_hbm, onsite_hbm, hop_row_hbm, hop_up_hbm, coefs_hbm, coupling_hbm,
    x_ref, w_ref, coef_ref, rim_ref, weight_ref, far_ref, *rest,
):
    *totals, partner_ref, states_ref, small_ref, coefs_ref, blocks, sems, row_sems = rest
    rows, slots = partner_hbm.shape
    cols = onsite_hbm.shape[2]
    tile = lax.axis_index("tile")
    all_rows = rows * lax.axis_size("tile")
    here = lax.rem(tile, 2)
    offsets = 2 * REACH + 1

    def kept(place):
        return place + here * (rows - 1 - 2 * place)

    copies = [
        pltpu.make_async_copy(src, dst, sems.at[i])
        for i, (src, dst) in enumerate(
            (
                (partner_hbm, partner_ref),
                (hop_up_hbm, small_ref.at[0]),
                (onsite_hbm, small_ref.at[1]),
                (hop_row_hbm, small_ref.at[2]),
                (coefs_hbm, coefs_ref),
                (states_hbm, states_ref),
            )
        )
    ]

    def fetch(r):
        return pltpu.make_async_copy(coupling_hbm.at[r], blocks.at[r], row_sems.at[r])

    copies[0].start()
    for place in range(rows):
        fetch(kept(place)).start()
    for copy in copies[1:]:
        copy.start()

    for total in totals:
        total[...] = jnp.zeros_like(total)
    for copy in copies:
        copy.wait()
    for n in range(coefs_ref.shape[0]):
        weight_ref[n : n + 1, :] = jnp.full((1, cols), coefs_ref[n], jnp.float32)
    column = lax.broadcasted_iota(jnp.int32, (rows, cols), 1)
    parity = lax.broadcasted_iota(jnp.int32, (rows, cols), 0) + column + tile * rows
    odd = lax.rem(column[0:1], 2) == 1
    for layer in range(2):
        bond = jnp.where(lax.rem(parity, 2) == 0, small_ref[0, layer], 0.0)
        hop_row = small_ref[2, layer]
        left = pltpu.roll(hop_row, 1, axis=1)
        for place in range(rows):
            back = rows - 1 - place
            at = slice(place, place + 1)

            def ours(value):
                return jnp.where(here == 0, value[at], value[back : back + 1])

            coef_ref[layer, 0, at] = ours(small_ref[1, layer])
            coef_ref[layer, 1, at] = ours(hop_row)
            coef_ref[layer, 2, at] = ours(left)
            if place < rows - 1:
                coef_ref[layer, 3, at] = jnp.where(here == 0, bond[at], bond[back - 1 : back])
            if place > 0:
                coef_ref[layer, 4, at] = jnp.where(here == 0, bond[place - 1 : place], bond[back : back + 1])
        last = bond[rows - 1 :]
        raw = jnp.where(odd, 1.0, 0.0)
        rim_ref[FAR - 1, layer : layer + 1] = jnp.where(here == 0, raw, last)
        rim_ref[MATE - 1, layer : layer + 1] = jnp.where(here == 0, last, raw)
        for place in range(rows):
            x_ref[layer, :, place * cols : (place + 1) * cols] = states_ref[layer, kept(place)]

    for pair in range(0, rows, PAIR):
        places = range(pair, pair + PAIR)
        for place in places:
            fetch(kept(place)).wait()
        for k in range(slots):
            for place in places:
                row = kept(place)
                slot = partner_ref[row, k]
                away = slot - tile * rows - row
                away = jnp.where(away > all_rows // 2, away - all_rows, away)
                away = jnp.where(away < -(all_rows // 2), away + all_rows, away)
                at = jnp.where(slot >= 0, REACH + (1 - 2 * here) * away, offsets)
                totals[place][at] += blocks[row, k].astype(jnp.float32)
    settle(totals, FAR, w_ref, cols)
    write_far(x_ref, w_ref, rim_ref, far_ref)


def to_mate(x_ref, w_ref, rim_ref, rows_ref, terms_ref):
    write_payload(x_ref, w_ref, rim_ref, MATE, rows_ref, terms_ref)


def to_mate_first(x_ref, rim_ref, *refs):
    *totals, rows_ref, terms_ref, w_ref = refs
    settle(totals, MATE, w_ref, rim_ref.shape[2])
    write_payload(x_ref, w_ref, rim_ref, MATE, rows_ref, terms_ref)


def inner(order, *refs):
    if order == 0:
        x_ref, coef_ref, weight_ref, *totals, sum_ref, filt_out, w_ref = refs
        settle(totals, LOCAL, w_ref, weight_ref.shape[1])
        scale = 1.0 / 12.0
    else:
        x_ref, prev_ref, filt_ref, w_ref, coef_ref, weight_ref, sum_ref, filt_out = refs
        scale = 2.0 / 12.0
    wide = x_ref.shape[2]
    cols = weight_ref.shape[1]
    rows = wide // cols
    first = x_ref[0].astype(jnp.bfloat16)
    second = x_ref[1].astype(jnp.bfloat16)
    for outs, term in products(second, w_ref, LOCAL, 1, cols):
        sum_ref[0, :, outs] = scale * term
    for outs, term in products(first, w_ref, LOCAL, 0, cols):
        sum_ref[1, :, outs] = scale * term
    for layer in range(2):
        for r in range(rows):
            here = slice(r * cols, (r + 1) * cols)
            x = x_ref[layer, :, here]

            def factor(i):
                return coef_ref[layer, i, r : r + 1, :]

            hop = factor(0) * x
            hop += factor(1) * pltpu.roll(x, cols - 1, axis=1)
            hop += factor(2) * pltpu.roll(x, 1, axis=1)
            if r < rows - 1:
                hop += factor(3) * x_ref[layer, :, (r + 1) * cols : (r + 2) * cols]
            if r > 0:
                hop += factor(4) * x_ref[layer, :, (r - 1) * cols : r * cols]
            term = sum_ref[layer, :, here] + scale * hop
            filt = weight_ref[order : order + 1, :] * x
            if order > 0:
                term -= prev_ref[layer, :, here]
                filt += filt_ref[layer, :, here]
            filt_out[layer, :, here] = filt
            sum_ref[layer, :, here] = term


def from_mate(scale, part_ref, w_ref, rim_ref, rows_ref, terms_ref, *refs):
    if len(refs) > 1:
        far_ref, sum_ref, *turned = refs
    else:
        (sum_ref,), turned = refs, []
    add_received(scale, rows_ref, terms_ref, w_ref, 1, rim_ref, MATE, part_ref, sum_ref)
    if turned:
        step = PAIR * rim_ref.shape[2]
        groups = sum_ref.shape[2] // step
        for group in range(groups):
            outs = slice(group * step, (group + 1) * step)
            for other in range(groups - group):
                ins = slice(other * step, (other + 1) * step)
                turned[0][ins, outs] = far_ref[outs, ins].T


def outer(scale, sum_ref, w_ref, turned_ref, rim_ref, got_ref, x_ref, far_ref):
    add_far(scale, got_ref, turned_ref, rim_ref, sum_ref, x_ref)
    write_far(x_ref, w_ref, rim_ref, far_ref)


def finish(scale, degree, sum_ref, filt_ref, turned_ref, rim_ref, weight_ref, got_ref, out_ref, x_ref):
    cols = rim_ref.shape[2]
    rows = out_ref.shape[1]
    add_far(scale, got_ref, turned_ref, rim_ref, sum_ref, x_ref)
    flip = lax.rem(lax.axis_index("tile"), 2)
    for layer in range(2):
        for place in range(rows):
            here = slice(place * cols, (place + 1) * cols)
            out_ref[layer, place + flip * (rows - 1 - 2 * place)] = (
                filt_ref[layer, :, here] + weight_ref[degree : degree + 1, :] * x_ref[layer, :, here]
            )


def call(kernel, outs, args, scratch=(), specs=None, limit=12, flops=1 << 20):
    return pl.pallas_call(
        kernel,
        out_shape=outs,
        in_specs=specs or [IN_VMEM] * len(args),
        out_specs=[IN_VMEM] * len(outs),
        scratch_shapes=list(scratch),
        cost_estimate=pl.CostEstimate(flops=flops, bytes_accessed=0, transcendentals=0),
        compiler_params=pltpu.CompilerParams(vmem_limit_bytes=limit << 20),
    )(*args)


def body(states, onsite, hop_row, hop_up, partner, coupling, coefs):
    rows, count, cols = states.shape[1:]
    slots = partner.shape[1]
    wide = rows * cols
    degree = coefs.shape[0] - 1
    size = lax.axis_size("tile")
    far_pairs = [(i, (i + 1) % size if i % 2 else (i - 1) % size) for i in range(size)]
    mate_pairs = [(i, i ^ 1) for i in range(size)]

    field = held((2, count, wide), jnp.float32)
    payload = held((count, 2 * wide + 2 * cols), jnp.bfloat16)
    parts = [held((count, wide + 2 * cols), jnp.bfloat16), held((count, wide), jnp.bfloat16)]
    matrix = held((wide, wide), jnp.bfloat16)
    x, w_far, coef, rim, weight, far, *totals = call(
        prepare,
        [field, matrix, held((2, 5, rows, cols), jnp.float32),
         held((2, 2, cols), jnp.float32), held((degree + 1, cols), jnp.float32), payload,
         *[held((2 * REACH + 2, cols, cols), jnp.float32)] * rows],
        [outside(v) for v in (partner, states, onsite, hop_row, hop_up, coefs, coupling)],
        scratch=[
            pltpu.SMEM((rows, slots), jnp.int32),
            pltpu.VMEM((2, rows, count, cols), jnp.float32),
            pltpu.VMEM((3, 2, rows, cols), jnp.float32),
            pltpu.SMEM((degree + 1,), jnp.float32),
            pltpu.VMEM((rows, slots, cols, cols), jnp.bfloat16),
            pltpu.SemaphoreType.DMA((6,)),
            pltpu.SemaphoreType.DMA((rows,)),
        ],
        specs=[ANYWHERE] * 7,
        limit=24,
    )
    w_far, coef, rim, weight, x = near(w_far), near(coef), near(rim), near(weight), near(x)
    totals = [near(total) for total in totals]
    prev = filt = None
    for order in range(degree):
        scale = 1.0 / 12.0 if order == 0 else 2.0 / 12.0
        got_far = lax.ppermute(far, "tile", far_pairs)
        if order == 0:
            *mate, w_mate = call(to_mate_first, [*parts, matrix], [x, rim, *totals])
            w_mate = near(w_mate)
        else:
            mate = call(to_mate, parts, [x, w_mate, rim])
        got_mate = [near(lax.ppermute(part, "tile", mate_pairs)) for part in mate]
        if order == 0:
            part, filt, w_local = call(
                functools.partial(inner, order), [field, field, matrix], [x, coef, weight, *totals]
            )
            w_local = near(w_local)
        else:
            part, filt = call(
                functools.partial(inner, order),
                [field, field],
                [x, near(prev), near(filt), w_local, coef, weight],
            )
        part, *turned_now = call(
            functools.partial(from_mate, scale),
            [field, matrix] if order == 0 else [field],
            [near(part), w_mate, rim, *got_mate] + ([w_far] if order == 0 else []),
            flops=0,
        )
        if order == 0:
            turned = near(turned_now[0])
        prev = x
        if order < degree - 1:
            x, far = call(
                functools.partial(outer, scale),
                [field, payload],
                [near(part), w_far, turned, rim, near(got_far)],
            )
            x = near(x)
        else:
            (out,) = call(
                functools.partial(finish, scale, degree),
                [jax.ShapeDtypeStruct(states.shape, jnp.float32)],
                [near(part), near(filt), turned, rim, weight, near(got_far)],
                scratch=[pltpu.VMEM((2, count, wide), jnp.float32)],
            )
    return out


def solution(mesh):
    placed = (
        P(None, "tile", "state", None),
        P(None, "tile", None),
        P(None, "tile", None),
        P(None, "tile", None),
        P("tile", None),
        P("tile", None, None, None),
        P(),
    )
    return jax.shard_map(
        body, mesh=mesh, in_specs=placed, out_specs=P(None, "tile", "state", None), check_vma=False
    )
```

```python
import functools

import jax
import jax.numpy as jnp
from jax import lax
from jax.experimental import pallas as pl
from jax.experimental.pallas import tpu as pltpu
from jax.sharding import PartitionSpec as P

REACH = 8
LOCAL, MATE, FAR = 0, 1, 2
IN_VMEM = pl.BlockSpec(memory_space=pltpu.VMEM)
ANYWHERE = pl.BlockSpec(memory_space=pl.ANY)
PAIR = 2


def near(x):
    return pltpu.with_memory_space_constraint(x, pltpu.VMEM)


def outside(x):
    return pltpu.with_memory_space_constraint(x, pltpu.HBM)


def held(shape, dtype):
    return pltpu.VMEM(shape, dtype)


def core():
    return lax.rem(lax.axis_index("tile"), 2)


def dot(x, w, contract):
    return lax.dot_general(x, w, (((1,), (contract,)), ((), ())), preferred_element_type=jnp.float32)


def span(side, group, groups, step):
    if side == FAR:
        return slice(0, (groups - group) * step)
    if side == MATE:
        return slice((groups - 1 - group) * step, groups * step)
    return slice(0, groups * step)


def products(x, w_ref, side, contract, cols):
    step = PAIR * cols
    groups = w_ref.shape[1] // step
    for group in range(groups):
        outs = slice(group * step, (group + 1) * step)
        ins = span(side, group, groups, step)
        block = w_ref[ins, outs] if contract == 0 else w_ref[outs, ins]
        yield outs, dot(x[:, ins], block, contract)


def write_payload(x_ref, w_ref, rim_ref, side, rows_ref, terms_ref):
    wide = x_ref.shape[2]
    cols = rim_ref.shape[2]
    edge = slice(0, cols) if side == FAR else slice(wide - cols, wide)
    which = side - 1
    rows_ref[:, 0:wide] = x_ref[1].astype(jnp.bfloat16)
    rim = x_ref[0, :, edge] * rim_ref[which, 0:1, :]
    rim += pltpu.roll(x_ref[1, :, edge] * rim_ref[which, 1:2, :], cols - 1, axis=1)
    high = rim.astype(jnp.bfloat16)
    rows_ref[:, wide : wide + cols] = high
    rows_ref[:, wide + cols :] = (rim - high.astype(jnp.float32)).astype(jnp.bfloat16)
    first = x_ref[0].astype(jnp.bfloat16)
    for outs, term in products(first, w_ref, side, 0, cols):
        terms_ref[:, outs] = term.astype(jnp.bfloat16)


def write_far(x_ref, w_ref, rim_ref, far_ref):
    cut = far_ref.shape[1] - x_ref.shape[2]
    write_payload(x_ref, w_ref, rim_ref, FAR, far_ref.at[:, 0:cut], far_ref.at[:, cut:])


def add_received(scale, rows_ref, terms_ref, w_ref, contract, rim_ref, side, from_ref, to_ref):
    wide = to_ref.shape[2]
    cols = rim_ref.shape[2]
    edge = slice(0, cols) if side == FAR else slice(wide - cols, wide)
    which = side - 1
    to_ref[1] = from_ref[1] + scale * terms_ref[...].astype(jnp.float32)
    for outs, term in products(rows_ref[:, 0:wide], w_ref, side, contract, cols):
        to_ref[0, :, outs] = from_ref[0, :, outs] + scale * term
    rim = rows_ref[:, wide : wide + cols].astype(jnp.float32)
    rim += rows_ref[:, wide + cols :].astype(jnp.float32)
    to_ref[0, :, edge] += scale * (rim * rim_ref[which, 0:1, :])
    to_ref[1, :, edge] += scale * (pltpu.roll(rim, 1, axis=1) * rim_ref[which, 1:2, :])


def add_far(scale, got_ref, turned_ref, rim_ref, from_ref, to_ref):
    cut = got_ref.shape[1] - to_ref.shape[2]
    add_received(
        scale, got_ref.at[:, 0:cut], got_ref.at[:, cut:], turned_ref, 0, rim_ref, FAR, from_ref, to_ref
    )


def settle(totals, side, w_ref, cols):
    rows = len(totals)

    def block(place, sigma):
        return (slice(place * cols, (place + 1) * cols), slice(sigma * cols, (sigma + 1) * cols))

    if side == FAR:
        empty = [(place, rows - place) for place in range(1, rows, PAIR)]
    elif side == MATE:
        empty = [(place, rows - PAIR - place) for place in range(0, rows, PAIR)]
    else:
        empty = []
    for place, sigma in empty:
        w_ref[block(place, sigma)] = jnp.zeros((cols, cols), jnp.bfloat16)
    for place in range(rows):
        for offset in range(2 * REACH + 1):
            reached = place + offset - REACH
            if side == FAR and reached < 0:
                sigma = -1 - reached
            elif side == LOCAL and 0 <= reached < rows:
                sigma = reached
            elif side == MATE and reached >= rows:
                sigma = 2 * rows - 1 - reached
            else:
                continue
            w_ref[block(place, sigma)] = totals[place][offset].astype(jnp.bfloat16)


def prepare(
    partner_hbm, states_hbm, onsite_hbm, hop_row_hbm, hop_up_hbm, coefs_hbm, coupling_hbm,
    x_ref, w_ref, coef_ref, rim_ref, weight_ref, far_ref, *rest,
):
    *totals, partner_ref, states_ref, small_ref, coefs_ref, blocks, sems, row_sems = rest
    rows, slots = partner_hbm.shape
    cols = onsite_hbm.shape[2]
    tile = lax.axis_index("tile")
    all_rows = rows * lax.axis_size("tile")
    here = lax.rem(tile, 2)
    offsets = 2 * REACH + 1

    def kept(place):
        return place + here * (rows - 1 - 2 * place)

    copies = [
        pltpu.make_async_copy(src, dst, sems.at[i])
        for i, (src, dst) in enumerate(
            (
                (partner_hbm, partner_ref),
                (hop_up_hbm, small_ref.at[0]),
                (onsite_hbm, small_ref.at[1]),
                (hop_row_hbm, small_ref.at[2]),
                (coefs_hbm, coefs_ref),
                (states_hbm, states_ref),
            )
        )
    ]

    def fetch(r):
        return pltpu.make_async_copy(coupling_hbm.at[r], blocks.at[r], row_sems.at[r])

    copies[0].start()
    for place in range(rows):
        fetch(kept(place)).start()
    for copy in copies[1:]:
        copy.start()

    for total in totals:
        total[...] = jnp.zeros_like(total)
    for copy in copies:
        copy.wait()
    for n in range(coefs_ref.shape[0]):
        weight_ref[n : n + 1, :] = jnp.full((1, cols), coefs_ref[n], jnp.float32)
    column = lax.broadcasted_iota(jnp.int32, (rows, cols), 1)
    parity = lax.broadcasted_iota(jnp.int32, (rows, cols), 0) + column + tile * rows
    odd = lax.rem(column[0:1], 2) == 1
    for layer in range(2):
        bond = jnp.where(lax.rem(parity, 2) == 0, small_ref[0, layer], 0.0)
        hop_row = small_ref[2, layer]
        left = pltpu.roll(hop_row, 1, axis=1)
        for place in range(rows):
            back = rows - 1 - place
            at = slice(place, place + 1)

            def ours(value):
                return jnp.where(here == 0, value[at], value[back : back + 1])

            coef_ref[layer, 0, at] = ours(small_ref[1, layer])
            coef_ref[layer, 1, at] = ours(hop_row)
            coef_ref[layer, 2, at] = ours(left)
            if place < rows - 1:
                coef_ref[layer, 3, at] = jnp.where(here == 0, bond[at], bond[back - 1 : back])
            if place > 0:
                coef_ref[layer, 4, at] = jnp.where(here == 0, bond[place - 1 : place], bond[back : back + 1])
        last = bond[rows - 1 :]
        raw = jnp.where(odd, 1.0, 0.0)
        rim_ref[FAR - 1, layer : layer + 1] = jnp.where(here == 0, raw, last)
        rim_ref[MATE - 1, layer : layer + 1] = jnp.where(here == 0, last, raw)
        for place in range(rows):
            x_ref[layer, :, place * cols : (place + 1) * cols] = states_ref[layer, kept(place)]

    for pair in range(0, rows, PAIR):
        places = range(pair, pair + PAIR)
        for place in places:
            fetch(kept(place)).wait()
        for k in range(slots):
            for place in places:
                row = kept(place)
                slot = partner_ref[row, k]
                away = slot - tile * rows - row
                away = jnp.where(away > all_rows // 2, away - all_rows, away)
                away = jnp.where(away < -(all_rows // 2), away + all_rows, away)
                at = jnp.where(slot >= 0, REACH + (1 - 2 * here) * away, offsets)
                totals[place][at] += blocks[row, k].astype(jnp.float32)
    settle(totals, FAR, w_ref, cols)
    write_far(x_ref, w_ref, rim_ref, far_ref)


def to_mate(x_ref, w_ref, rim_ref, rows_ref, terms_ref):
    write_payload(x_ref, w_ref, rim_ref, MATE, rows_ref, terms_ref)


def to_mate_first(x_ref, rim_ref, *refs):
    *totals, rows_ref, terms_ref, w_ref = refs
    settle(totals, MATE, w_ref, rim_ref.shape[2])
    write_payload(x_ref, w_ref, rim_ref, MATE, rows_ref, terms_ref)


def inner(order, *refs):
    if order == 0:
        x_ref, coef_ref, weight_ref, *totals, sum_ref, filt_out, w_ref = refs
        settle(totals, LOCAL, w_ref, weight_ref.shape[1])
        scale = 1.0 / 12.0
    else:
        x_ref, prev_ref, filt_ref, w_ref, coef_ref, weight_ref, sum_ref, filt_out = refs
        scale = 2.0 / 12.0
    wide = x_ref.shape[2]
    cols = weight_ref.shape[1]
    rows = wide // cols
    first = x_ref[0].astype(jnp.bfloat16)
    second = x_ref[1].astype(jnp.bfloat16)
    for outs, term in products(second, w_ref, LOCAL, 1, cols):
        sum_ref[0, :, outs] = scale * term
    for outs, term in products(first, w_ref, LOCAL, 0, cols):
        sum_ref[1, :, outs] = scale * term
    for layer in range(2):
        for r in range(rows):
            here = slice(r * cols, (r + 1) * cols)
            x = x_ref[layer, :, here]

            def factor(i):
                return coef_ref[layer, i, r : r + 1, :]

            hop = factor(0) * x
            hop += factor(1) * pltpu.roll(x, cols - 1, axis=1)
            hop += factor(2) * pltpu.roll(x, 1, axis=1)
            if r < rows - 1:
                hop += factor(3) * x_ref[layer, :, (r + 1) * cols : (r + 2) * cols]
            if r > 0:
                hop += factor(4) * x_ref[layer, :, (r - 1) * cols : r * cols]
            term = sum_ref[layer, :, here] + scale * hop
            filt = weight_ref[order : order + 1, :] * x
            if order > 0:
                term -= prev_ref[layer, :, here]
                filt += filt_ref[layer, :, here]
            filt_out[layer, :, here] = filt
            sum_ref[layer, :, here] = term


def from_mate(scale, part_ref, w_ref, rim_ref, rows_ref, terms_ref, *refs):
    if len(refs) > 1:
        far_ref, sum_ref, *turned = refs
    else:
        (sum_ref,), turned = refs, []
    add_received(scale, rows_ref, terms_ref, w_ref, 1, rim_ref, MATE, part_ref, sum_ref)
    if turned:
        step = PAIR * rim_ref.shape[2]
        groups = sum_ref.shape[2] // step
        for group in range(groups):
            outs = slice(group * step, (group + 1) * step)
            for other in range(groups - group):
                ins = slice(other * step, (other + 1) * step)
                turned[0][ins, outs] = far_ref[outs, ins].T


def outer(scale, mine, sum_ref, w_ref, turned_ref, rim_ref, got_ref, *refs):
    x_ref, far_ref = refs[-2:]

    @pl.when(core() == mine)
    def _():
        add_far(scale, got_ref, turned_ref, rim_ref, sum_ref, x_ref)
        write_far(x_ref, w_ref, rim_ref, far_ref)


def finish(scale, degree, sum_ref, filt_ref, turned_ref, rim_ref, weight_ref, up_ref, down_ref, out_ref, x_ref):
    cols = rim_ref.shape[2]
    rows = out_ref.shape[1]
    flip = core()
    for mine, got_ref in enumerate((up_ref, down_ref)):

        @pl.when(flip == mine)
        def _():
            add_far(scale, got_ref, turned_ref, rim_ref, sum_ref, x_ref)

    for layer in range(2):
        for place in range(rows):
            here = slice(place * cols, (place + 1) * cols)
            out_ref[layer, place + flip * (rows - 1 - 2 * place)] = (
                filt_ref[layer, :, here] + weight_ref[degree : degree + 1, :] * x_ref[layer, :, here]
            )


def call(kernel, outs, args, scratch=(), specs=None, limit=12, flops=1 << 20, aliases=None):
    return pl.pallas_call(
        kernel,
        out_shape=outs,
        in_specs=specs or [IN_VMEM] * len(args),
        out_specs=[IN_VMEM] * len(outs),
        scratch_shapes=list(scratch),
        input_output_aliases=aliases or {},
        cost_estimate=pl.CostEstimate(flops=flops, bytes_accessed=0, transcendentals=0),
        compiler_params=pltpu.CompilerParams(vmem_limit_bytes=limit << 20),
    )(*args)


def body(states, onsite, hop_row, hop_up, partner, coupling, coefs):
    rows, count, cols = states.shape[1:]
    slots = partner.shape[1]
    wide = rows * cols
    degree = coefs.shape[0] - 1
    size = lax.axis_size("tile")
    up_pairs = [(i, (i + 1) % size) for i in range(size)]
    down_pairs = [((i + 1) % size, i) for i in range(size)]
    mate_pairs = [(i, i ^ 1) for i in range(size)]

    field = held((2, count, wide), jnp.float32)
    payload = held((count, 2 * wide + 2 * cols), jnp.bfloat16)
    parts = [held((count, wide + 2 * cols), jnp.bfloat16), held((count, wide), jnp.bfloat16)]
    matrix = held((wide, wide), jnp.bfloat16)
    x, w_far, coef, rim, weight, far, *totals = call(
        prepare,
        [field, matrix, held((2, 5, rows, cols), jnp.float32),
         held((2, 2, cols), jnp.float32), held((degree + 1, cols), jnp.float32), payload,
         *[held((2 * REACH + 2, cols, cols), jnp.float32)] * rows],
        [outside(v) for v in (partner, states, onsite, hop_row, hop_up, coefs, coupling)],
        scratch=[
            pltpu.SMEM((rows, slots), jnp.int32),
            pltpu.VMEM((2, rows, count, cols), jnp.float32),
            pltpu.VMEM((3, 2, rows, cols), jnp.float32),
            pltpu.SMEM((degree + 1,), jnp.float32),
            pltpu.VMEM((rows, slots, cols, cols), jnp.bfloat16),
            pltpu.SemaphoreType.DMA((6,)),
            pltpu.SemaphoreType.DMA((rows,)),
        ],
        specs=[ANYWHERE] * 7,
        limit=24,
    )
    w_far, coef, rim, weight, x = near(w_far), near(coef), near(rim), near(weight), near(x)
    totals = [near(total) for total in totals]
    prev = filt = None
    far = {0: far, 1: far}
    for order in range(degree):
        scale = 1.0 / 12.0 if order == 0 else 2.0 / 12.0
        got = {1: lax.ppermute(far[0], "tile", down_pairs), 0: lax.ppermute(far[1], "tile", up_pairs)}
        if order == 0:
            *mate, w_mate = call(to_mate_first, [*parts, matrix], [x, rim, *totals])
            w_mate = near(w_mate)
        else:
            mate = call(to_mate, parts, [x, w_mate, rim])
        got_mate = [near(lax.ppermute(part, "tile", mate_pairs)) for part in mate]
        if order == 0:
            part, filt, w_local = call(
                functools.partial(inner, order), [field, field, matrix], [x, coef, weight, *totals]
            )
            w_local = near(w_local)
        else:
            part, filt = call(
                functools.partial(inner, order),
                [field, field],
                [x, near(prev), near(filt), w_local, coef, weight],
            )
        part, *turned_now = call(
            functools.partial(from_mate, scale),
            [field, matrix] if order == 0 else [field],
            [near(part), w_mate, rim, *got_mate] + ([w_far] if order == 0 else []),
            flops=0,
        )
        if order == 0:
            turned = near(turned_now[0])
        prev = x
        if order < degree - 1:
            now, later = (1, 0) if order % 2 == 0 else (0, 1)
            x, far[now] = call(
                functools.partial(outer, scale, now),
                [field, payload],
                [near(part), w_far, turned, rim, near(got[now])],
            )
            x, far[later] = call(
                functools.partial(outer, scale, later),
                [field, payload],
                [near(part), w_far, turned, rim, near(got[later]), near(x)],
                aliases={5: 0},
            )
            x = near(x)
        else:
            (out,) = call(
                functools.partial(finish, scale, degree),
                [jax.ShapeDtypeStruct(states.shape, jnp.float32)],
                [near(part), near(filt), turned, rim, weight, near(got[0]), near(got[1])],
                scratch=[pltpu.VMEM((2, count, wide), jnp.float32)],
            )
    return out


def solution(mesh):
    placed = (
        P(None, "tile", "state", None),
        P(None, "tile", None),
        P(None, "tile", None),
        P(None, "tile", None),
        P("tile", None),
        P("tile", None, None, None),
        P(),
    )
    return jax.shard_map(
        body, mesh=mesh, in_specs=placed, out_specs=P(None, "tile", "state", None), check_vma=False
    )
```

```python
import functools

import jax
import jax.numpy as jnp
from jax import lax
from jax.experimental import pallas as pl
from jax.experimental.pallas import tpu as pltpu
from jax.sharding import PartitionSpec as P

REACH = 8
LOCAL, MATE, FAR = 0, 1, 2
IN_VMEM = pl.BlockSpec(memory_space=pltpu.VMEM)
ANYWHERE = pl.BlockSpec(memory_space=pl.ANY)
PAIR = 2


def near(x):
    return pltpu.with_memory_space_constraint(x, pltpu.VMEM)


def outside(x):
    return pltpu.with_memory_space_constraint(x, pltpu.HBM)


def held(shape, dtype):
    return pltpu.VMEM(shape, dtype)


def core():
    return lax.rem(lax.axis_index("tile"), 2)


def dot(x, w, contract):
    return lax.dot_general(x, w, (((1,), (contract,)), ((), ())), preferred_element_type=jnp.float32)


def span(side, group, groups, step):
    if side == FAR:
        return slice(0, (groups - group) * step)
    if side == MATE:
        return slice((groups - 1 - group) * step, groups * step)
    return slice(0, groups * step)


def products(x, w_ref, side, contract, cols):
    step = PAIR * cols
    groups = w_ref.shape[1] // step
    for group in range(groups):
        outs = slice(group * step, (group + 1) * step)
        ins = span(side, group, groups, step)
        block = w_ref[ins, outs] if contract == 0 else w_ref[outs, ins]
        yield outs, dot(x[:, ins], block, contract)


def write_payload(x_ref, w_ref, rim_ref, side, rows_ref, terms_ref):
    wide = x_ref.shape[2]
    cols = rim_ref.shape[2]
    edge = slice(0, cols) if side == FAR else slice(wide - cols, wide)
    which = side - 1
    rows_ref[:, 0:wide] = x_ref[1].astype(jnp.bfloat16)
    rim = x_ref[0, :, edge] * rim_ref[which, 0:1, :]
    rim += pltpu.roll(x_ref[1, :, edge] * rim_ref[which, 1:2, :], cols - 1, axis=1)
    high = rim.astype(jnp.bfloat16)
    rows_ref[:, wide : wide + cols] = high
    rows_ref[:, wide + cols :] = (rim - high.astype(jnp.float32)).astype(jnp.bfloat16)
    first = x_ref[0].astype(jnp.bfloat16)
    for outs, term in products(first, w_ref, side, 0, cols):
        terms_ref[:, outs] = term.astype(jnp.bfloat16)


def write_far(x_ref, w_ref, rim_ref, far_ref):
    cut = far_ref.shape[1] - x_ref.shape[2]
    write_payload(x_ref, w_ref, rim_ref, FAR, far_ref.at[:, 0:cut], far_ref.at[:, cut:])


def add_received(scale, rows_ref, terms_ref, w_ref, contract, rim_ref, side, from_ref, to_ref):
    wide = to_ref.shape[2]
    cols = rim_ref.shape[2]
    edge = slice(0, cols) if side == FAR else slice(wide - cols, wide)
    which = side - 1
    to_ref[1] = from_ref[1] + scale * terms_ref[...].astype(jnp.float32)
    for outs, term in products(rows_ref[:, 0:wide], w_ref, side, contract, cols):
        to_ref[0, :, outs] = from_ref[0, :, outs] + scale * term
    rim = rows_ref[:, wide : wide + cols].astype(jnp.float32)
    rim += rows_ref[:, wide + cols :].astype(jnp.float32)
    to_ref[0, :, edge] += scale * (rim * rim_ref[which, 0:1, :])
    to_ref[1, :, edge] += scale * (pltpu.roll(rim, 1, axis=1) * rim_ref[which, 1:2, :])


def add_far(scale, got_ref, turned_ref, rim_ref, from_ref, to_ref):
    cut = got_ref.shape[1] - to_ref.shape[2]
    add_received(
        scale, got_ref.at[:, 0:cut], got_ref.at[:, cut:], turned_ref, 0, rim_ref, FAR, from_ref, to_ref
    )


def settle(totals, side, w_ref, cols):
    rows = len(totals)

    def block(place, sigma):
        return (slice(place * cols, (place + 1) * cols), slice(sigma * cols, (sigma + 1) * cols))

    if side == FAR:
        empty = [(place, rows - place) for place in range(1, rows, PAIR)]
    elif side == MATE:
        empty = [(place, rows - PAIR - place) for place in range(0, rows, PAIR)]
    else:
        empty = []
    for place, sigma in empty:
        w_ref[block(place, sigma)] = jnp.zeros((cols, cols), jnp.bfloat16)
    for place in range(rows):
        for offset in range(2 * REACH + 1):
            reached = place + offset - REACH
            if side == FAR and reached < 0:
                sigma = -1 - reached
            elif side == LOCAL and 0 <= reached < rows:
                sigma = reached
            elif side == MATE and reached >= rows:
                sigma = 2 * rows - 1 - reached
            else:
                continue
            w_ref[block(place, sigma)] = totals[place][offset].astype(jnp.bfloat16)


def prepare(
    partner_hbm, states_hbm, onsite_hbm, hop_row_hbm, hop_up_hbm, coefs_hbm, coupling_hbm,
    x_ref, w_ref, coef_ref, rim_ref, weight_ref, far_ref, *rest,
):
    *totals, partner_ref, states_ref, small_ref, coefs_ref, blocks, sems, row_sems = rest
    rows, slots = partner_hbm.shape
    cols = onsite_hbm.shape[2]
    tile = lax.axis_index("tile")
    all_rows = rows * lax.axis_size("tile")
    here = lax.rem(tile, 2)
    offsets = 2 * REACH + 1

    def kept(place):
        return place + here * (rows - 1 - 2 * place)

    copies = [
        pltpu.make_async_copy(src, dst, sems.at[i])
        for i, (src, dst) in enumerate(
            (
                (partner_hbm, partner_ref),
                (hop_up_hbm, small_ref.at[0]),
                (onsite_hbm, small_ref.at[1]),
                (hop_row_hbm, small_ref.at[2]),
                (coefs_hbm, coefs_ref),
                (states_hbm, states_ref),
            )
        )
    ]

    def fetch(r):
        return pltpu.make_async_copy(coupling_hbm.at[r], blocks.at[r], row_sems.at[r])

    copies[0].start()
    for place in range(rows):
        fetch(kept(place)).start()
    for copy in copies[1:]:
        copy.start()

    for total in totals:
        total[...] = jnp.zeros_like(total)
    for copy in copies:
        copy.wait()
    for n in range(coefs_ref.shape[0]):
        weight_ref[n : n + 1, :] = jnp.full((1, cols), coefs_ref[n], jnp.float32)
    column = lax.broadcasted_iota(jnp.int32, (rows, cols), 1)
    parity = lax.broadcasted_iota(jnp.int32, (rows, cols), 0) + column + tile * rows
    odd = lax.rem(column[0:1], 2) == 1
    for layer in range(2):
        bond = jnp.where(lax.rem(parity, 2) == 0, small_ref[0, layer], 0.0)
        hop_row = small_ref[2, layer]
        left = pltpu.roll(hop_row, 1, axis=1)
        for place in range(rows):
            back = rows - 1 - place
            at = slice(place, place + 1)

            def ours(value):
                return jnp.where(here == 0, value[at], value[back : back + 1])

            coef_ref[layer, 0, at] = ours(small_ref[1, layer])
            coef_ref[layer, 1, at] = ours(hop_row)
            coef_ref[layer, 2, at] = ours(left)
            if place < rows - 1:
                coef_ref[layer, 3, at] = jnp.where(here == 0, bond[at], bond[back - 1 : back])
            if place > 0:
                coef_ref[layer, 4, at] = jnp.where(here == 0, bond[place - 1 : place], bond[back : back + 1])
        last = bond[rows - 1 :]
        raw = jnp.where(odd, 1.0, 0.0)
        rim_ref[FAR - 1, layer : layer + 1] = jnp.where(here == 0, raw, last)
        rim_ref[MATE - 1, layer : layer + 1] = jnp.where(here == 0, last, raw)
        for place in range(rows):
            x_ref[layer, :, place * cols : (place + 1) * cols] = states_ref[layer, kept(place)]

    for pair in range(0, rows, PAIR):
        places = range(pair, pair + PAIR)
        for place in places:
            fetch(kept(place)).wait()
        for k in range(slots):
            for place in places:
                row = kept(place)
                slot = partner_ref[row, k]
                away = slot - tile * rows - row
                away = jnp.where(away > all_rows // 2, away - all_rows, away)
                away = jnp.where(away < -(all_rows // 2), away + all_rows, away)
                at = jnp.where(slot >= 0, REACH + (1 - 2 * here) * away, offsets)
                totals[place][at] += blocks[row, k].astype(jnp.float32)
    settle(totals, FAR, w_ref, cols)
    write_far(x_ref, w_ref, rim_ref, far_ref)


def to_mate(x_ref, w_ref, rim_ref, rows_ref, terms_ref):
    write_payload(x_ref, w_ref, rim_ref, MATE, rows_ref, terms_ref)


def to_mate_first(x_ref, rim_ref, *refs):
    *totals, rows_ref, terms_ref, w_ref = refs
    settle(totals, MATE, w_ref, rim_ref.shape[2])
    write_payload(x_ref, w_ref, rim_ref, MATE, rows_ref, terms_ref)


def inner(order, *refs):
    if order == 0:
        x_ref, coef_ref, weight_ref, *totals, sum_ref, filt_out, w_ref = refs
        settle(totals, LOCAL, w_ref, weight_ref.shape[1])
        scale = 1.0 / 12.0
    else:
        x_ref, prev_ref, filt_ref, w_ref, coef_ref, weight_ref, sum_ref, filt_out = refs
        scale = 2.0 / 12.0
    wide = x_ref.shape[2]
    cols = weight_ref.shape[1]
    rows = wide // cols
    first = x_ref[0].astype(jnp.bfloat16)
    second = x_ref[1].astype(jnp.bfloat16)
    for outs, term in products(second, w_ref, LOCAL, 1, cols):
        sum_ref[0, :, outs] = scale * term
    for outs, term in products(first, w_ref, LOCAL, 0, cols):
        sum_ref[1, :, outs] = scale * term
    for layer in range(2):
        for r in range(rows):
            here = slice(r * cols, (r + 1) * cols)
            x = x_ref[layer, :, here]

            def factor(i):
                return coef_ref[layer, i, r : r + 1, :]

            hop = factor(0) * x
            hop += factor(1) * pltpu.roll(x, cols - 1, axis=1)
            hop += factor(2) * pltpu.roll(x, 1, axis=1)
            if r < rows - 1:
                hop += factor(3) * x_ref[layer, :, (r + 1) * cols : (r + 2) * cols]
            if r > 0:
                hop += factor(4) * x_ref[layer, :, (r - 1) * cols : r * cols]
            term = sum_ref[layer, :, here] + scale * hop
            filt = weight_ref[order : order + 1, :] * x
            if order > 0:
                term -= prev_ref[layer, :, here]
                filt += filt_ref[layer, :, here]
            filt_out[layer, :, here] = filt
            sum_ref[layer, :, here] = term


def from_mate(scale, part_ref, w_ref, rim_ref, rows_ref, terms_ref, *refs):
    if len(refs) > 1:
        far_ref, sum_ref, *turned = refs
    else:
        (sum_ref,), turned = refs, []
    add_received(scale, rows_ref, terms_ref, w_ref, 1, rim_ref, MATE, part_ref, sum_ref)
    if turned:
        step = PAIR * rim_ref.shape[2]
        groups = sum_ref.shape[2] // step
        for group in range(groups):
            outs = slice(group * step, (group + 1) * step)
            for other in range(groups - group):
                ins = slice(other * step, (other + 1) * step)
                turned[0][ins, outs] = far_ref[outs, ins].T


def outer(scale, mine, sum_ref, w_ref, turned_ref, rim_ref, got_ref, *refs):
    x_ref, far_ref = refs[-2:]

    @pl.when(core() == mine)
    def _():
        add_far(scale, got_ref, turned_ref, rim_ref, sum_ref, x_ref)
        write_far(x_ref, w_ref, rim_ref, far_ref)


def finish(scale, degree, sum_ref, filt_ref, turned_ref, rim_ref, weight_ref, up_ref, down_ref, out_ref, x_ref):
    cols = rim_ref.shape[2]
    rows = out_ref.shape[1]
    flip = core()
    for mine, got_ref in enumerate((up_ref, down_ref)):

        @pl.when(flip == mine)
        def _():
            add_far(scale, got_ref, turned_ref, rim_ref, sum_ref, x_ref)

    for layer in range(2):
        for place in range(rows):
            here = slice(place * cols, (place + 1) * cols)
            out_ref[layer, place + flip * (rows - 1 - 2 * place)] = (
                filt_ref[layer, :, here] + weight_ref[degree : degree + 1, :] * x_ref[layer, :, here]
            )


def call(kernel, outs, args, scratch=(), specs=None, limit=12, flops=1 << 20, aliases=None):
    return pl.pallas_call(
        kernel,
        out_shape=outs,
        in_specs=specs or [IN_VMEM] * len(args),
        out_specs=[IN_VMEM] * len(outs),
        scratch_shapes=list(scratch),
        input_output_aliases=aliases or {},
        cost_estimate=pl.CostEstimate(flops=flops, bytes_accessed=0, transcendentals=0),
        compiler_params=pltpu.CompilerParams(vmem_limit_bytes=limit << 20),
    )(*args)


def body(states, onsite, hop_row, hop_up, partner, coupling, coefs):
    rows, count, cols = states.shape[1:]
    slots = partner.shape[1]
    wide = rows * cols
    degree = coefs.shape[0] - 1
    size = lax.axis_size("tile")
    up_pairs = [(i, (i + 1) % size) for i in range(size)]
    down_pairs = [((i + 1) % size, i) for i in range(size)]
    far_pairs = [up_pairs[i] if i % 2 else down_pairs[i - 1] for i in range(size)]
    mate_pairs = [(i, i ^ 1) for i in range(size)]

    field = held((2, count, wide), jnp.float32)
    payload = held((count, 2 * wide + 2 * cols), jnp.bfloat16)
    parts = [held((count, wide + 2 * cols), jnp.bfloat16), held((count, wide), jnp.bfloat16)]
    matrix = held((wide, wide), jnp.bfloat16)
    x, w_far, coef, rim, weight, far, *totals = call(
        prepare,
        [field, matrix, held((2, 5, rows, cols), jnp.float32),
         held((2, 2, cols), jnp.float32), held((degree + 1, cols), jnp.float32), payload,
         *[held((2 * REACH + 2, cols, cols), jnp.float32)] * rows],
        [outside(v) for v in (partner, states, onsite, hop_row, hop_up, coefs, coupling)],
        scratch=[
            pltpu.SMEM((rows, slots), jnp.int32),
            pltpu.VMEM((2, rows, count, cols), jnp.float32),
            pltpu.VMEM((3, 2, rows, cols), jnp.float32),
            pltpu.SMEM((degree + 1,), jnp.float32),
            pltpu.VMEM((rows, slots, cols, cols), jnp.bfloat16),
            pltpu.SemaphoreType.DMA((6,)),
            pltpu.SemaphoreType.DMA((rows,)),
        ],
        specs=[ANYWHERE] * 7,
        limit=24,
    )
    w_far, coef, rim, weight, x = near(w_far), near(coef), near(rim), near(weight), near(x)
    totals = [near(total) for total in totals]
    prev = filt = None
    for order in range(degree):
        scale = 1.0 / 12.0 if order == 0 else 2.0 / 12.0
        if order == 0:
            got = [lax.ppermute(far, "tile", far_pairs)] * 2
        else:
            got = [lax.ppermute(far[1], "tile", up_pairs), lax.ppermute(far[0], "tile", down_pairs)]
        if order == 0:
            *mate, w_mate = call(to_mate_first, [*parts, matrix], [x, rim, *totals])
            w_mate = near(w_mate)
        else:
            mate = call(to_mate, parts, [x, w_mate, rim])
        got_mate = [near(lax.ppermute(part, "tile", mate_pairs)) for part in mate]
        if order == 0:
            part, filt, w_local = call(
                functools.partial(inner, order), [field, field, matrix], [x, coef, weight, *totals]
            )
            w_local = near(w_local)
        else:
            part, filt = call(
                functools.partial(inner, order),
                [field, field],
                [x, near(prev), near(filt), w_local, coef, weight],
            )
        part, *turned_now = call(
            functools.partial(from_mate, scale),
            [field, matrix] if order == 0 else [field],
            [near(part), w_mate, rim, *got_mate] + ([w_far] if order == 0 else []),
            flops=0,
        )
        if order == 0:
            turned = near(turned_now[0])
        prev = x
        if order < degree - 1:
            now, later = (1, 0) if order % 2 == 0 else (0, 1)
            far = [None, None]
            x, far[now] = call(
                functools.partial(outer, scale, now),
                [field, payload],
                [near(part), w_far, turned, rim, near(got[now])],
            )
            x, far[later] = call(
                functools.partial(outer, scale, later),
                [field, payload],
                [near(part), w_far, turned, rim, near(got[later]), near(x)],
                aliases={5: 0},
            )
            x = near(x)
        else:
            (out,) = call(
                functools.partial(finish, scale, degree),
                [jax.ShapeDtypeStruct(states.shape, jnp.float32)],
                [near(part), near(filt), turned, rim, weight, near(got[0]), near(got[1])],
                scratch=[pltpu.VMEM((2, count, wide), jnp.float32)],
            )
    return out


def solution(mesh):
    placed = (
        P(None, "tile", "state", None),
        P(None, "tile", None),
        P(None, "tile", None),
        P(None, "tile", None),
        P("tile", None),
        P("tile", None, None, None),
        P(),
    )
    return jax.shard_map(
        body, mesh=mesh, in_specs=placed, out_specs=P(None, "tile", "state", None), check_vma=False
    )
```

```python
import functools

import jax
import jax.numpy as jnp
from jax import lax
from jax.experimental import pallas as pl
from jax.experimental.pallas import tpu as pltpu
from jax.sharding import PartitionSpec as P

REACH = 8
LOCAL, MATE, FAR = 0, 1, 2
IN_VMEM = pl.BlockSpec(memory_space=pltpu.VMEM)
ANYWHERE = pl.BlockSpec(memory_space=pl.ANY)
PAIR = 2


def near(x):
    return pltpu.with_memory_space_constraint(x, pltpu.VMEM)


def outside(x):
    return pltpu.with_memory_space_constraint(x, pltpu.HBM)


def held(shape, dtype):
    return pltpu.VMEM(shape, dtype)


def core():
    return lax.rem(lax.axis_index("tile"), 2)


def dot(x, w, contract):
    return lax.dot_general(x, w, (((1,), (contract,)), ((), ())), preferred_element_type=jnp.float32)


def span(side, group, groups, step):
    if side == FAR:
        return slice(0, (groups - group) * step)
    if side == MATE:
        return slice((groups - 1 - group) * step, groups * step)
    return slice(0, groups * step)


def products(x, w_ref, side, contract, cols):
    step = PAIR * cols
    groups = w_ref.shape[1] // step
    for group in range(groups):
        outs = slice(group * step, (group + 1) * step)
        ins = span(side, group, groups, step)
        block = w_ref[ins, outs] if contract == 0 else w_ref[outs, ins]
        yield outs, dot(x[:, ins], block, contract)


def write_payload(x_ref, w_ref, rim_ref, side, rows_ref, terms_ref):
    wide = x_ref.shape[2]
    cols = rim_ref.shape[2]
    edge = slice(0, cols) if side == FAR else slice(wide - cols, wide)
    which = side - 1
    rows_ref[:, 0:wide] = x_ref[1].astype(jnp.bfloat16)
    rim = x_ref[0, :, edge] * rim_ref[which, 0:1, :]
    rim += pltpu.roll(x_ref[1, :, edge] * rim_ref[which, 1:2, :], cols - 1, axis=1)
    high = rim.astype(jnp.bfloat16)
    rows_ref[:, wide : wide + cols] = high
    rows_ref[:, wide + cols :] = (rim - high.astype(jnp.float32)).astype(jnp.bfloat16)
    first = x_ref[0].astype(jnp.bfloat16)
    for outs, term in products(first, w_ref, side, 0, cols):
        terms_ref[:, outs] = term.astype(jnp.bfloat16)


def write_far(x_ref, w_ref, rim_ref, far_ref):
    cut = far_ref.shape[1] - x_ref.shape[2]
    write_payload(x_ref, w_ref, rim_ref, FAR, far_ref.at[:, 0:cut], far_ref.at[:, cut:])


def add_received(scale, rows_ref, terms_ref, w_ref, contract, rim_ref, side, from_ref, to_ref):
    wide = to_ref.shape[2]
    cols = rim_ref.shape[2]
    edge = slice(0, cols) if side == FAR else slice(wide - cols, wide)
    which = side - 1
    to_ref[1] = from_ref[1] + scale * terms_ref[...].astype(jnp.float32)
    for outs, term in products(rows_ref[:, 0:wide], w_ref, side, contract, cols):
        to_ref[0, :, outs] = from_ref[0, :, outs] + scale * term
    rim = rows_ref[:, wide : wide + cols].astype(jnp.float32)
    rim += rows_ref[:, wide + cols :].astype(jnp.float32)
    to_ref[0, :, edge] += scale * (rim * rim_ref[which, 0:1, :])
    to_ref[1, :, edge] += scale * (pltpu.roll(rim, 1, axis=1) * rim_ref[which, 1:2, :])


def add_far(scale, got_ref, turned_ref, rim_ref, from_ref, to_ref):
    cut = got_ref.shape[1] - to_ref.shape[2]
    add_received(
        scale, got_ref.at[:, 0:cut], got_ref.at[:, cut:], turned_ref, 0, rim_ref, FAR, from_ref, to_ref
    )


def settle(totals, side, w_ref, cols):
    rows = len(totals)

    def block(place, sigma):
        return (slice(place * cols, (place + 1) * cols), slice(sigma * cols, (sigma + 1) * cols))

    if side == FAR:
        empty = [(place, rows - place) for place in range(1, rows, PAIR)]
    elif side == MATE:
        empty = [(place, rows - PAIR - place) for place in range(0, rows, PAIR)]
    else:
        empty = []
    for place, sigma in empty:
        w_ref[block(place, sigma)] = jnp.zeros((cols, cols), jnp.bfloat16)
    for place in range(rows):
        for offset in range(2 * REACH + 1):
            reached = place + offset - REACH
            if side == FAR and reached < 0:
                sigma = -1 - reached
            elif side == LOCAL and 0 <= reached < rows:
                sigma = reached
            elif side == MATE and reached >= rows:
                sigma = 2 * rows - 1 - reached
            else:
                continue
            w_ref[block(place, sigma)] = totals[place][offset].astype(jnp.bfloat16)


def prepare(
    partner_hbm, states_hbm, onsite_hbm, hop_row_hbm, hop_up_hbm, coefs_hbm, coupling_hbm,
    x_ref, w_ref, coef_ref, rim_ref, weight_ref, far_ref, *rest,
):
    *totals, partner_ref, states_ref, small_ref, coefs_ref, blocks, sems, row_sems = rest
    rows, slots = partner_hbm.shape
    cols = onsite_hbm.shape[2]
    tile = lax.axis_index("tile")
    all_rows = rows * lax.axis_size("tile")
    here = lax.rem(tile, 2)
    offsets = 2 * REACH + 1

    def kept(place):
        return place + here * (rows - 1 - 2 * place)

    copies = [
        pltpu.make_async_copy(src, dst, sems.at[i])
        for i, (src, dst) in enumerate(
            (
                (partner_hbm, partner_ref),
                (hop_up_hbm, small_ref.at[0]),
                (onsite_hbm, small_ref.at[1]),
                (hop_row_hbm, small_ref.at[2]),
                (coefs_hbm, coefs_ref),
                (states_hbm, states_ref),
            )
        )
    ]

    def fetch(r):
        return pltpu.make_async_copy(coupling_hbm.at[r], blocks.at[r], row_sems.at[r])

    copies[0].start()
    for place in range(rows):
        fetch(kept(place)).start()
    for copy in copies[1:]:
        copy.start()

    for total in totals:
        total[...] = jnp.zeros_like(total)
    for copy in copies:
        copy.wait()
    for n in range(coefs_ref.shape[0]):
        weight_ref[n : n + 1, :] = jnp.full((1, cols), coefs_ref[n], jnp.float32)
    column = lax.broadcasted_iota(jnp.int32, (rows, cols), 1)
    parity = lax.broadcasted_iota(jnp.int32, (rows, cols), 0) + column + tile * rows
    odd = lax.rem(column[0:1], 2) == 1
    for layer in range(2):
        bond = jnp.where(lax.rem(parity, 2) == 0, small_ref[0, layer], 0.0)
        hop_row = small_ref[2, layer]
        left = pltpu.roll(hop_row, 1, axis=1)
        for place in range(rows):
            back = rows - 1 - place
            at = slice(place, place + 1)

            def ours(value):
                return jnp.where(here == 0, value[at], value[back : back + 1])

            coef_ref[layer, 0, at] = ours(small_ref[1, layer])
            coef_ref[layer, 1, at] = ours(hop_row)
            coef_ref[layer, 2, at] = ours(left)
            if place < rows - 1:
                coef_ref[layer, 3, at] = jnp.where(here == 0, bond[at], bond[back - 1 : back])
            if place > 0:
                coef_ref[layer, 4, at] = jnp.where(here == 0, bond[place - 1 : place], bond[back : back + 1])
        last = bond[rows - 1 :]
        raw = jnp.where(odd, 1.0, 0.0)
        rim_ref[FAR - 1, layer : layer + 1] = jnp.where(here == 0, raw, last)
        rim_ref[MATE - 1, layer : layer + 1] = jnp.where(here == 0, last, raw)
        for place in range(rows):
            x_ref[layer, :, place * cols : (place + 1) * cols] = states_ref[layer, kept(place)]

    for pair in range(0, rows, PAIR):
        places = range(pair, pair + PAIR)
        for place in places:
            fetch(kept(place)).wait()
        for k in range(slots):
            for place in places:
                row = kept(place)
                slot = partner_ref[row, k]
                away = slot - tile * rows - row
                away = jnp.where(away > all_rows // 2, away - all_rows, away)
                away = jnp.where(away < -(all_rows // 2), away + all_rows, away)
                at = jnp.where(slot >= 0, REACH + (1 - 2 * here) * away, offsets)
                totals[place][at] += blocks[row, k].astype(jnp.float32)
    settle(totals, FAR, w_ref, cols)
    write_far(x_ref, w_ref, rim_ref, far_ref)


def to_mate(x_ref, w_ref, rim_ref, rows_ref, terms_ref):
    write_payload(x_ref, w_ref, rim_ref, MATE, rows_ref, terms_ref)


def to_mate_first(x_ref, rim_ref, *refs):
    *totals, rows_ref, terms_ref, w_ref = refs
    settle(totals, MATE, w_ref, rim_ref.shape[2])
    write_payload(x_ref, w_ref, rim_ref, MATE, rows_ref, terms_ref)


def inner(order, *refs):
    if order == 0:
        x_ref, coef_ref, weight_ref, *totals, sum_ref, filt_out, w_ref = refs
        settle(totals, LOCAL, w_ref, weight_ref.shape[1])
        scale = 1.0 / 12.0
    else:
        x_ref, prev_ref, filt_ref, w_ref, coef_ref, weight_ref, sum_ref, filt_out = refs
        scale = 2.0 / 12.0
    wide = x_ref.shape[2]
    cols = weight_ref.shape[1]
    rows = wide // cols
    first = x_ref[0].astype(jnp.bfloat16)
    second = x_ref[1].astype(jnp.bfloat16)
    for outs, term in products(second, w_ref, LOCAL, 1, cols):
        sum_ref[0, :, outs] = scale * term
    for outs, term in products(first, w_ref, LOCAL, 0, cols):
        sum_ref[1, :, outs] = scale * term
    for layer in range(2):
        for r in range(rows):
            here = slice(r * cols, (r + 1) * cols)
            x = x_ref[layer, :, here]

            def factor(i):
                return coef_ref[layer, i, r : r + 1, :]

            hop = factor(0) * x
            hop += factor(1) * pltpu.roll(x, cols - 1, axis=1)
            hop += factor(2) * pltpu.roll(x, 1, axis=1)
            if r < rows - 1:
                hop += factor(3) * x_ref[layer, :, (r + 1) * cols : (r + 2) * cols]
            if r > 0:
                hop += factor(4) * x_ref[layer, :, (r - 1) * cols : r * cols]
            term = sum_ref[layer, :, here] + scale * hop
            filt = weight_ref[order : order + 1, :] * x
            if order > 0:
                term -= prev_ref[layer, :, here]
                filt += filt_ref[layer, :, here]
            filt_out[layer, :, here] = filt
            sum_ref[layer, :, here] = term


def from_mate(scale, part_ref, w_ref, rim_ref, rows_ref, terms_ref, *refs):
    if len(refs) > 1:
        far_ref, sum_ref, *turned = refs
    else:
        (sum_ref,), turned = refs, []
    add_received(scale, rows_ref, terms_ref, w_ref, 1, rim_ref, MATE, part_ref, sum_ref)
    if turned:
        step = PAIR * rim_ref.shape[2]
        groups = sum_ref.shape[2] // step
        for group in range(groups):
            outs = slice(group * step, (group + 1) * step)
            for other in range(groups - group):
                ins = slice(other * step, (other + 1) * step)
                turned[0][ins, outs] = far_ref[outs, ins].T


def outer(scale, mine, sum_ref, w_ref, turned_ref, rim_ref, got_ref, *refs):
    x_ref, far_ref = refs[-2:]

    @pl.when(core() == mine)
    def _():
        add_far(scale, got_ref, turned_ref, rim_ref, sum_ref, x_ref)
        write_far(x_ref, w_ref, rim_ref, far_ref)


def finish(scale, degree, sum_ref, filt_ref, turned_ref, rim_ref, weight_ref, up_ref, down_ref, out_ref, x_ref):
    cols = rim_ref.shape[2]
    rows = out_ref.shape[1]
    flip = core()
    for mine, got_ref in enumerate((up_ref, down_ref)):

        @pl.when(flip == mine)
        def _():
            add_far(scale, got_ref, turned_ref, rim_ref, sum_ref, x_ref)

    for layer in range(2):
        for place in range(rows):
            here = slice(place * cols, (place + 1) * cols)
            out_ref[layer, place + flip * (rows - 1 - 2 * place)] = (
                filt_ref[layer, :, here] + weight_ref[degree : degree + 1, :] * x_ref[layer, :, here]
            )


def call(kernel, outs, args, scratch=(), specs=None, limit=12, flops=1 << 20, aliases=None):
    return pl.pallas_call(
        kernel,
        out_shape=outs,
        in_specs=specs or [IN_VMEM] * len(args),
        out_specs=[IN_VMEM] * len(outs),
        scratch_shapes=list(scratch),
        input_output_aliases=aliases or {},
        cost_estimate=pl.CostEstimate(flops=flops, bytes_accessed=0, transcendentals=0),
        compiler_params=pltpu.CompilerParams(vmem_limit_bytes=limit << 20),
    )(*args)


def body(states, onsite, hop_row, hop_up, partner, coupling, coefs):
    rows, count, cols = states.shape[1:]
    slots = partner.shape[1]
    wide = rows * cols
    degree = coefs.shape[0] - 1
    size = lax.axis_size("tile")
    up_pairs = [(i, (i + 1) % size) for i in range(size)]
    down_pairs = [((i + 1) % size, i) for i in range(size)]
    mate_pairs = [(i, i ^ 1) for i in range(size)]

    field = held((2, count, wide), jnp.float32)
    payload = held((count, 2 * wide + 2 * cols), jnp.bfloat16)
    parts = [held((count, wide + 2 * cols), jnp.bfloat16), held((count, wide), jnp.bfloat16)]
    matrix = held((wide, wide), jnp.bfloat16)
    x, w_far, coef, rim, weight, far, *totals = call(
        prepare,
        [field, matrix, held((2, 5, rows, cols), jnp.float32),
         held((2, 2, cols), jnp.float32), held((degree + 1, cols), jnp.float32), payload,
         *[held((2 * REACH + 2, cols, cols), jnp.float32)] * rows],
        [outside(v) for v in (partner, states, onsite, hop_row, hop_up, coefs, coupling)],
        scratch=[
            pltpu.SMEM((rows, slots), jnp.int32),
            pltpu.VMEM((2, rows, count, cols), jnp.float32),
            pltpu.VMEM((3, 2, rows, cols), jnp.float32),
            pltpu.SMEM((degree + 1,), jnp.float32),
            pltpu.VMEM((rows, slots, cols, cols), jnp.bfloat16),
            pltpu.SemaphoreType.DMA((6,)),
            pltpu.SemaphoreType.DMA((rows,)),
        ],
        specs=[ANYWHERE] * 7,
        limit=24,
    )
    w_far, coef, rim, weight, x = near(w_far), near(coef), near(rim), near(weight), near(x)
    totals = [near(total) for total in totals]
    prev = filt = None
    far = {0: far, 1: far}
    for order in range(degree):
        scale = 1.0 / 12.0 if order == 0 else 2.0 / 12.0
        got = {1: lax.ppermute(far[0], "tile", down_pairs), 0: lax.ppermute(far[1], "tile", up_pairs)}
        if order == 0:
            *mate, w_mate = call(to_mate_first, [*parts, matrix], [x, rim, *totals])
            w_mate = near(w_mate)
        else:
            mate = call(to_mate, parts, [x, w_mate, rim])
        got_mate = [near(lax.ppermute(part, "tile", mate_pairs)) for part in mate]
        if order == 0:
            part, filt, w_local = call(
                functools.partial(inner, order), [field, field, matrix], [x, coef, weight, *totals]
            )
            w_local = near(w_local)
        else:
            part, filt = call(
                functools.partial(inner, order),
                [field, field],
                [x, near(prev), near(filt), w_local, coef, weight],
            )
        part, *turned_now = call(
            functools.partial(from_mate, scale),
            [field, matrix] if order == 0 else [field],
            [near(part), w_mate, rim, *got_mate] + ([w_far] if order == 0 else []),
            flops=0,
        )
        if order == 0:
            turned = near(turned_now[0])
        prev = x
        if order < degree - 1:
            now, later = (0, 1) if order % 2 == 0 else (1, 0)
            x, far[now] = call(
                functools.partial(outer, scale, now),
                [field, payload],
                [near(part), w_far, turned, rim, near(got[now])],
            )
            x, far[later] = call(
                functools.partial(outer, scale, later),
                [field, payload],
                [near(part), w_far, turned, rim, near(got[later]), near(x)],
                aliases={5: 0},
            )
            x = near(x)
        else:
            (out,) = call(
                functools.partial(finish, scale, degree),
                [jax.ShapeDtypeStruct(states.shape, jnp.float32)],
                [near(part), near(filt), turned, rim, weight, near(got[0]), near(got[1])],
                scratch=[pltpu.VMEM((2, count, wide), jnp.float32)],
            )
    return out


def solution(mesh):
    placed = (
        P(None, "tile", "state", None),
        P(None, "tile", None),
        P(None, "tile", None),
        P(None, "tile", None),
        P("tile", None),
        P("tile", None, None, None),
        P(),
    )
    return jax.shard_map(
        body, mesh=mesh, in_specs=placed, out_specs=P(None, "tile", "state", None), check_vma=False
    )
```

```python
import functools

import jax
import jax.numpy as jnp
from jax import lax
from jax.experimental import pallas as pl
from jax.experimental.pallas import tpu as pltpu
from jax.sharding import PartitionSpec as P

REACH = 8
LOCAL, MATE, FAR = 0, 1, 2
IN_VMEM = pl.BlockSpec(memory_space=pltpu.VMEM)
ANYWHERE = pl.BlockSpec(memory_space=pl.ANY)
PAIR = 2


def near(x):
    return pltpu.with_memory_space_constraint(x, pltpu.VMEM)


def outside(x):
    return pltpu.with_memory_space_constraint(x, pltpu.HBM)


def held(shape, dtype):
    return pltpu.VMEM(shape, dtype)


def core():
    return lax.rem(lax.axis_index("tile"), 2)


def dot(x, w, contract):
    return lax.dot_general(x, w, (((1,), (contract,)), ((), ())), preferred_element_type=jnp.float32)


def span(side, group, groups, step):
    if side == FAR:
        return slice(0, (groups - group) * step)
    if side == MATE:
        return slice((groups - 1 - group) * step, groups * step)
    return slice(0, groups * step)


def products(x, w_ref, side, contract, cols):
    step = PAIR * cols
    groups = w_ref.shape[1] // step
    for group in range(groups):
        outs = slice(group * step, (group + 1) * step)
        ins = span(side, group, groups, step)
        block = w_ref[ins, outs] if contract == 0 else w_ref[outs, ins]
        yield outs, dot(x[:, ins], block, contract)


def write_payload(x_ref, w_ref, rim_ref, side, rows_ref, terms_ref):
    wide = x_ref.shape[2]
    cols = rim_ref.shape[2]
    edge = slice(0, cols) if side == FAR else slice(wide - cols, wide)
    which = side - 1
    rows_ref[:, 0:wide] = x_ref[1].astype(jnp.bfloat16)
    rim = x_ref[0, :, edge] * rim_ref[which, 0:1, :]
    rim += pltpu.roll(x_ref[1, :, edge] * rim_ref[which, 1:2, :], cols - 1, axis=1)
    high = rim.astype(jnp.bfloat16)
    rows_ref[:, wide : wide + cols] = high
    rows_ref[:, wide + cols :] = (rim - high.astype(jnp.float32)).astype(jnp.bfloat16)
    first = x_ref[0].astype(jnp.bfloat16)
    for outs, term in products(first, w_ref, side, 0, cols):
        terms_ref[:, outs] = term.astype(jnp.bfloat16)


def write_far(x_ref, w_ref, rim_ref, far_ref):
    cut = far_ref.shape[1] - x_ref.shape[2]
    write_payload(x_ref, w_ref, rim_ref, FAR, far_ref.at[:, 0:cut], far_ref.at[:, cut:])


def add_received(scale, rows_ref, terms_ref, w_ref, contract, rim_ref, side, from_ref, to_ref):
    wide = to_ref.shape[2]
    cols = rim_ref.shape[2]
    edge = slice(0, cols) if side == FAR else slice(wide - cols, wide)
    which = side - 1
    to_ref[1] = from_ref[1] + scale * terms_ref[...].astype(jnp.float32)
    for outs, term in products(rows_ref[:, 0:wide], w_ref, side, contract, cols):
        to_ref[0, :, outs] = from_ref[0, :, outs] + scale * term
    rim = rows_ref[:, wide : wide + cols].astype(jnp.float32)
    rim += rows_ref[:, wide + cols :].astype(jnp.float32)
    to_ref[0, :, edge] += scale * (rim * rim_ref[which, 0:1, :])
    to_ref[1, :, edge] += scale * (pltpu.roll(rim, 1, axis=1) * rim_ref[which, 1:2, :])


def add_far(scale, got_ref, turned_ref, rim_ref, from_ref, to_ref):
    cut = got_ref.shape[1] - to_ref.shape[2]
    add_received(
        scale, got_ref.at[:, 0:cut], got_ref.at[:, cut:], turned_ref, 0, rim_ref, FAR, from_ref, to_ref
    )


def settle(totals, side, w_ref, cols):
    rows = len(totals)

    def block(place, sigma):
        return (slice(place * cols, (place + 1) * cols), slice(sigma * cols, (sigma + 1) * cols))

    if side == FAR:
        empty = [(place, rows - place) for place in range(1, rows, PAIR)]
    elif side == MATE:
        empty = [(place, rows - PAIR - place) for place in range(0, rows, PAIR)]
    else:
        empty = []
    for place, sigma in empty:
        w_ref[block(place, sigma)] = jnp.zeros((cols, cols), jnp.bfloat16)
    for place in range(rows):
        for offset in range(2 * REACH + 1):
            reached = place + offset - REACH
            if side == FAR and reached < 0:
                sigma = -1 - reached
            elif side == LOCAL and 0 <= reached < rows:
                sigma = reached
            elif side == MATE and reached >= rows:
                sigma = 2 * rows - 1 - reached
            else:
                continue
            w_ref[block(place, sigma)] = totals[place][offset].astype(jnp.bfloat16)


def prepare(
    partner_hbm, states_hbm, onsite_hbm, hop_row_hbm, hop_up_hbm, coefs_hbm, coupling_hbm,
    x_ref, w_ref, coef_ref, rim_ref, weight_ref, far_ref, *rest,
):
    *totals, partner_ref, states_ref, small_ref, coefs_ref, blocks, sems, row_sems = rest
    rows, slots = partner_hbm.shape
    cols = onsite_hbm.shape[2]
    tile = lax.axis_index("tile")
    all_rows = rows * lax.axis_size("tile")
    here = lax.rem(tile, 2)
    offsets = 2 * REACH + 1

    def kept(place):
        return place + here * (rows - 1 - 2 * place)

    copies = [
        pltpu.make_async_copy(src, dst, sems.at[i])
        for i, (src, dst) in enumerate(
            (
                (partner_hbm, partner_ref),
                (hop_up_hbm, small_ref.at[0]),
                (onsite_hbm, small_ref.at[1]),
                (hop_row_hbm, small_ref.at[2]),
                (coefs_hbm, coefs_ref),
                (states_hbm, states_ref),
            )
        )
    ]

    def fetch(r):
        return pltpu.make_async_copy(coupling_hbm.at[r], blocks.at[r], row_sems.at[r])

    copies[0].start()
    for place in range(rows):
        fetch(kept(place)).start()
    for copy in copies[1:]:
        copy.start()

    for total in totals:
        total[...] = jnp.zeros_like(total)
    copies[0].wait()
    for pair in range(0, rows, PAIR):
        places = range(pair, pair + PAIR)
        for place in places:
            fetch(kept(place)).wait()
        for k in range(slots):
            for place in places:
                row = kept(place)
                slot = partner_ref[row, k]
                away = slot - tile * rows - row
                away = jnp.where(away > all_rows // 2, away - all_rows, away)
                away = jnp.where(away < -(all_rows // 2), away + all_rows, away)
                at = jnp.where(slot >= 0, REACH + (1 - 2 * here) * away, offsets)
                totals[place][at] += blocks[row, k].astype(jnp.float32)

    for copy in copies[1:]:
        copy.wait()
    for n in range(coefs_ref.shape[0]):
        weight_ref[n : n + 1, :] = jnp.full((1, cols), coefs_ref[n], jnp.float32)
    column = lax.broadcasted_iota(jnp.int32, (rows, cols), 1)
    parity = lax.broadcasted_iota(jnp.int32, (rows, cols), 0) + column + tile * rows
    odd = lax.rem(column[0:1], 2) == 1
    for layer in range(2):
        bond = jnp.where(lax.rem(parity, 2) == 0, small_ref[0, layer], 0.0)
        hop_row = small_ref[2, layer]
        left = pltpu.roll(hop_row, 1, axis=1)
        for place in range(rows):
            back = rows - 1 - place
            at = slice(place, place + 1)

            def ours(value):
                return jnp.where(here == 0, value[at], value[back : back + 1])

            coef_ref[layer, 0, at] = ours(small_ref[1, layer])
            coef_ref[layer, 1, at] = ours(hop_row)
            coef_ref[layer, 2, at] = ours(left)
            if place < rows - 1:
                coef_ref[layer, 3, at] = jnp.where(here == 0, bond[at], bond[back - 1 : back])
            if place > 0:
                coef_ref[layer, 4, at] = jnp.where(here == 0, bond[place - 1 : place], bond[back : back + 1])
        last = bond[rows - 1 :]
        raw = jnp.where(odd, 1.0, 0.0)
        rim_ref[FAR - 1, layer : layer + 1] = jnp.where(here == 0, raw, last)
        rim_ref[MATE - 1, layer : layer + 1] = jnp.where(here == 0, last, raw)
        for place in range(rows):
            x_ref[layer, :, place * cols : (place + 1) * cols] = states_ref[layer, kept(place)]

    settle(totals, FAR, w_ref, cols)
    write_far(x_ref, w_ref, rim_ref, far_ref)


def to_mate(x_ref, w_ref, rim_ref, rows_ref, terms_ref):
    write_payload(x_ref, w_ref, rim_ref, MATE, rows_ref, terms_ref)


def to_mate_first(x_ref, rim_ref, *refs):
    *totals, rows_ref, terms_ref, w_ref = refs
    settle(totals, MATE, w_ref, rim_ref.shape[2])
    write_payload(x_ref, w_ref, rim_ref, MATE, rows_ref, terms_ref)


def inner(order, *refs):
    if order == 0:
        x_ref, coef_ref, weight_ref, *totals, sum_ref, filt_out, w_ref = refs
        settle(totals, LOCAL, w_ref, weight_ref.shape[1])
        scale = 1.0 / 12.0
    else:
        x_ref, prev_ref, filt_ref, w_ref, coef_ref, weight_ref, sum_ref, filt_out = refs
        scale = 2.0 / 12.0
    wide = x_ref.shape[2]
    cols = weight_ref.shape[1]
    rows = wide // cols
    first = x_ref[0].astype(jnp.bfloat16)
    second = x_ref[1].astype(jnp.bfloat16)
    for outs, term in products(second, w_ref, LOCAL, 1, cols):
        sum_ref[0, :, outs] = scale * term
    for outs, term in products(first, w_ref, LOCAL, 0, cols):
        sum_ref[1, :, outs] = scale * term
    for layer in range(2):
        for r in range(rows):
            here = slice(r * cols, (r + 1) * cols)
            x = x_ref[layer, :, here]

            def factor(i):
                return coef_ref[layer, i, r : r + 1, :]

            hop = factor(0) * x
            hop += factor(1) * pltpu.roll(x, cols - 1, axis=1)
            hop += factor(2) * pltpu.roll(x, 1, axis=1)
            if r < rows - 1:
                hop += factor(3) * x_ref[layer, :, (r + 1) * cols : (r + 2) * cols]
            if r > 0:
                hop += factor(4) * x_ref[layer, :, (r - 1) * cols : r * cols]
            term = sum_ref[layer, :, here] + scale * hop
            filt = weight_ref[order : order + 1, :] * x
            if order > 0:
                term -= prev_ref[layer, :, here]
                filt += filt_ref[layer, :, here]
            filt_out[layer, :, here] = filt
            sum_ref[layer, :, here] = term


def from_mate(scale, part_ref, w_ref, rim_ref, rows_ref, terms_ref, *refs):
    if len(refs) > 1:
        far_ref, sum_ref, *turned = refs
    else:
        (sum_ref,), turned = refs, []
    add_received(scale, rows_ref, terms_ref, w_ref, 1, rim_ref, MATE, part_ref, sum_ref)
    if turned:
        step = PAIR * rim_ref.shape[2]
        groups = sum_ref.shape[2] // step
        for group in range(groups):
            outs = slice(group * step, (group + 1) * step)
            for other in range(groups - group):
                ins = slice(other * step, (other + 1) * step)
                turned[0][ins, outs] = far_ref[outs, ins].T


def outer(scale, mine, sum_ref, w_ref, turned_ref, rim_ref, got_ref, *refs):
    x_ref, far_ref = refs[-2:]

    @pl.when(core() == mine)
    def _():
        add_far(scale, got_ref, turned_ref, rim_ref, sum_ref, x_ref)
        write_far(x_ref, w_ref, rim_ref, far_ref)


def finish(scale, degree, sum_ref, filt_ref, turned_ref, rim_ref, weight_ref, up_ref, down_ref, out_ref, x_ref):
    cols = rim_ref.shape[2]
    rows = out_ref.shape[1]
    flip = core()
    for mine, got_ref in enumerate((up_ref, down_ref)):

        @pl.when(flip == mine)
        def _():
            add_far(scale, got_ref, turned_ref, rim_ref, sum_ref, x_ref)

    for layer in range(2):
        for place in range(rows):
            here = slice(place * cols, (place + 1) * cols)
            out_ref[layer, place + flip * (rows - 1 - 2 * place)] = (
                filt_ref[layer, :, here] + weight_ref[degree : degree + 1, :] * x_ref[layer, :, here]
            )


def call(kernel, outs, args, scratch=(), specs=None, limit=12, flops=1 << 20, aliases=None):
    return pl.pallas_call(
        kernel,
        out_shape=outs,
        in_specs=specs or [IN_VMEM] * len(args),
        out_specs=[IN_VMEM] * len(outs),
        scratch_shapes=list(scratch),
        input_output_aliases=aliases or {},
        cost_estimate=pl.CostEstimate(flops=flops, bytes_accessed=0, transcendentals=0),
        compiler_params=pltpu.CompilerParams(vmem_limit_bytes=limit << 20),
    )(*args)


def body(states, onsite, hop_row, hop_up, partner, coupling, coefs):
    rows, count, cols = states.shape[1:]
    slots = partner.shape[1]
    wide = rows * cols
    degree = coefs.shape[0] - 1
    size = lax.axis_size("tile")
    up_pairs = [(i, (i + 1) % size) for i in range(size)]
    down_pairs = [((i + 1) % size, i) for i in range(size)]
    mate_pairs = [(i, i ^ 1) for i in range(size)]

    field = held((2, count, wide), jnp.float32)
    payload = held((count, 2 * wide + 2 * cols), jnp.bfloat16)
    parts = [held((count, wide + 2 * cols), jnp.bfloat16), held((count, wide), jnp.bfloat16)]
    matrix = held((wide, wide), jnp.bfloat16)
    x, w_far, coef, rim, weight, far, *totals = call(
        prepare,
        [field, matrix, held((2, 5, rows, cols), jnp.float32),
         held((2, 2, cols), jnp.float32), held((degree + 1, cols), jnp.float32), payload,
         *[held((2 * REACH + 2, cols, cols), jnp.float32)] * rows],
        [outside(v) for v in (partner, states, onsite, hop_row, hop_up, coefs, coupling)],
        scratch=[
            pltpu.SMEM((rows, slots), jnp.int32),
            pltpu.VMEM((2, rows, count, cols), jnp.float32),
            pltpu.VMEM((3, 2, rows, cols), jnp.float32),
            pltpu.SMEM((degree + 1,), jnp.float32),
            pltpu.VMEM((rows, slots, cols, cols), jnp.bfloat16),
            pltpu.SemaphoreType.DMA((6,)),
            pltpu.SemaphoreType.DMA((rows,)),
        ],
        specs=[ANYWHERE] * 7,
        limit=24,
    )
    w_far, coef, rim, weight, x = near(w_far), near(coef), near(rim), near(weight), near(x)
    totals = [near(total) for total in totals]
    prev = filt = None
    far = {0: far, 1: far}
    for order in range(degree):
        scale = 1.0 / 12.0 if order == 0 else 2.0 / 12.0
        got = {1: lax.ppermute(far[0], "tile", down_pairs), 0: lax.ppermute(far[1], "tile", up_pairs)}
        if order == 0:
            *mate, w_mate = call(to_mate_first, [*parts, matrix], [x, rim, *totals])
            w_mate = near(w_mate)
        else:
            mate = call(to_mate, parts, [x, w_mate, rim])
        got_mate = [near(lax.ppermute(part, "tile", mate_pairs)) for part in mate]
        if order == 0:
            part, filt, w_local = call(
                functools.partial(inner, order), [field, field, matrix], [x, coef, weight, *totals]
            )
            w_local = near(w_local)
        else:
            part, filt = call(
                functools.partial(inner, order),
                [field, field],
                [x, near(prev), near(filt), w_local, coef, weight],
            )
        part, *turned_now = call(
            functools.partial(from_mate, scale),
            [field, matrix] if order == 0 else [field],
            [near(part), w_mate, rim, *got_mate] + ([w_far] if order == 0 else []),
            flops=0,
        )
        if order == 0:
            turned = near(turned_now[0])
        prev = x
        if order < degree - 1:
            now, later = (0, 1) if order % 2 == 0 else (1, 0)
            x, far[now] = call(
                functools.partial(outer, scale, now),
                [field, payload],
                [near(part), w_far, turned, rim, near(got[now])],
            )
            x, far[later] = call(
                functools.partial(outer, scale, later),
                [field, payload],
                [near(part), w_far, turned, rim, near(got[later]), near(x)],
                aliases={5: 0},
            )
            x = near(x)
        else:
            (out,) = call(
                functools.partial(finish, scale, degree),
                [jax.ShapeDtypeStruct(states.shape, jnp.float32)],
                [near(part), near(filt), turned, rim, weight, near(got[0]), near(got[1])],
                scratch=[pltpu.VMEM((2, count, wide), jnp.float32)],
            )
    return out


def solution(mesh):
    placed = (
        P(None, "tile", "state", None),
        P(None, "tile", None),
        P(None, "tile", None),
        P(None, "tile", None),
        P("tile", None),
        P("tile", None, None, None),
        P(),
    )
    return jax.shard_map(
        body, mesh=mesh, in_specs=placed, out_specs=P(None, "tile", "state", None), check_vma=False
    )
```

```python
import functools

import jax
import jax.numpy as jnp
from jax import lax
from jax.experimental import pallas as pl
from jax.experimental.pallas import tpu as pltpu
from jax.sharding import PartitionSpec as P

REACH = 8
LOCAL, MATE, FAR = 0, 1, 2
IN_VMEM = pl.BlockSpec(memory_space=pltpu.VMEM)
ANYWHERE = pl.BlockSpec(memory_space=pl.ANY)
PAIR = 2


def near(x):
    return pltpu.with_memory_space_constraint(x, pltpu.VMEM)


def outside(x):
    return pltpu.with_memory_space_constraint(x, pltpu.HBM)


def held(shape, dtype):
    return pltpu.VMEM(shape, dtype)


def core():
    return lax.rem(lax.axis_index("tile"), 2)


def dot(x, w, contract):
    return lax.dot_general(x, w, (((1,), (contract,)), ((), ())), preferred_element_type=jnp.float32)


def span(side, group, groups, step):
    if side == FAR:
        return slice(0, (groups - group) * step)
    if side == MATE:
        return slice((groups - 1 - group) * step, groups * step)
    return slice(0, groups * step)


def products(x, w_ref, side, contract, cols):
    step = PAIR * cols
    groups = w_ref.shape[1] // step
    for group in range(groups):
        outs = slice(group * step, (group + 1) * step)
        ins = span(side, group, groups, step)
        block = w_ref[ins, outs] if contract == 0 else w_ref[outs, ins]
        yield outs, dot(x[:, ins], block, contract)


def write_payload(x_ref, w_ref, rim_ref, side, rows_ref, terms_ref):
    wide = x_ref.shape[2]
    cols = rim_ref.shape[2]
    edge = slice(0, cols) if side == FAR else slice(wide - cols, wide)
    which = side - 1
    rows_ref[:, 0:wide] = x_ref[1].astype(jnp.bfloat16)
    rim = x_ref[0, :, edge] * rim_ref[which, 0:1, :]
    rim += pltpu.roll(x_ref[1, :, edge] * rim_ref[which, 1:2, :], cols - 1, axis=1)
    high = rim.astype(jnp.bfloat16)
    rows_ref[:, wide : wide + cols] = high
    rows_ref[:, wide + cols :] = (rim - high.astype(jnp.float32)).astype(jnp.bfloat16)
    first = x_ref[0].astype(jnp.bfloat16)
    for outs, term in products(first, w_ref, side, 0, cols):
        terms_ref[:, outs] = term.astype(jnp.bfloat16)


def write_far(x_ref, w_ref, rim_ref, far_ref):
    cut = far_ref.shape[1] - x_ref.shape[2]
    write_payload(x_ref, w_ref, rim_ref, FAR, far_ref.at[:, 0:cut], far_ref.at[:, cut:])


def add_received(scale, rows_ref, terms_ref, w_ref, contract, rim_ref, side, from_ref, to_ref):
    wide = to_ref.shape[2]
    cols = rim_ref.shape[2]
    edge = slice(0, cols) if side == FAR else slice(wide - cols, wide)
    which = side - 1
    to_ref[1] = from_ref[1] + scale * terms_ref[...].astype(jnp.float32)
    for outs, term in products(rows_ref[:, 0:wide], w_ref, side, contract, cols):
        to_ref[0, :, outs] = from_ref[0, :, outs] + scale * term
    rim = rows_ref[:, wide : wide + cols].astype(jnp.float32)
    rim += rows_ref[:, wide + cols :].astype(jnp.float32)
    to_ref[0, :, edge] += scale * (rim * rim_ref[which, 0:1, :])
    to_ref[1, :, edge] += scale * (pltpu.roll(rim, 1, axis=1) * rim_ref[which, 1:2, :])


def add_far(scale, got_ref, turned_ref, rim_ref, from_ref, to_ref):
    cut = got_ref.shape[1] - to_ref.shape[2]
    add_received(
        scale, got_ref.at[:, 0:cut], got_ref.at[:, cut:], turned_ref, 0, rim_ref, FAR, from_ref, to_ref
    )


def settle(totals, side, w_ref, cols):
    rows = len(totals)

    def block(place, sigma):
        return (slice(place * cols, (place + 1) * cols), slice(sigma * cols, (sigma + 1) * cols))

    if side == FAR:
        empty = [(place, rows - place) for place in range(1, rows, PAIR)]
    elif side == MATE:
        empty = [(place, rows - PAIR - place) for place in range(0, rows, PAIR)]
    else:
        empty = []
    for place, sigma in empty:
        w_ref[block(place, sigma)] = jnp.zeros((cols, cols), jnp.bfloat16)
    for place in range(rows):
        for offset in range(2 * REACH + 1):
            reached = place + offset - REACH
            if side == FAR and reached < 0:
                sigma = -1 - reached
            elif side == LOCAL and 0 <= reached < rows:
                sigma = reached
            elif side == MATE and reached >= rows:
                sigma = 2 * rows - 1 - reached
            else:
                continue
            w_ref[block(place, sigma)] = totals[place][offset].astype(jnp.bfloat16)


def prepare(
    partner_hbm, states_hbm, onsite_hbm, hop_row_hbm, hop_up_hbm, coefs_hbm, coupling_hbm,
    x_ref, w_ref, coef_ref, rim_ref, weight_ref, far_ref, *rest,
):
    *totals, partner_ref, states_ref, small_ref, coefs_ref, blocks, sems, row_sems = rest
    rows, slots = partner_hbm.shape
    cols = onsite_hbm.shape[2]
    tile = lax.axis_index("tile")
    all_rows = rows * lax.axis_size("tile")
    here = lax.rem(tile, 2)
    offsets = 2 * REACH + 1

    def kept(place):
        return place + here * (rows - 1 - 2 * place)

    copies = [
        pltpu.make_async_copy(src, dst, sems.at[i])
        for i, (src, dst) in enumerate(
            (
                (partner_hbm, partner_ref),
                (hop_up_hbm, small_ref.at[0]),
                (onsite_hbm, small_ref.at[1]),
                (hop_row_hbm, small_ref.at[2]),
                (coefs_hbm, coefs_ref),
                (states_hbm, states_ref),
            )
        )
    ]

    def fetch(r):
        return pltpu.make_async_copy(coupling_hbm.at[r], blocks.at[r], row_sems.at[r])

    for copy in copies:
        copy.start()
    for place in range(rows):
        fetch(kept(place)).start()

    for total in totals:
        total[...] = jnp.zeros_like(total)
    for copy in copies:
        copy.wait()
    for n in range(coefs_ref.shape[0]):
        weight_ref[n : n + 1, :] = jnp.full((1, cols), coefs_ref[n], jnp.float32)
    column = lax.broadcasted_iota(jnp.int32, (rows, cols), 1)
    parity = lax.broadcasted_iota(jnp.int32, (rows, cols), 0) + column + tile * rows
    odd = lax.rem(column[0:1], 2) == 1
    for layer in range(2):
        bond = jnp.where(lax.rem(parity, 2) == 0, small_ref[0, layer], 0.0)
        hop_row = small_ref[2, layer]
        left = pltpu.roll(hop_row, 1, axis=1)
        for place in range(rows):
            back = rows - 1 - place
            at = slice(place, place + 1)

            def ours(value):
                return jnp.where(here == 0, value[at], value[back : back + 1])

            coef_ref[layer, 0, at] = ours(small_ref[1, layer])
            coef_ref[layer, 1, at] = ours(hop_row)
            coef_ref[layer, 2, at] = ours(left)
            if place < rows - 1:
                coef_ref[layer, 3, at] = jnp.where(here == 0, bond[at], bond[back - 1 : back])
            if place > 0:
                coef_ref[layer, 4, at] = jnp.where(here == 0, bond[place - 1 : place], bond[back : back + 1])
        last = bond[rows - 1 :]
        raw = jnp.where(odd, 1.0, 0.0)
        rim_ref[FAR - 1, layer : layer + 1] = jnp.where(here == 0, raw, last)
        rim_ref[MATE - 1, layer : layer + 1] = jnp.where(here == 0, last, raw)
        for place in range(rows):
            x_ref[layer, :, place * cols : (place + 1) * cols] = states_ref[layer, kept(place)]

    for pair in range(0, rows, PAIR):
        places = range(pair, pair + PAIR)
        for place in places:
            fetch(kept(place)).wait()
        for k in range(slots):
            for place in places:
                row = kept(place)
                slot = partner_ref[row, k]
                away = slot - tile * rows - row
                away = jnp.where(away > all_rows // 2, away - all_rows, away)
                away = jnp.where(away < -(all_rows // 2), away + all_rows, away)
                at = jnp.where(slot >= 0, REACH + (1 - 2 * here) * away, offsets)
                totals[place][at] += blocks[row, k].astype(jnp.float32)

    settle(totals, FAR, w_ref, cols)
    write_far(x_ref, w_ref, rim_ref, far_ref)


def to_mate(x_ref, w_ref, rim_ref, rows_ref, terms_ref):
    write_payload(x_ref, w_ref, rim_ref, MATE, rows_ref, terms_ref)


def to_mate_first(x_ref, rim_ref, *refs):
    *totals, rows_ref, terms_ref, w_ref = refs
    settle(totals, MATE, w_ref, rim_ref.shape[2])
    write_payload(x_ref, w_ref, rim_ref, MATE, rows_ref, terms_ref)


def inner(order, *refs):
    if order == 0:
        x_ref, coef_ref, weight_ref, *totals, sum_ref, filt_out, w_ref = refs
        settle(totals, LOCAL, w_ref, weight_ref.shape[1])
        scale = 1.0 / 12.0
    else:
        x_ref, prev_ref, filt_ref, w_ref, coef_ref, weight_ref, sum_ref, filt_out = refs
        scale = 2.0 / 12.0
    wide = x_ref.shape[2]
    cols = weight_ref.shape[1]
    rows = wide // cols
    first = x_ref[0].astype(jnp.bfloat16)
    second = x_ref[1].astype(jnp.bfloat16)
    for outs, term in products(second, w_ref, LOCAL, 1, cols):
        sum_ref[0, :, outs] = scale * term
    for outs, term in products(first, w_ref, LOCAL, 0, cols):
        sum_ref[1, :, outs] = scale * term
    for layer in range(2):
        for r in range(rows):
            here = slice(r * cols, (r + 1) * cols)
            x = x_ref[layer, :, here]

            def factor(i):
                return coef_ref[layer, i, r : r + 1, :]

            hop = factor(0) * x
            hop += factor(1) * pltpu.roll(x, cols - 1, axis=1)
            hop += factor(2) * pltpu.roll(x, 1, axis=1)
            if r < rows - 1:
                hop += factor(3) * x_ref[layer, :, (r + 1) * cols : (r + 2) * cols]
            if r > 0:
                hop += factor(4) * x_ref[layer, :, (r - 1) * cols : r * cols]
            term = sum_ref[layer, :, here] + scale * hop
            filt = weight_ref[order : order + 1, :] * x
            if order > 0:
                term -= prev_ref[layer, :, here]
                filt += filt_ref[layer, :, here]
            filt_out[layer, :, here] = filt
            sum_ref[layer, :, here] = term


def from_mate(scale, part_ref, w_ref, rim_ref, rows_ref, terms_ref, *refs):
    if len(refs) > 1:
        far_ref, sum_ref, *turned = refs
    else:
        (sum_ref,), turned = refs, []
    add_received(scale, rows_ref, terms_ref, w_ref, 1, rim_ref, MATE, part_ref, sum_ref)
    if turned:
        step = PAIR * rim_ref.shape[2]
        groups = sum_ref.shape[2] // step
        for group in range(groups):
            outs = slice(group * step, (group + 1) * step)
            for other in range(groups - group):
                ins = slice(other * step, (other + 1) * step)
                turned[0][ins, outs] = far_ref[outs, ins].T


def outer(scale, mine, sum_ref, w_ref, turned_ref, rim_ref, got_ref, *refs):
    x_ref, far_ref = refs[-2:]

    @pl.when(core() == mine)
    def _():
        add_far(scale, got_ref, turned_ref, rim_ref, sum_ref, x_ref)
        write_far(x_ref, w_ref, rim_ref, far_ref)


def finish(scale, degree, sum_ref, filt_ref, turned_ref, rim_ref, weight_ref, up_ref, down_ref, out_ref, x_ref):
    cols = rim_ref.shape[2]
    rows = out_ref.shape[1]
    flip = core()
    for mine, got_ref in enumerate((up_ref, down_ref)):

        @pl.when(flip == mine)
        def _():
            add_far(scale, got_ref, turned_ref, rim_ref, sum_ref, x_ref)

    for layer in range(2):
        for place in range(rows):
            here = slice(place * cols, (place + 1) * cols)
            out_ref[layer, place + flip * (rows - 1 - 2 * place)] = (
                filt_ref[layer, :, here] + weight_ref[degree : degree + 1, :] * x_ref[layer, :, here]
            )


def call(kernel, outs, args, scratch=(), specs=None, limit=12, flops=1 << 20, aliases=None):
    return pl.pallas_call(
        kernel,
        out_shape=outs,
        in_specs=specs or [IN_VMEM] * len(args),
        out_specs=[IN_VMEM] * len(outs),
        scratch_shapes=list(scratch),
        input_output_aliases=aliases or {},
        cost_estimate=pl.CostEstimate(flops=flops, bytes_accessed=0, transcendentals=0),
        compiler_params=pltpu.CompilerParams(vmem_limit_bytes=limit << 20),
    )(*args)


def body(states, onsite, hop_row, hop_up, partner, coupling, coefs):
    rows, count, cols = states.shape[1:]
    slots = partner.shape[1]
    wide = rows * cols
    degree = coefs.shape[0] - 1
    size = lax.axis_size("tile")
    up_pairs = [(i, (i + 1) % size) for i in range(size)]
    down_pairs = [((i + 1) % size, i) for i in range(size)]
    mate_pairs = [(i, i ^ 1) for i in range(size)]

    field = held((2, count, wide), jnp.float32)
    payload = held((count, 2 * wide + 2 * cols), jnp.bfloat16)
    parts = [held((count, wide + 2 * cols), jnp.bfloat16), held((count, wide), jnp.bfloat16)]
    matrix = held((wide, wide), jnp.bfloat16)
    x, w_far, coef, rim, weight, far, *totals = call(
        prepare,
        [field, matrix, held((2, 5, rows, cols), jnp.float32),
         held((2, 2, cols), jnp.float32), held((degree + 1, cols), jnp.float32), payload,
         *[held((2 * REACH + 2, cols, cols), jnp.float32)] * rows],
        [outside(v) for v in (partner, states, onsite, hop_row, hop_up, coefs, coupling)],
        scratch=[
            pltpu.SMEM((rows, slots), jnp.int32),
            pltpu.VMEM((2, rows, count, cols), jnp.float32),
            pltpu.VMEM((3, 2, rows, cols), jnp.float32),
            pltpu.SMEM((degree + 1,), jnp.float32),
            pltpu.VMEM((rows, slots, cols, cols), jnp.bfloat16),
            pltpu.SemaphoreType.DMA((6,)),
            pltpu.SemaphoreType.DMA((rows,)),
        ],
        specs=[ANYWHERE] * 7,
        limit=24,
    )
    w_far, coef, rim, weight, x = near(w_far), near(coef), near(rim), near(weight), near(x)
    totals = [near(total) for total in totals]
    prev = filt = None
    far = {0: far, 1: far}
    for order in range(degree):
        scale = 1.0 / 12.0 if order == 0 else 2.0 / 12.0
        got = {1: lax.ppermute(far[0], "tile", down_pairs), 0: lax.ppermute(far[1], "tile", up_pairs)}
        if order == 0:
            *mate, w_mate = call(to_mate_first, [*parts, matrix], [x, rim, *totals])
            w_mate = near(w_mate)
        else:
            mate = call(to_mate, parts, [x, w_mate, rim])
        got_mate = [near(lax.ppermute(part, "tile", mate_pairs)) for part in mate]
        if order == 0:
            part, filt, w_local = call(
                functools.partial(inner, order), [field, field, matrix], [x, coef, weight, *totals]
            )
            w_local = near(w_local)
        else:
            part, filt = call(
                functools.partial(inner, order),
                [field, field],
                [x, near(prev), near(filt), w_local, coef, weight],
            )
        part, *turned_now = call(
            functools.partial(from_mate, scale),
            [field, matrix] if order == 0 else [field],
            [near(part), w_mate, rim, *got_mate] + ([w_far] if order == 0 else []),
            flops=0,
        )
        if order == 0:
            turned = near(turned_now[0])
        prev = x
        if order < degree - 1:
            now, later = (0, 1) if order % 2 == 0 else (1, 0)
            x, far[now] = call(
                functools.partial(outer, scale, now),
                [field, payload],
                [near(part), w_far, turned, rim, near(got[now])],
            )
            x, far[later] = call(
                functools.partial(outer, scale, later),
                [field, payload],
                [near(part), w_far, turned, rim, near(got[later]), near(x)],
                aliases={5: 0},
            )
            x = near(x)
        else:
            (out,) = call(
                functools.partial(finish, scale, degree),
                [jax.ShapeDtypeStruct(states.shape, jnp.float32)],
                [near(part), near(filt), turned, rim, weight, near(got[0]), near(got[1])],
                scratch=[pltpu.VMEM((2, count, wide), jnp.float32)],
            )
    return out


def solution(mesh):
    placed = (
        P(None, "tile", "state", None),
        P(None, "tile", None),
        P(None, "tile", None),
        P(None, "tile", None),
        P("tile", None),
        P("tile", None, None, None),
        P(),
    )
    return jax.shard_map(
        body, mesh=mesh, in_specs=placed, out_specs=P(None, "tile", "state", None), check_vma=False
    )
```

```python
import functools

import jax
import jax.numpy as jnp
from jax import lax
from jax.experimental import pallas as pl
from jax.experimental.pallas import tpu as pltpu
from jax.sharding import PartitionSpec as P

REACH = 8
LOCAL, MATE, FAR = 0, 1, 2
IN_VMEM = pl.BlockSpec(memory_space=pltpu.VMEM)
ANYWHERE = pl.BlockSpec(memory_space=pl.ANY)
PAIR = 2


def near(x):
    return pltpu.with_memory_space_constraint(x, pltpu.VMEM)


def outside(x):
    return pltpu.with_memory_space_constraint(x, pltpu.HBM)


def held(shape, dtype):
    return pltpu.VMEM(shape, dtype)


def core():
    return lax.rem(lax.axis_index("tile"), 2)


def dot(x, w, contract):
    return lax.dot_general(x, w, (((1,), (contract,)), ((), ())), preferred_element_type=jnp.float32)


def span(side, group, groups, step):
    if side == FAR:
        return slice(0, (groups - group) * step)
    if side == MATE:
        return slice((groups - 1 - group) * step, groups * step)
    return slice(0, groups * step)


def products(x, w_ref, side, contract, cols):
    step = PAIR * cols
    groups = w_ref.shape[1] // step
    for group in range(groups):
        outs = slice(group * step, (group + 1) * step)
        ins = span(side, group, groups, step)
        block = w_ref[ins, outs] if contract == 0 else w_ref[outs, ins]
        yield outs, dot(x[:, ins], block, contract)


def write_payload(x_ref, w_ref, rim_ref, side, rows_ref, terms_ref):
    wide = x_ref.shape[2]
    cols = rim_ref.shape[2]
    edge = slice(0, cols) if side == FAR else slice(wide - cols, wide)
    which = side - 1
    rows_ref[:, 0:wide] = x_ref[1].astype(jnp.bfloat16)
    rim = x_ref[0, :, edge] * rim_ref[which, 0:1, :]
    rim += pltpu.roll(x_ref[1, :, edge] * rim_ref[which, 1:2, :], cols - 1, axis=1)
    high = rim.astype(jnp.bfloat16)
    rows_ref[:, wide : wide + cols] = high
    rows_ref[:, wide + cols :] = (rim - high.astype(jnp.float32)).astype(jnp.bfloat16)
    first = x_ref[0].astype(jnp.bfloat16)
    for outs, term in products(first, w_ref, side, 0, cols):
        terms_ref[:, outs] = term.astype(jnp.bfloat16)


def write_far(x_ref, w_ref, rim_ref, far_ref):
    cut = far_ref.shape[1] - x_ref.shape[2]
    write_payload(x_ref, w_ref, rim_ref, FAR, far_ref.at[:, 0:cut], far_ref.at[:, cut:])


def add_received(scale, rows_ref, terms_ref, w_ref, contract, rim_ref, side, from_ref, to_ref):
    wide = to_ref.shape[2]
    cols = rim_ref.shape[2]
    edge = slice(0, cols) if side == FAR else slice(wide - cols, wide)
    which = side - 1
    to_ref[1] = from_ref[1] + scale * terms_ref[...].astype(jnp.float32)
    for outs, term in products(rows_ref[:, 0:wide], w_ref, side, contract, cols):
        to_ref[0, :, outs] = from_ref[0, :, outs] + scale * term
    rim = rows_ref[:, wide : wide + cols].astype(jnp.float32)
    rim += rows_ref[:, wide + cols :].astype(jnp.float32)
    to_ref[0, :, edge] += scale * (rim * rim_ref[which, 0:1, :])
    to_ref[1, :, edge] += scale * (pltpu.roll(rim, 1, axis=1) * rim_ref[which, 1:2, :])


def add_far(scale, got_ref, turned_ref, rim_ref, from_ref, to_ref):
    cut = got_ref.shape[1] - to_ref.shape[2]
    add_received(
        scale, got_ref.at[:, 0:cut], got_ref.at[:, cut:], turned_ref, 0, rim_ref, FAR, from_ref, to_ref
    )


def settle(totals, side, w_ref, cols):
    rows = len(totals)

    def block(place, sigma):
        return (slice(place * cols, (place + 1) * cols), slice(sigma * cols, (sigma + 1) * cols))

    if side == FAR:
        empty = [(place, rows - place) for place in range(1, rows, PAIR)]
    elif side == MATE:
        empty = [(place, rows - PAIR - place) for place in range(0, rows, PAIR)]
    else:
        empty = []
    for place, sigma in empty:
        w_ref[block(place, sigma)] = jnp.zeros((cols, cols), jnp.bfloat16)
    for place in range(rows):
        for offset in range(2 * REACH + 1):
            reached = place + offset - REACH
            if side == FAR and reached < 0:
                sigma = -1 - reached
            elif side == LOCAL and 0 <= reached < rows:
                sigma = reached
            elif side == MATE and reached >= rows:
                sigma = 2 * rows - 1 - reached
            else:
                continue
            w_ref[block(place, sigma)] = totals[place][offset].astype(jnp.bfloat16)


def turn(w_ref, side, turned_ref, cols):
    step = PAIR * cols
    groups = w_ref.shape[1] // step
    for group in range(groups):
        outs = slice(group * step, (group + 1) * step)
        inside = span(side, group, groups, step)
        for start in range(inside.start, inside.stop, step):
            ins = slice(start, start + step)
            turned_ref[ins, outs] = w_ref[outs, ins].T


def prepare(
    partner_hbm, states_hbm, onsite_hbm, hop_row_hbm, hop_up_hbm, coefs_hbm, coupling_hbm,
    x_ref, w_ref, coef_ref, rim_ref, weight_ref, far_ref, *rest,
):
    *totals, partner_ref, states_ref, small_ref, coefs_ref, blocks, sems, row_sems = rest
    rows, slots = partner_hbm.shape
    cols = onsite_hbm.shape[2]
    tile = lax.axis_index("tile")
    all_rows = rows * lax.axis_size("tile")
    here = lax.rem(tile, 2)
    offsets = 2 * REACH + 1

    def kept(place):
        return place + here * (rows - 1 - 2 * place)

    copies = [
        pltpu.make_async_copy(src, dst, sems.at[i])
        for i, (src, dst) in enumerate(
            (
                (partner_hbm, partner_ref),
                (hop_up_hbm, small_ref.at[0]),
                (onsite_hbm, small_ref.at[1]),
                (hop_row_hbm, small_ref.at[2]),
                (coefs_hbm, coefs_ref),
                (states_hbm, states_ref),
            )
        )
    ]

    def fetch(r):
        return pltpu.make_async_copy(coupling_hbm.at[r], blocks.at[r], row_sems.at[r])

    copies[0].start()
    for place in range(rows):
        fetch(kept(place)).start()
    for copy in copies[1:]:
        copy.start()

    for total in totals:
        total[...] = jnp.zeros_like(total)
    copies[0].wait()
    for pair in range(0, rows, PAIR):
        places = range(pair, pair + PAIR)
        for place in places:
            fetch(kept(place)).wait()
        for k in range(slots):
            for place in places:
                row = kept(place)
                slot = partner_ref[row, k]
                away = slot - tile * rows - row
                away = jnp.where(away > all_rows // 2, away - all_rows, away)
                away = jnp.where(away < -(all_rows // 2), away + all_rows, away)
                at = jnp.where(slot >= 0, REACH + (1 - 2 * here) * away, offsets)
                totals[place][at] += blocks[row, k].astype(jnp.float32)

    for copy in copies[1:]:
        copy.wait()
    for n in range(coefs_ref.shape[0]):
        weight_ref[n : n + 1, :] = jnp.full((1, cols), coefs_ref[n], jnp.float32)
    column = lax.broadcasted_iota(jnp.int32, (rows, cols), 1)
    parity = lax.broadcasted_iota(jnp.int32, (rows, cols), 0) + column + tile * rows
    odd = lax.rem(column[0:1], 2) == 1
    for layer in range(2):
        bond = jnp.where(lax.rem(parity, 2) == 0, small_ref[0, layer], 0.0)
        hop_row = small_ref[2, layer]
        left = pltpu.roll(hop_row, 1, axis=1)
        for place in range(rows):
            back = rows - 1 - place
            at = slice(place, place + 1)

            def ours(value):
                return jnp.where(here == 0, value[at], value[back : back + 1])

            coef_ref[layer, 0, at] = ours(small_ref[1, layer])
            coef_ref[layer, 1, at] = ours(hop_row)
            coef_ref[layer, 2, at] = ours(left)
            if place < rows - 1:
                coef_ref[layer, 3, at] = jnp.where(here == 0, bond[at], bond[back - 1 : back])
            if place > 0:
                coef_ref[layer, 4, at] = jnp.where(here == 0, bond[place - 1 : place], bond[back : back + 1])
        last = bond[rows - 1 :]
        raw = jnp.where(odd, 1.0, 0.0)
        rim_ref[FAR - 1, layer : layer + 1] = jnp.where(here == 0, raw, last)
        rim_ref[MATE - 1, layer : layer + 1] = jnp.where(here == 0, last, raw)
        for place in range(rows):
            x_ref[layer, :, place * cols : (place + 1) * cols] = states_ref[layer, kept(place)]

    settle(totals, FAR, w_ref, cols)
    write_far(x_ref, w_ref, rim_ref, far_ref)


def to_mate(x_ref, w_ref, rim_ref, rows_ref, terms_ref):
    write_payload(x_ref, w_ref, rim_ref, MATE, rows_ref, terms_ref)


def to_mate_first(x_ref, rim_ref, *refs):
    *totals, rows_ref, terms_ref, w_ref, turned_ref = refs
    settle(totals, MATE, w_ref, rim_ref.shape[2])
    turn(w_ref, MATE, turned_ref, rim_ref.shape[2])
    write_payload(x_ref, w_ref, rim_ref, MATE, rows_ref, terms_ref)


def inner(order, *refs):
    if order == 0:
        x_ref, coef_ref, weight_ref, *totals, sum_ref, filt_out, w_ref, turned_ref = refs
        settle(totals, LOCAL, w_ref, weight_ref.shape[1])
        turn(w_ref, LOCAL, turned_ref, weight_ref.shape[1])
        scale = 1.0 / 12.0
    else:
        x_ref, prev_ref, filt_ref, w_ref, turned_ref, coef_ref, weight_ref, sum_ref, filt_out = refs
        scale = 2.0 / 12.0
    wide = x_ref.shape[2]
    cols = weight_ref.shape[1]
    rows = wide // cols
    first = x_ref[0].astype(jnp.bfloat16)
    second = x_ref[1].astype(jnp.bfloat16)
    for outs, term in products(second, turned_ref, LOCAL, 0, cols):
        sum_ref[0, :, outs] = scale * term
    for outs, term in products(first, w_ref, LOCAL, 0, cols):
        sum_ref[1, :, outs] = scale * term
    for layer in range(2):
        for r in range(rows):
            here = slice(r * cols, (r + 1) * cols)
            x = x_ref[layer, :, here]

            def factor(i):
                return coef_ref[layer, i, r : r + 1, :]

            hop = factor(0) * x
            hop += factor(1) * pltpu.roll(x, cols - 1, axis=1)
            hop += factor(2) * pltpu.roll(x, 1, axis=1)
            if r < rows - 1:
                hop += factor(3) * x_ref[layer, :, (r + 1) * cols : (r + 2) * cols]
            if r > 0:
                hop += factor(4) * x_ref[layer, :, (r - 1) * cols : r * cols]
            term = sum_ref[layer, :, here] + scale * hop
            filt = weight_ref[order : order + 1, :] * x
            if order > 0:
                term -= prev_ref[layer, :, here]
                filt += filt_ref[layer, :, here]
            filt_out[layer, :, here] = filt
            sum_ref[layer, :, here] = term


def from_mate(scale, part_ref, w_ref, rim_ref, rows_ref, terms_ref, *refs):
    if len(refs) > 1:
        far_ref, sum_ref, *turned = refs
    else:
        (sum_ref,), turned = refs, []
    add_received(scale, rows_ref, terms_ref, w_ref, 0, rim_ref, MATE, part_ref, sum_ref)
    if turned:
        turn(far_ref, FAR, turned[0], rim_ref.shape[2])


def outer(scale, mine, sum_ref, w_ref, turned_ref, rim_ref, got_ref, *refs):
    x_ref, far_ref = refs[-2:]

    @pl.when(core() == mine)
    def _():
        add_far(scale, got_ref, turned_ref, rim_ref, sum_ref, x_ref)
        write_far(x_ref, w_ref, rim_ref, far_ref)


def finish(scale, degree, sum_ref, filt_ref, turned_ref, rim_ref, weight_ref, up_ref, down_ref, out_ref, x_ref):
    cols = rim_ref.shape[2]
    rows = out_ref.shape[1]
    flip = core()
    for mine, got_ref in enumerate((up_ref, down_ref)):

        @pl.when(flip == mine)
        def _():
            add_far(scale, got_ref, turned_ref, rim_ref, sum_ref, x_ref)

    for layer in range(2):
        for place in range(rows):
            here = slice(place * cols, (place + 1) * cols)
            out_ref[layer, place + flip * (rows - 1 - 2 * place)] = (
                filt_ref[layer, :, here] + weight_ref[degree : degree + 1, :] * x_ref[layer, :, here]
            )


def call(kernel, outs, args, scratch=(), specs=None, limit=12, flops=1 << 20, aliases=None):
    return pl.pallas_call(
        kernel,
        out_shape=outs,
        in_specs=specs or [IN_VMEM] * len(args),
        out_specs=[IN_VMEM] * len(outs),
        scratch_shapes=list(scratch),
        input_output_aliases=aliases or {},
        cost_estimate=pl.CostEstimate(flops=flops, bytes_accessed=0, transcendentals=0),
        compiler_params=pltpu.CompilerParams(vmem_limit_bytes=limit << 20),
    )(*args)


def body(states, onsite, hop_row, hop_up, partner, coupling, coefs):
    rows, count, cols = states.shape[1:]
    slots = partner.shape[1]
    wide = rows * cols
    degree = coefs.shape[0] - 1
    size = lax.axis_size("tile")
    up_pairs = [(i, (i + 1) % size) for i in range(size)]
    down_pairs = [((i + 1) % size, i) for i in range(size)]
    mate_pairs = [(i, i ^ 1) for i in range(size)]

    field = held((2, count, wide), jnp.float32)
    payload = held((count, 2 * wide + 2 * cols), jnp.bfloat16)
    parts = [held((count, wide + 2 * cols), jnp.bfloat16), held((count, wide), jnp.bfloat16)]
    matrix = held((wide, wide), jnp.bfloat16)
    x, w_far, coef, rim, weight, far, *totals = call(
        prepare,
        [field, matrix, held((2, 5, rows, cols), jnp.float32),
         held((2, 2, cols), jnp.float32), held((degree + 1, cols), jnp.float32), payload,
         *[held((2 * REACH + 2, cols, cols), jnp.float32)] * rows],
        [outside(v) for v in (partner, states, onsite, hop_row, hop_up, coefs, coupling)],
        scratch=[
            pltpu.SMEM((rows, slots), jnp.int32),
            pltpu.VMEM((2, rows, count, cols), jnp.float32),
            pltpu.VMEM((3, 2, rows, cols), jnp.float32),
            pltpu.SMEM((degree + 1,), jnp.float32),
            pltpu.VMEM((rows, slots, cols, cols), jnp.bfloat16),
            pltpu.SemaphoreType.DMA((6,)),
            pltpu.SemaphoreType.DMA((rows,)),
        ],
        specs=[ANYWHERE] * 7,
        limit=24,
    )
    w_far, coef, rim, weight, x = near(w_far), near(coef), near(rim), near(weight), near(x)
    totals = [near(total) for total in totals]
    prev = filt = None
    far = {0: far, 1: far}
    for order in range(degree):
        scale = 1.0 / 12.0 if order == 0 else 2.0 / 12.0
        got = {1: lax.ppermute(far[0], "tile", down_pairs), 0: lax.ppermute(far[1], "tile", up_pairs)}
        if order == 0:
            *mate, w_mate, m_turned = call(
                to_mate_first, [*parts, matrix, matrix], [x, rim, *totals]
            )
            w_mate, m_turned = near(w_mate), near(m_turned)
        else:
            mate = call(to_mate, parts, [x, w_mate, rim])
        got_mate = [near(lax.ppermute(part, "tile", mate_pairs)) for part in mate]
        if order == 0:
            part, filt, w_local, w_turned = call(
                functools.partial(inner, order),
                [field, field, matrix, matrix],
                [x, coef, weight, *totals],
            )
            w_local, w_turned = near(w_local), near(w_turned)
        else:
            part, filt = call(
                functools.partial(inner, order),
                [field, field],
                [x, near(prev), near(filt), w_local, w_turned, coef, weight],
            )
        part, *turned_now = call(
            functools.partial(from_mate, scale),
            [field, matrix] if order == 0 else [field],
            [near(part), m_turned, rim, *got_mate] + ([w_far] if order == 0 else []),
            flops=0,
        )
        if order == 0:
            turned = near(turned_now[0])
        prev = x
        if order < degree - 1:
            now, later = (0, 1) if order % 2 == 0 else (1, 0)
            x, far[now] = call(
                functools.partial(outer, scale, now),
                [field, payload],
                [near(part), w_far, turned, rim, near(got[now])],
            )
            x, far[later] = call(
                functools.partial(outer, scale, later),
                [field, payload],
                [near(part), w_far, turned, rim, near(got[later]), near(x)],
                aliases={5: 0},
            )
            x = near(x)
        else:
            (out,) = call(
                functools.partial(finish, scale, degree),
                [jax.ShapeDtypeStruct(states.shape, jnp.float32)],
                [near(part), near(filt), turned, rim, weight, near(got[0]), near(got[1])],
                scratch=[pltpu.VMEM((2, count, wide), jnp.float32)],
            )
    return out


def solution(mesh):
    placed = (
        P(None, "tile", "state", None),
        P(None, "tile", None),
        P(None, "tile", None),
        P(None, "tile", None),
        P("tile", None),
        P("tile", None, None, None),
        P(),
    )
    return jax.shard_map(
        body, mesh=mesh, in_specs=placed, out_specs=P(None, "tile", "state", None), check_vma=False
    )
```
